256 devices in a mesh: gx: 4 (over y), gy: 8 (over x, core), gz: 8 (over z).
Axes of the slice: x: 4, y: 4, z: 8, core: 2. Of those that a mesh axis runs over, the one named last changes fastest.
Arguments:
- velocity: float32 [3, 32, 64, 1024], P(None, 'gx', 'gy', 'gz'), may hold values from -6 to 6
- features: bfloat16 [16, 32, 64, 1024], P(None, 'gx', 'gy', 'gz'), may hold values from -6 to 6
- density: float32 [32, 64, 1024], P('gx', 'gy', 'gz'), may hold values from 0.5 to 2
- target: float32 [3, 32, 64, 1024], P(None, 'gx', 'gy', 'gz'), may hold values from -6 to 6
- weight_in: bfloat16 [16, 64], replicated, may hold values from -1.5 to 1.5
- bias_in: float32 [64], replicated, may hold values from -3 to 3
- weight_out: bfloat16 [64, 3], replicated, may hold values from -0.75 to 0.75
- open_faces: int32 [6], replicated, may hold values from 0 to 1
Outputs:
- new_velocity: float32 [3, 32, 64, 1024], P(None, 'gx', 'gy', 'gz')
- grad_weight_in: float32 [16, 64], replicated
- grad_bias_in: float32 [64], replicated
- grad_weight_out: float32 [64, 3], replicated
The draws below stay inside these ranges and needn't reach their ends.
Inputs may be any that keep to these rules, and one draw needn't show every extreme that they name: `open_faces`: entries in the order low first, high first, low second, high second, low third, high third face; 1 marks an open face (pressure zero beyond it), 0 a wall.
All inputs are finite; a program needn't handle non-finite values.
Results may differ from the reference program's by a relative error of at most 0.0012.
Values sent between devices are 32-bit elements; how exact they have to be, the bound alone decides.
No kernel may reach another device: no remote copies, remote signals or barrier semaphores. Data moves between devices by JAX's collectives and lax.ppermute only.
A program may use at most 128 MiB of HBM per device.

```python
import math
import jax
import jax.numpy as jnp
from jax import lax

FEAT = 16
HIDDEN_SIZE = 64
CYCLES = 2
SWEEPS = 3
COARSE_SWEEPS = 6
NX = 32
NY = 64
NZ = 1024


PERIOD_MAIN = 40.0


PERIOD_SIDE = 56.0


def smooth_flux(key):
    phase_key, amplitude_key, rough_key = jax.random.split(key, 3)
    phases = jax.random.uniform(phase_key, (3, 2), jnp.float32, 0.0, 2.0 * math.pi)
    amplitude = 3.0 * jax.random.uniform(amplitude_key, (3,), jnp.float32, 0.6, 1.0)
    rough_part = jnp.clip(jax.random.normal(rough_key, (3, NX, NY, NZ), jnp.float32), -2.5, 2.5)
    positions = (jnp.arange(NX, dtype=jnp.float32).reshape(-1, 1, 1), jnp.arange(NY, dtype=jnp.float32).reshape(1, -1, 1), jnp.arange(NZ, dtype=jnp.float32).reshape(1, 1, -1))
    components = []
    for direction in range(3):
        lengthwise = jnp.sin(2.0 * math.pi * positions[direction] / PERIOD_MAIN + phases[direction, 0])
        crosswise = 0.75 + 0.25 * jnp.cos(2.0 * math.pi * positions[(direction + 1) % 3] / PERIOD_SIDE + phases[direction, 1])
        components.append(jnp.broadcast_to(amplitude[direction] * lengthwise * crosswise, (NX, NY, NZ)))
    return jnp.stack(components) + rough_part


def draw_velocity(key, part):
    return smooth_flux(jax.random.fold_in(key, 11))


def draw_target(key, part):
    return smooth_flux(jax.random.fold_in(key, 23))


def touch_ends(array, stream_key, least, high):
    longest = array.shape.index(max(array.shape))
    spots = []
    for shift in (0, 1):
        where = [jax.random.randint(jax.random.fold_in(stream_key, axis), (), 0, length) for axis, length in enumerate(array.shape)]
        where[longest] = (where[longest] + shift) % array.shape[longest]
        spots.append(tuple(where))
    return array.at[spots[0]].set(least).at[spots[1]].set(high)


def block_scale(rng, shape, cuts, low, largest):
    gain = 1.0
    for dim, shards_of in cuts:
        draws = jax.random.uniform(jax.random.fold_in(jax.random.fold_in(rng, 6), dim), (shards_of,), jnp.float32, low / len(cuts), largest / len(cuts))
        gain = gain * jnp.repeat(jnp.exp(draws), shape[dim] // shards_of).reshape((-1,) + (1,) * (len(shape) - 1 - dim))
    return gain


def gaussian(stream_key, extent, deviation, most, pieces=(), kind=jnp.bfloat16):
    gain = block_scale(stream_key, extent, pieces, -0.22, 0.18) if pieces else 1.0
    array = jax.random.normal(stream_key, extent, jnp.float32) * deviation * gain
    return jnp.minimum(jnp.maximum(array, -most), most).astype(kind)


def setup_inputs(seed: int = 0) -> dict:
    key_of = jax.random.split(jax.random.key(seed), 9)
    return {
        "velocity": draw_velocity(jax.random.fold_in(key_of[8], 71), 0),
        "features": gaussian(key_of[1], (FEAT, NX, NY, NZ), 1.0, 6.0, ((1, 4), (2, 8), (3, 8))),
        "density": jnp.clip(jnp.exp(math.log(2.0) - 1.3862944 * jax.random.uniform(key_of[2], (NX, NY, NZ), jnp.float32) ** block_scale(key_of[2], (NX, NY, NZ), ((0, 4), (1, 8), (2, 8)), -0.2, 0.2)), 0.5, 2.0),
        "target": draw_target(jax.random.fold_in(key_of[8], 71), 0),
        "weight_in": gaussian(key_of[4], (FEAT, HIDDEN_SIZE), FEAT ** -0.5, 1.5),
        "bias_in": gaussian(key_of[5], (HIDDEN_SIZE,), 0.5, 3.0, (), jnp.float32),
        "weight_out": gaussian(key_of[6], (HIDDEN_SIZE, 3), HIDDEN_SIZE ** -0.5, 0.75),
        "open_faces": touch_ends(jax.random.randint(key_of[7], (6,), 0, 2), jax.random.fold_in(key_of[7], 1), 0, 1).astype(jnp.int32),
    }


RELAXATION = 0.8
MASS_SHIFT = 0.05
SHAPES = ((-1, 1, 1), (1, -1, 1), (1, 1, -1))


def zero_padded(field):
    return jnp.pad(field, 1)


def edge_factors(length, offset, whole_length, lower_flag, upper_flag):
    position = jnp.arange(length, dtype=jnp.int32) + offset
    lower = jnp.where(position == 0, lower_flag.astype(jnp.float32), jnp.float32(1.0))
    upper = jnp.where(position == whole_length - 1, upper_flag.astype(jnp.float32), jnp.float32(1.0))
    return lower, upper


def coefficients(padded_density, factors, weight):
    centre = padded_density[1:-1, 1:-1, 1:-1]
    following = (padded_density[2:, 1:-1, 1:-1], padded_density[1:-1, 2:, 1:-1], padded_density[1:-1, 1:-1, 2:])
    preceding = (padded_density[:-2, 1:-1, 1:-1], padded_density[1:-1, :-2, 1:-1], padded_density[1:-1, 1:-1, :-2])
    upper_coefs = tuple(weight * 2.0 / (centre + following[direction]) * factors[direction][1].reshape(SHAPES[direction]) for direction in range(3))
    lower_coefs = tuple(weight * 2.0 / (centre + preceding[direction]) * factors[direction][0].reshape(SHAPES[direction]) for direction in range(3))
    diagonal = MASS_SHIFT + upper_coefs[0] + lower_coefs[0] + upper_coefs[1] + lower_coefs[1] + upper_coefs[2] + lower_coefs[2]
    return upper_coefs, lower_coefs, diagonal


def neighbour_sum(padded_field, upper_coefs, lower_coefs):
    summed = upper_coefs[0] * padded_field[2:, 1:-1, 1:-1] + lower_coefs[0] * padded_field[:-2, 1:-1, 1:-1]
    summed = summed + upper_coefs[1] * padded_field[1:-1, 2:, 1:-1] + lower_coefs[1] * padded_field[1:-1, :-2, 1:-1]
    summed = summed + upper_coefs[2] * padded_field[1:-1, 1:-1, 2:] + lower_coefs[2] * padded_field[1:-1, 1:-1, :-2]
    return summed


def apply_level(field, level_data):
    return level_data[3] * field - neighbour_sum(level_data[0](field), level_data[1], level_data[2])


def smooth_once(iterate, source, level_data):
    return iterate + RELAXATION * (source - apply_level(iterate, level_data)) / level_data[3]


def relax_from_zero(source, level_data, sweeps_count):
    iterate = RELAXATION * source / level_data[3]
    for repeat in range(sweeps_count - 1):
        iterate = smooth_once(iterate, source, level_data)
    return iterate


def restrict(field):
    span_first, span_second, span_third = field.shape
    return field.reshape(span_first // 2, 2, span_second // 2, 2, span_third // 2, 2).mean(axis=(1, 3, 5))


def prolong(field):
    span_first, span_second, span_third = field.shape
    spread = jnp.broadcast_to(field[:, None, :, None, :, None], (span_first, 2, span_second, 2, span_third, 2))
    return spread.reshape(2 * span_first, 2 * span_second, 2 * span_third)


def multigrid_cycle(source, levels, coarse_solve):
    level_data = levels[0]
    iterate = relax_from_zero(source, level_data, SWEEPS)
    residue = source - apply_level(iterate, level_data)
    if len(levels) > 1:
        correction = multigrid_cycle(restrict(residue), levels[1:], coarse_solve)
    else:
        correction = coarse_solve(restrict(residue))
    iterate = iterate + prolong(correction)
    for repeat in range(SWEEPS):
        iterate = smooth_once(iterate, source, level_data)
    return iterate


def pressure_solve(source, levels, coarse_solve):
    iterate = multigrid_cycle(source, levels, coarse_solve)
    for repeat in range(CYCLES - 1):
        iterate = iterate + multigrid_cycle(source - apply_level(iterate, levels[0]), levels, coarse_solve)
    return iterate


def divergence(fluxes, padder):
    first = padder(fluxes[0])[:-2, 1:-1, 1:-1]
    second = padder(fluxes[1])[1:-1, :-2, 1:-1]
    third = padder(fluxes[2])[1:-1, 1:-1, :-2]
    return (fluxes[0] - first) + (fluxes[1] - second) + (fluxes[2] - third)


def upward_differences(field, padder):
    padded = padder(field)
    return (padded[2:, 1:-1, 1:-1] - field, padded[1:-1, 2:, 1:-1] - field, padded[1:-1, 1:-1, 2:] - field)


def closure_plane(feature_plane, weight_in, bias_in, weight_out):
    columns = feature_plane.reshape(feature_plane.shape[0], -1)
    before = jnp.dot(weight_in.T, columns, preferred_element_type=jnp.float32) + bias_in[:, None]
    gate = jax.nn.sigmoid(before)
    hidden = (before * gate).astype(jnp.bfloat16)
    output = jnp.dot(weight_out.T, hidden, preferred_element_type=jnp.float32)
    return output.reshape((3,) + feature_plane.shape[1:])


def closure_field(features, weight_in, bias_in, weight_out):
    def one_plane(index):
        feature_plane = lax.dynamic_index_in_dim(features, index, 1, keepdims=False)
        return closure_plane(feature_plane, weight_in, bias_in, weight_out)

    stacked = lax.map(one_plane, jnp.arange(features.shape[1], dtype=jnp.int32))
    return jnp.moveaxis(stacked, 0, 1)


def gradient_plane(totals, feature_plane, grad_plane, weight_in, bias_in, weight_out):
    columns = feature_plane.reshape(feature_plane.shape[0], -1)
    before = jnp.dot(weight_in.T, columns, preferred_element_type=jnp.float32) + bias_in[:, None]
    gate = jax.nn.sigmoid(before)
    hidden = (before * gate).astype(jnp.bfloat16)
    upstream = grad_plane.reshape(3, -1).astype(jnp.bfloat16)
    grad_out = lax.dot_general(hidden, upstream, (((1,), (1,)), ((), ())), preferred_element_type=jnp.float32)
    grad_hidden = jnp.dot(weight_out, upstream, preferred_element_type=jnp.float32)
    grad_before = grad_hidden * (gate * (1.0 + before * (1.0 - gate)))
    grad_bias = jnp.sum(grad_before, axis=1)
    grad_in = lax.dot_general(columns, grad_before.astype(jnp.bfloat16), (((1,), (1,)), ((), ())), preferred_element_type=jnp.float32)
    return (totals[0] + grad_in, totals[1] + grad_bias, totals[2] + grad_out)


def closure_gradients(features, grad_correction, weight_in, bias_in, weight_out):
    def step_plane(totals, index):
        feature_plane = lax.dynamic_index_in_dim(features, index, 1, keepdims=False)
        grad_plane = lax.dynamic_index_in_dim(grad_correction, index, 1, keepdims=False)
        return gradient_plane(totals, feature_plane, grad_plane, weight_in, bias_in, weight_out), None

    start = (jnp.zeros(weight_in.shape, jnp.float32), jnp.zeros(bias_in.shape, jnp.float32), jnp.zeros(weight_out.shape, jnp.float32))
    totals, unused = lax.scan(step_plane, start, jnp.arange(features.shape[1], dtype=jnp.int32))
    return totals


def training_step(velocity, features, target, weight_in, bias_in, weight_out, levels, coarse_solve, fine_factors, cells_total):
    padder = levels[0][0]
    upper_coefs = levels[0][1]
    outlets = tuple(fine_factors[direction][1].reshape(SHAPES[direction]) for direction in range(3))
    correction = closure_field(features, weight_in, bias_in, weight_out)
    fluxes = tuple((velocity[direction] + correction[direction]) * outlets[direction] for direction in range(3))
    source = -divergence(fluxes, padder)
    pressure = pressure_solve(source, levels, coarse_solve)
    rises = upward_differences(pressure, padder)
    new_velocity = jnp.stack([fluxes[direction] - upper_coefs[direction] * rises[direction] for direction in range(3)])
    misfit = (new_velocity - target) / cells_total
    weighted = tuple(upper_coefs[direction] * misfit[direction] for direction in range(3))
    grad_pressure = divergence(weighted, padder)
    grad_source = pressure_solve(grad_pressure, levels, coarse_solve)
    drops = upward_differences(grad_source, padder)
    grad_correction = jnp.stack([(misfit[direction] + drops[direction]) * outlets[direction] for direction in range(3)])
    totals = closure_gradients(features, grad_correction, weight_in, bias_in, weight_out)
    return new_velocity, totals


def reference(velocity, features, density, target, weight_in, bias_in, weight_out, open_faces):
    def level_factors(shape_now):
        return tuple(edge_factors(shape_now[direction], 0, shape_now[direction], open_faces[2 * direction], open_faces[2 * direction + 1]) for direction in range(3))

    def make_level(level_density, weight):
        upper_coefs, lower_coefs, diagonal = coefficients(zero_padded(level_density), level_factors(level_density.shape), weight)
        return (zero_padded, upper_coefs, lower_coefs, diagonal)

    density_one = restrict(density)
    density_two = restrict(density_one)
    levels = (make_level(density, 1.0), make_level(density_one, 0.25))
    coarse_level = make_level(density_two, 0.0625)

    def coarse_solve(source):
        return relax_from_zero(source, coarse_level, COARSE_SWEEPS)

    new_velocity, totals = training_step(velocity, features, target, weight_in, bias_in, weight_out, levels, coarse_solve, level_factors(density.shape), density.size)
    return (new_velocity, totals[0], totals[1], totals[2])
```

```python
import jax
import jax.numpy as jnp
from jax import lax
from jax.experimental import pallas as pl
from jax.experimental.pallas import tpu as pltpu
from jax.sharding import Mesh
from jax.sharding import PartitionSpec as P

GY = ("gy_0", "gy_1")
XY = ("gx", "gy_0", "gy_1")
ALL = ("gx", "gy_0", "gy_1", "gz")
F32 = jnp.float32
BF16 = jnp.bfloat16
HIGHEST = lax.Precision.HIGHEST
MASS_SHIFT = 0.05
CELLS = 2097152.0

NXP, NYP, NZP = 22, 24, 256
REGION = (NXP, NYP, NZP)
L1 = (20, 32, 128)
L2 = (10, 16, 128)


def shaped(shape, dtype=F32):
    return jax.ShapeDtypeStruct(shape, dtype)


def call(body, outs, args, scratch=(), smem=()):
    specs = [
        pl.BlockSpec(memory_space=pltpu.SMEM if i in smem else pltpu.VMEM) for i in range(len(args))
    ]
    return pl.pallas_call(
        body,
        out_shape=outs,
        in_specs=specs,
        out_specs=[pl.BlockSpec(memory_space=pltpu.VMEM)] * len(outs),
        scratch_shapes=list(scratch),
        compiler_params=pltpu.CompilerParams(vmem_limit_bytes=48 << 20),
    )(*args)


def back(x, axis):
    return pltpu.roll(x, x.shape[axis] - 1, axis)


def forth(x, axis):
    return pltpu.roll(x, 1, axis)


def exact_dot(a, b):
    return jnp.dot(a, b, precision=HIGHEST, preferred_element_type=F32)


def planes(lo, hi, body, unroll=2):
    def step(i, carry):
        body(i)
        return carry

    lax.fori_loop(lo, hi, step, 0, unroll=unroll)


def around(src, ax, ay, az, i):
    v = src[i]
    y, z = ay[i], az[i]
    total = ax[i] * src[i + 1] + ax[i - 1] * src[i - 1]
    total = total + (y * back(v, 0) + forth(y * v, 0))
    return v, total + (z * back(v, 1) + forth(z * v, 1))


def sweep(src, dst, s, w, ax, ay, az, lo, hi):
    def one(i):
        v, total = around(src, ax, ay, az, i)
        dst[i] = 0.2 * v + w[i] * (s[i] + total)

    planes(lo, hi, one)


def first_sweep(dst, s, w, lo, hi):
    def one(i):
        dst[i] = w[i] * s[i]

    planes(lo, hi, one)


def face(here, there, weight, low, high):
    has, next_has = here > 0.0, there > 0.0
    factor = jnp.where(
        has, jnp.where(next_has, F32(1.0), high), jnp.where(next_has, low, F32(0.0))
    )
    total = jnp.where(has | next_has, here + there, F32(1.0))
    return weight * 2.0 / total * factor


def coefficients(rho, opens, weight, refs, lo, hi, whole_y):
    ax, ay, az, w, d = refs
    low, high = opens
    count = rho.shape[1]

    def one_face(i):
        ax[i] = face(rho[i], rho[i + 1], weight, low[0], high[0])

    planes(lo - 1, hi, one_face, 1)

    def one(i):
        r = rho[i]
        after = back(r, 0)
        before = forth(r, 0)
        row = lax.broadcasted_iota(jnp.int32, r.shape, 0)
        if whole_y:
            after = jnp.where(row == count - 1, F32(0.0), after)
            before = jnp.where(row == 0, F32(0.0), before)
        up_y = face(r, after, weight, low[1], high[1])
        down_y = face(before, r, weight, low[1], high[1])
        up_z = face(r, back(r, 1), weight, low[2], high[2])
        diagonal = MASS_SHIFT + ax[i] + ax[i - 1] + up_y + down_y + up_z + forth(up_z, 1)
        ay[i] = jnp.where(row == count - 1, F32(0.0), up_y) if whole_y else up_y
        az[i] = up_z
        d[i] = diagonal
        w[i] = jnp.where(r > 0.0, 0.8 / diagonal, F32(0.0))

    planes(lo, hi, one, 1)


def lane_pairs(cells, kept, repeat):
    row = lax.broadcasted_iota(jnp.int32, (cells, kept), 0)
    col = lax.broadcasted_iota(jnp.int32, (cells, kept), 1)
    return jnp.where(row // 2 == col % repeat, F32(1.0), F32(0.0))


def lane_spread(cells, kept):
    row = lax.broadcasted_iota(jnp.int32, (cells, kept), 0)
    col = lax.broadcasted_iota(jnp.int32, (cells, kept), 1)
    return jnp.where(col // 2 == row, F32(1.0), F32(0.0))


def block_means(read, rows, out, out_row):
    pairs = [read(7 + 2 * k) + read(8 + 2 * k) for k in range(4)]
    rows[...] = exact_dot(jnp.concatenate(pairs, axis=0), lane_pairs(256, 128, 128))
    total = rows[pl.ds(0, 16, stride=2), :] + rows[pl.ds(1, 16, stride=2), :]
    out[out_row : out_row + 16, :] = 0.125 * total


def presmooth(s, v, va, coefs, rows, out):
    ax, ay, az, w, d = coefs
    first_sweep(v, s, w, 1, 21)
    sweep(v, va, s, w, ax, ay, az, 2, 20)
    sweep(va, v, s, w, ax, ay, az, 3, 19)

    def residue(i):
        centre, total = around(v, ax, ay, az, i)
        return (s[i] + total - d[i] * centre)[8:16]

    block_means(residue, rows, out, 0)


def opens_of(sc):
    values = [sc[3 + k].astype(F32) for k in range(6)]
    return values[0::2], values[1::2]


def start_body(sc, b, rho, ax, ay, az, w, d, v, out, va, rows):
    coefs = (ax, ay, az, w, d)
    for ref in (ax, ay, az, w, d, v):
        ref[0] = jnp.zeros((NYP, NZP), F32)
        ref[21] = jnp.zeros((NYP, NZP), F32)
    coefficients(rho, opens_of(sc), 1.0, coefs, 1, 21, False)
    presmooth(b, v, va, coefs, rows, out)
    block_means(lambda i: rho[i, 8:16, :], rows, out, 16)


def pre_body(b, ax, ay, az, w, d, v, out, va, rows):
    v[0] = jnp.zeros((NYP, NZP), F32)
    v[21] = jnp.zeros((NYP, NZP), F32)
    presmooth(b, v, va, (ax, ay, az, w, d), rows, out)


def again_body(b, p, ax, ay, az, w, d, s, v, out, va, rows):
    for ref in (s, v):
        ref[0] = jnp.zeros((NYP, NZP), F32)
        ref[21] = jnp.zeros((NYP, NZP), F32)

    def one(i):
        centre, total = around(p, ax, ay, az, i)
        s[i] = b[i] + total - d[i] * centre

    planes(1, 21, one)
    presmooth(s, v, va, (ax, ay, az, w, d), rows, out)


def whole_plane(parts, first, dst):
    for k in range(2):
        dst[k] = jnp.zeros((32, 128), F32)
        dst[18 + k] = jnp.zeros((32, 128), F32)
    for device in range(32):
        x, y = divmod(device, 8)
        for k in range(4):
            dst[2 + 4 * x + k, 4 * y : 4 * y + 4, :] = parts[
                device, first + 4 * k : first + 4 * k + 4, :
            ]


def restrict_whole(read, rows, dst):
    for k in range(8):
        rows[32 * k : 32 * k + 32, :] = read(2 + 2 * k) + read(3 + 2 * k)
    rows[...] = exact_dot(rows[...], lane_pairs(128, 128, 64))
    for k in range(8):
        total = (
            rows[pl.ds(32 * k, 16, stride=2), :] + rows[pl.ds(32 * k + 1, 16, stride=2), :]
        )
        dst[1 + k] = 0.125 * total


def coarse_body(
    sc, parts, ax1, ay1, az1, w1, d1, ax2, ay2, az2, w2, d2, rho1, rho2, rows
):
    for ref in (ax1, ay1, az1, w1, d1):
        ref[...] = jnp.zeros(L1, F32)
    for ref in (ax2, ay2, az2, w2, d2, rho2):
        ref[...] = jnp.zeros(L2, F32)
    opens = opens_of(sc)
    whole_plane(parts, 16, rho1)
    coefficients(rho1, opens, 0.25, (ax1, ay1, az1, w1, d1), 2, 18, True)
    restrict_whole(lambda i: rho1[i], rows, rho2)
    coefficients(rho2, opens, 0.0625, (ax2, ay2, az2, w2, d2), 1, 9, True)


def correct(
    sc, parts, coefs1, coefs2, s1, v1, u1, s2, v2, u2, rows, wide_a, wide_b
):
    ax1, ay1, az1, w1, d1 = coefs1
    ax2, ay2, az2, w2, d2 = coefs2
    whole_plane(parts, 0, s1)
    for ref in (v1, u1):
        for k in (0, 1, 18, 19):
            ref[k] = jnp.zeros((32, 128), F32)
    for ref in (v2, u2):
        for k in (0, 9):
            ref[k] = jnp.zeros((16, 128), F32)
    first_sweep(v1, s1, w1, 2, 18)
    sweep(v1, u1, s1, w1, ax1, ay1, az1, 2, 18)
    sweep(u1, v1, s1, w1, ax1, ay1, az1, 2, 18)

    def residue(i):
        centre, total = around(v1, ax1, ay1, az1, i)
        return s1[i] + total - d1[i] * centre

    restrict_whole(residue, rows, s2)
    first_sweep(v2, s2, w2, 1, 9)
    for k in range(5):
        a, b = (v2, u2) if k % 2 == 0 else (u2, v2)
        sweep(a, b, s2, w2, ax2, ay2, az2, 1, 9)
    spread = exact_dot(
        jnp.concatenate([u2[1 + k] for k in range(8)], axis=0), lane_spread(128, 128)
    )
    rows[pl.ds(0, 128, stride=2), :] = spread
    rows[pl.ds(1, 128, stride=2), :] = spread
    for k in range(8):
        more = rows[32 * k : 32 * k + 32, :]
        v1[2 + 2 * k] = v1[2 + 2 * k] + more
        v1[3 + 2 * k] = v1[3 + 2 * k] + more
    sweep(v1, u1, s1, w1, ax1, ay1, az1, 2, 18)
    sweep(u1, v1, s1, w1, ax1, ay1, az1, 2, 18)
    sweep(v1, u1, s1, w1, ax1, ay1, az1, 2, 18)
    base = sc[0] * 4
    near = jnp.concatenate([u1[base + k] for k in range(8)], axis=0)
    wide = exact_dot(near, lane_spread(128, 256))
    for lanes, ref in ((slice(0, 128), wide_a), (slice(128, 256), wide_b)):
        for k in range(8):
            ref[80 * k : 80 * k + 8, :] = jnp.zeros((8, 128), F32)
            ref[80 * k + 72 : 80 * k + 80, :] = jnp.zeros((8, 128), F32)
            part = wide[32 * k : 32 * k + 32, lanes]
            ref[pl.ds(80 * k + 8, 32, stride=2), :] = part
            ref[pl.ds(80 * k + 9, 32, stride=2), :] = part


def postsmooth(sc, s, v, coefs, wide_a, wide_b, va, vb):
    ax, ay, az, w = coefs
    row = pl.multiple_of(sc[1] * 8, 8)
    for i in range(3, 19):
        k = (i - 3) // 2
        more = jnp.concatenate(
            [wide_a[pl.ds(80 * k + row, 24), :], wide_b[pl.ds(80 * k + row, 24), :]], axis=1
        )
        va[i] = v[i] + more
    sweep(va, vb, s, w, ax, ay, az, 4, 18)
    sweep(vb, va, s, w, ax, ay, az, 5, 17)


POST_SCRATCH = (
    [pltpu.VMEM(L1, F32)] * 3
    + [pltpu.VMEM(L2, F32)] * 3
    + [pltpu.VMEM((256, 128), F32)]
    + [pltpu.VMEM((640, 128), F32)] * 2
    + [pltpu.VMEM(REGION, F32)] * 2
)


def post_own_body(
    sc, parts, ax1, ay1, az1, w1, d1, ax2, ay2, az2, w2, d2, s, v, ax, ay, az, w, out, *scratch
):
    *inner, wide_a, wide_b, va, vb = scratch
    correct(
        sc,
        parts,
        (ax1, ay1, az1, w1, d1),
        (ax2, ay2, az2, w2, d2),
        *inner,
        wide_a,
        wide_b,
    )
    postsmooth(sc, s, v, (ax, ay, az, w), wide_a, wide_b, va, vb)
    for i in range(8):
        centre, total = around(va, ax, ay, az, i + 7)
        new = 0.2 * centre + w[i + 7] * (s[i + 7] + total)
        out[i] = new[8:16, 0:128]


def post_near_body(
    sc, parts, ax1, ay1, az1, w1, d1, ax2, ay2, az2, w2, d2, s, v, ax, ay, az, w, p, out, *scratch
):
    *inner, wide_a, wide_b, va, vb = scratch
    correct(
        sc,
        parts,
        (ax1, ay1, az1, w1, d1),
        (ax2, ay2, az2, w2, d2),
        *inner,
        wide_a,
        wide_b,
    )
    postsmooth(sc, s, v, (ax, ay, az, w), wide_a, wide_b, va, vb)
    for i in range(10):
        centre, total = around(va, ax, ay, az, i + 6)
        out[i] = p[i + 6] + 0.2 * centre + w[i + 6] * (s[i + 6] + total)


def closure_body(
    sc, features, kin, bias, kout, velocity, target, flux, slope, hidden, face_x, face_y, face_z
):
    _, high = opens_of(sc)
    high_x = jnp.where(sc[0] == 3, high[0], F32(1.0))
    high_y = jnp.where(sc[1] == 7, high[1], F32(1.0))
    high_z = jnp.where(sc[2] == 7, high[2], F32(1.0))
    row = lax.broadcasted_iota(jnp.int32, (8, 128), 0)
    col = lax.broadcasted_iota(jnp.int32, (8, 128), 1)
    factor_y = jnp.where(row == 7, high_y, F32(1.0))
    factor_z = jnp.where(col == 127, high_z, F32(1.0))

    def one(x):
        columns = features[:, x, :, :].astype(F32).reshape(128, 128).astype(BF16)
        before = jnp.dot(kin[...], columns, preferred_element_type=F32) + bias[...]
        gate = 1.0 / (1.0 + jnp.exp(-before))
        unit = (before * gate).astype(BF16)
        hidden[x] = unit
        slope[x] = gate * (1.0 + before * (1.0 - gate))
        shift = jnp.dot(kout[...], unit, preferred_element_type=F32)
        factor_x = jnp.where(x == 7, high_x, F32(1.0))
        flux[0, x] = (velocity[0, x] + shift[0:8]) * factor_x
        flux[1, x] = (velocity[1, x] + shift[8:16]) * factor_y
        flux[2, x] = (velocity[2, x] + shift[16:24]) * factor_z

    planes(0, 8, one, 1)
    face_x[0] = flux[0, 7]
    face_x[1] = target[0, 7]
    for x in range(8):
        face_y[0, x : x + 1, :] = flux[1, x, 7:8, :]
        face_y[1, x : x + 1, :] = target[1, x, 7:8, :]
    face_z[0] = flux[2]
    face_z[1] = target[2]


def shifted(field, low_x, low_y, low_z, x):
    row = lax.broadcasted_iota(jnp.int32, (8, 128), 0)
    col = lax.broadcasted_iota(jnp.int32, (8, 128), 1)
    before_x = low_x() if x == 0 else field(0, x - 1)
    before_y = jnp.where(row == 0, low_y(x), forth(field(1, x), 0))
    before_z = jnp.where(col == 0, low_z(x), forth(field(2, x), 1))
    return before_x, before_y, before_z


def source_body(flux, low_x, low_y, low_z, out):
    for x in range(8):
        bx, by, bz = shifted(
            lambda d, i: flux[d, i],
            lambda: low_x[0],
            lambda i: jnp.broadcast_to(low_y[0, i : i + 1, :], (8, 128)),
            lambda i: forth(low_z[0, i], 1),
            x,
        )
        out[x] = -((flux[0, x] - bx) + (flux[1, x] - by) + (flux[2, x] - bz))


def middle_body(sc, near, flux, target, low_x, low_y, low_z, ax, ay, az, new, misfit, out):
    scale = F32(1.0 / CELLS)
    inner = [jnp.where(sc[d] > 0, F32(1.0), F32(0.0)) for d in range(3)]

    def rises(i):
        p = near[i]
        return p, back(p, 0) - p, back(p, 1) - p

    for x in range(8):
        p, rise_y, rise_z = rises(x + 1)
        rise_x = near[x + 2] - p
        parts = (ax[x + 7] * rise_x, ay[x + 7] * rise_y, az[x + 7] * rise_z)
        for d in range(3):
            value = flux[d, x] - parts[d][8:16, 0:128]
            new[d, x] = value
            misfit[d, x] = (value - target[d, x]) * scale

    def low_weighted_x():
        up = ax[6, 8:16, 0:128]
        rise = (near[1] - near[0])[8:16, 0:128]
        return up * ((low_x[0] - up * rise - low_x[1]) * (scale * inner[0]))

    def low_weighted_y(x):
        up = ay[x + 7, 7:8, 0:128]
        rise = near[x + 1, 8:9, 0:128] - near[x + 1, 7:8, 0:128]
        value = low_y[0, x : x + 1, :] - up * rise - low_y[1, x : x + 1, :]
        return jnp.broadcast_to(up * (value * (scale * inner[1])), (8, 128))

    def low_weighted_z(x):
        p = near[x + 1, 8:16, :]
        rise = (back(p, 1) - p)[:, 128:256]
        up = az[x + 7, 8:16, 128:256]
        value = up * ((low_z[0, x] - up * rise - low_z[1, x]) * (scale * inner[2]))
        return forth(value, 1)

    refs = (ax, ay, az)

    def weighted(d, x):
        return refs[d][x + 7, 8:16, 0:128] * misfit[d, x]

    for x in range(8):
        bx, by, bz = shifted(weighted, low_weighted_x, low_weighted_y, low_weighted_z, x)
        out[x] = (weighted(0, x) - bx) + (weighted(1, x) - by) + (weighted(2, x) - bz)


def gradient_body(sc, near, misfit, features, slope, hidden, kback, out, acc_in, acc_bias, acc_out):
    _, high = opens_of(sc)
    high_x = jnp.where(sc[0] == 3, high[0], F32(1.0))
    high_y = jnp.where(sc[1] == 7, high[1], F32(1.0))
    high_z = jnp.where(sc[2] == 7, high[2], F32(1.0))
    row = lax.broadcasted_iota(jnp.int32, (8, 128), 0)
    col = lax.broadcasted_iota(jnp.int32, (8, 128), 1)
    factor_y = jnp.where(row == 7, high_y, F32(1.0))
    factor_z = jnp.where(col == 127, high_z, F32(1.0))
    acc_in[...] = jnp.zeros((128, 512), F32)
    acc_bias[...] = jnp.zeros((512, 128), F32)
    acc_out[...] = jnp.zeros((24, 512), F32)
    across = (((1,), (1,)), ((), ()))

    def one(x):
        p = near[x + 1]
        rise_x = (near[x + 2] - p)[8:16, 0:128]
        rise_y = (back(p, 0) - p)[8:16, 0:128]
        rise_z = (back(p, 1) - p)[8:16, 0:128]
        factor_x = jnp.where(x == 7, high_x, F32(1.0))
        grads = jnp.concatenate(
            [
                (misfit[0, x] + rise_x) * factor_x,
                (misfit[1, x] + rise_y) * factor_y,
                (misfit[2, x] + rise_z) * factor_z,
            ],
            axis=0,
        ).astype(BF16)
        columns = features[:, x, :, :].astype(F32).reshape(128, 128).astype(BF16)
        grad_before = jnp.dot(kback[...], grads, preferred_element_type=F32) * slope[x]
        acc_bias[...] += grad_before
        acc_in[...] += lax.dot_general(
            columns, grad_before.astype(BF16), across, preferred_element_type=F32
        )
        acc_out[...] += lax.dot_general(grads, hidden[x], across, preferred_element_type=F32)

    planes(0, 8, one, 1)

    def same(count):
        r = lax.broadcasted_iota(jnp.int32, (count, 512), 0)
        c = lax.broadcasted_iota(jnp.int32, (count, 512), 1)
        return r % 8 == c % 8

    def grouped(count, groups):
        r = lax.broadcasted_iota(jnp.int32, (groups, count), 0)
        c = lax.broadcasted_iota(jnp.int32, (groups, count), 1)
        return jnp.where(c // 8 == r, F32(1.0), F32(0.0))

    hr = lax.broadcasted_iota(jnp.int32, (512, 64), 0)
    hc = lax.broadcasted_iota(jnp.int32, (512, 64), 1)
    fold = jnp.where(hr // 8 == hc, F32(1.0), F32(0.0))
    in_part = exact_dot(grouped(128, 16), jnp.where(same(128), acc_in[...], F32(0.0)))
    out_part = exact_dot(grouped(24, 8), jnp.where(same(24), acc_out[...], F32(0.0)))
    bias_part = lax.dot_general(
        jnp.ones((8, 128), F32), acc_bias[...], across, precision=HIGHEST, preferred_element_type=F32
    )
    folded = exact_dot(jnp.concatenate([in_part, out_part, bias_part], axis=0), fold)
    out[0:8, 0:64] = folded[0:8]
    out[0:8, 64:128] = folded[8:16]
    out[8:16, 0:64] = folded[16:24]
    out[8:16, 64:128] = folded[24:32]


def ups(axis):
    count = lax.axis_size(axis)
    return [(i, i + 1) for i in range(count - 1)]


def downs(axis):
    return [(b, a) for a, b in ups(axis)]


def exchanged(own):
    after = lax.ppermute(own, "gz", downs("gz"))
    before = lax.ppermute(own, "gz", ups("gz"))
    lane = lax.broadcasted_iota(jnp.int32, own.shape, 3)
    wide = jnp.concatenate([own, jnp.where(lane < 64, after, before)], axis=3)
    low = lax.ppermute(wide[:, 1:8], "gx", ups("gx"))
    high = lax.ppermute(wide[:, 0:7], "gx", downs("gx"))
    wide = jnp.concatenate([low, wide, high], axis=1)
    low = lax.ppermute(wide, GY, ups(GY))
    high = lax.ppermute(wide, GY, downs(GY))
    return jnp.concatenate([low, wide, high], axis=2)


def over_plane(part):
    copies = jnp.broadcast_to(part, (32, *part.shape))
    return lax.all_to_all(copies, XY, split_axis=0, concat_axis=0, tiled=True)


def summed(part, axes):
    for axis in axes:
        copies = jnp.broadcast_to(part, (lax.axis_size(axis), *part.shape))
        part = jnp.sum(lax.all_to_all(copies, axis, split_axis=0, concat_axis=0, tiled=True), axis=0)
    return part


def per_device(velocity, features, density, target, weight_in, bias_in, weight_out, open_faces):
    place = jnp.stack([lax.axis_index("gx"), lax.axis_index(GY), lax.axis_index("gz")])
    sc = jnp.concatenate([place.astype(jnp.int32), open_faces])
    eye = jnp.eye(8, dtype=BF16)
    kin = jnp.kron(weight_in.T, eye)
    kout = jnp.kron(weight_out.T, eye)
    kback = jnp.kron(weight_out, eye)
    bias = jnp.broadcast_to(bias_in[:, None, None], (64, 8, 128)).reshape(512, 128)
    block = (8, 8, 128)
    flux, slope, hidden, face_x, face_y, face_z = call(
        closure_body,
        [
            shaped((3, *block)),
            shaped((8, 512, 128)),
            shaped((8, 512, 128), BF16),
            shaped((2, 8, 128)),
            shaped((2, 8, 128)),
            shaped((2, *block)),
        ],
        (sc, features, kin, bias, kout, velocity, target),
        smem=(0,),
    )
    low_x = lax.ppermute(face_x, "gx", ups("gx"))
    low_y = lax.ppermute(face_y, GY, ups(GY))
    low_z = lax.ppermute(face_z, "gz", ups("gz"))
    (source,) = call(source_body, [shaped(block)], (flux, low_x, low_y, low_z))
    both = exchanged(jnp.stack([source, density]))
    region = shaped(REGION)
    one_region = [pltpu.VMEM(REGION, F32), pltpu.VMEM((32, 128), F32)]
    *coefs, v, part = call(
        start_body,
        [region] * 6 + [shaped((32, 128))],
        (sc, both[0], both[1]),
        one_region,
        smem=(0,),
    )
    ax, ay, az, w, d = coefs
    parts = over_plane(part)
    coarse = call(
        coarse_body,
        [shaped(L1)] * 5 + [shaped(L2)] * 5,
        (sc, parts),
        [pltpu.VMEM(L1, F32), pltpu.VMEM(L2, F32), pltpu.VMEM((256, 128), F32)],
        smem=(0,),
    )

    def finish_solve(b, v, parts):
        (own,) = call(
            post_own_body,
            [shaped(block)],
            (sc, parts, *coarse, b, v, ax, ay, az, w),
            POST_SCRATCH,
            smem=(0,),
        )
        p = exchanged(own[None])[0]
        s, v, part = call(
            again_body, [region, region, shaped((16, 128))], (b, p, *coefs), one_region
        )
        (near,) = call(
            post_near_body,
            [shaped((10, NYP, NZP))],
            (sc, over_plane(part), *coarse, s, v, ax, ay, az, w, p),
            POST_SCRATCH,
            smem=(0,),
        )
        return near

    near = finish_solve(both[0], v, parts)
    new_velocity, misfit, grad_pressure = call(
        middle_body,
        [shaped((3, *block)), shaped((3, *block)), shaped(block)],
        (sc, near, flux, target, low_x, low_y, low_z, ax, ay, az),
        smem=(0,),
    )
    b = exchanged(grad_pressure[None])[0]
    v, part = call(pre_body, [region, shaped((16, 128))], (b, *coefs), one_region)
    near = finish_solve(b, v, over_plane(part))
    (packed,) = call(
        gradient_body,
        [shaped((16, 128))],
        (sc, near, misfit, features, slope, hidden, kback),
        [pltpu.VMEM((128, 512), F32), pltpu.VMEM((512, 128), F32), pltpu.VMEM((24, 512), F32)],
        smem=(0,),
    )
    total = summed(packed, (("gy_1", "gz"), ("gx", "gy_0")))
    grad_in = jnp.concatenate([total[0:8, 0:64], total[0:8, 64:128]], axis=0)
    return new_velocity, grad_in, total[8, 64:128], total[8:11, 0:64].T


def solution(mesh):
    split = Mesh(
        mesh.devices.reshape(mesh.shape["gx"], 4, 2, mesh.shape["gz"]), ("gx", "gy_0", "gy_1", "gz")
    )
    placed = (
        P(None, "gx", GY, "gz"),
        P(None, "gx", GY, "gz"),
        P("gx", GY, "gz"),
        P(None, "gx", GY, "gz"),
        P(),
        P(),
        P(),
        P(),
    )
    return jax.shard_map(
        per_device,
        mesh=split,
        in_specs=placed,
        out_specs=(P(None, "gx", GY, "gz"), P(), P(), P()),
        check_vma=False,
    )
```

```python
import jax
import jax.numpy as jnp
from jax import lax
from jax.experimental import pallas as pl
from jax.experimental.pallas import tpu as pltpu
from jax.sharding import Mesh
from jax.sharding import PartitionSpec as P

GY = ("gy_0", "gy_1")
XY = ("gx", "gy_0", "gy_1")
ALL = ("gx", "gy_0", "gy_1", "gz")
F32 = jnp.float32
BF16 = jnp.bfloat16
HIGHEST = lax.Precision.HIGHEST
MASS_SHIFT = 0.05
CELLS = 2097152.0

NXP, NYP, NZP = 22, 24, 256
REGION = (NXP, NYP, NZP)
L1 = (20, 32, 128)
L2 = (10, 16, 128)
UNROLL = {24: 2, 32: 8, 16: 8}


def shaped(shape, dtype=F32):
    return jax.ShapeDtypeStruct(shape, dtype)


def call(body, outs, args, scratch=(), smem=()):
    specs = [
        pl.BlockSpec(memory_space=pltpu.SMEM if i in smem else pltpu.VMEM) for i in range(len(args))
    ]
    return pl.pallas_call(
        body,
        out_shape=outs,
        in_specs=specs,
        out_specs=[pl.BlockSpec(memory_space=pltpu.VMEM)] * len(outs),
        scratch_shapes=list(scratch),
        compiler_params=pltpu.CompilerParams(vmem_limit_bytes=20 << 20),
    )(*args)


def back(x, axis):
    return pltpu.roll(x, x.shape[axis] - 1, axis)


def forth(x, axis):
    return pltpu.roll(x, 1, axis)


def exact_dot(a, b):
    return jnp.dot(a, b, precision=HIGHEST, preferred_element_type=F32)


def chosen_dot(a, b):
    high = a.astype(BF16)
    rest = a - high.astype(F32)
    middle = rest.astype(BF16)
    low = (rest - middle.astype(F32)).astype(BF16)
    count = a.shape[0]
    parts = jnp.dot(
        jnp.concatenate([high, middle, low], axis=0), b.astype(BF16), preferred_element_type=F32
    )
    return (parts[2 * count :] + parts[count : 2 * count]) + parts[:count]


def planes(lo, hi, body, unroll=2):
    def step(i, carry):
        body(i)
        return carry

    lax.fori_loop(lo, hi, step, 0, unroll=unroll)


def around(src, ax, ay, az, i):
    v = src[i]
    y, z = ay[i], az[i]
    total = ax[i] * src[i + 1] + ax[i - 1] * src[i - 1]
    total = total + (y * back(v, 0) + forth(y * v, 0))
    return v, total + (z * back(v, 1) + forth(z * v, 1))


def sweep(src, dst, s, w, ax, ay, az, lo, hi):
    def one(i):
        v, total = around(src, ax, ay, az, i)
        dst[i] = 0.2 * v + w[i] * (s[i] + total)

    planes(lo, hi, one, UNROLL[src.shape[1]])


def first_sweep(dst, s, w, lo, hi):
    def one(i):
        dst[i] = w[i] * s[i]

    planes(lo, hi, one, UNROLL[s.shape[1]])


def face(here, there, weight, low, high):
    has, next_has = here > 0.0, there > 0.0
    factor = jnp.where(
        has, jnp.where(next_has, F32(1.0), high), jnp.where(next_has, low, F32(0.0))
    )
    total = jnp.where(has | next_has, here + there, F32(1.0))
    return weight * 2.0 / total * factor


def coefficients(rho, opens, weight, refs, lo, hi, whole_y):
    ax, ay, az, w, d = refs
    low, high = opens
    count = rho.shape[1]

    def one_face(i):
        ax[i] = face(rho[i], rho[i + 1], weight, low[0], high[0])

    planes(lo - 1, hi, one_face, 2)

    def one(i):
        r = rho[i]
        after = back(r, 0)
        before = forth(r, 0)
        row = lax.broadcasted_iota(jnp.int32, r.shape, 0)
        if whole_y:
            after = jnp.where(row == count - 1, F32(0.0), after)
            before = jnp.where(row == 0, F32(0.0), before)
        up_y = face(r, after, weight, low[1], high[1])
        down_y = face(before, r, weight, low[1], high[1])
        up_z = face(r, back(r, 1), weight, low[2], high[2])
        diagonal = MASS_SHIFT + ax[i] + ax[i - 1] + up_y + down_y + up_z + forth(up_z, 1)
        ay[i] = jnp.where(row == count - 1, F32(0.0), up_y) if whole_y else up_y
        az[i] = up_z
        d[i] = diagonal
        w[i] = jnp.where(r > 0.0, 0.8 / diagonal, F32(0.0))

    planes(lo, hi, one, 2)


def lane_pairs(cells, kept, repeat):
    row = lax.broadcasted_iota(jnp.int32, (cells, kept), 0)
    col = lax.broadcasted_iota(jnp.int32, (cells, kept), 1)
    return jnp.where(row // 2 == col % repeat, F32(1.0), F32(0.0))


def lane_spread(cells, kept):
    row = lax.broadcasted_iota(jnp.int32, (cells, kept), 0)
    col = lax.broadcasted_iota(jnp.int32, (cells, kept), 1)
    return jnp.where(col // 2 == row, F32(1.0), F32(0.0))


def block_means(read, rows, out, out_row):
    pairs = [read(7 + 2 * k) + read(8 + 2 * k) for k in range(4)]
    rows[...] = chosen_dot(jnp.concatenate(pairs, axis=0), lane_pairs(256, 128, 128))
    total = rows[pl.ds(0, 16, stride=2), :] + rows[pl.ds(1, 16, stride=2), :]
    out[out_row : out_row + 16, :] = 0.125 * total


def presmooth(s, v, va, coefs, rows, out):
    ax, ay, az, w, d = coefs
    first_sweep(v, s, w, 1, 21)
    sweep(v, va, s, w, ax, ay, az, 2, 20)
    sweep(va, v, s, w, ax, ay, az, 3, 19)

    def residue(i):
        centre, total = around(v, ax, ay, az, i)
        return (s[i] + total - d[i] * centre)[8:16]

    block_means(residue, rows, out, 0)


def opens_of(sc):
    values = [sc[3 + k].astype(F32) for k in range(6)]
    return values[0::2], values[1::2]


def start_body(sc, b, rho, ax, ay, az, w, d, v, out, va, rows):
    coefs = (ax, ay, az, w, d)
    for ref in (ax, ay, az, w, d, v):
        ref[0] = jnp.zeros((NYP, NZP), F32)
        ref[21] = jnp.zeros((NYP, NZP), F32)
    coefficients(rho, opens_of(sc), 1.0, coefs, 1, 21, False)
    presmooth(b, v, va, coefs, rows, out)
    block_means(lambda i: rho[i, 8:16, :], rows, out, 16)


def pre_body(b, ax, ay, az, w, d, v, out, va, rows):
    v[0] = jnp.zeros((NYP, NZP), F32)
    v[21] = jnp.zeros((NYP, NZP), F32)
    presmooth(b, v, va, (ax, ay, az, w, d), rows, out)


def again_body(b, p, ax, ay, az, w, d, s, v, out, va, rows):
    for ref in (s, v):
        ref[0] = jnp.zeros((NYP, NZP), F32)
        ref[21] = jnp.zeros((NYP, NZP), F32)

    def one(i):
        centre, total = around(p, ax, ay, az, i)
        s[i] = b[i] + total - d[i] * centre

    planes(1, 21, one)
    presmooth(s, v, va, (ax, ay, az, w, d), rows, out)


def whole_plane(parts, first, dst):
    for k in range(2):
        dst[k] = jnp.zeros((32, 128), F32)
        dst[18 + k] = jnp.zeros((32, 128), F32)
    for device in range(32):
        x, y = divmod(device, 8)
        for k in range(4):
            dst[2 + 4 * x + k, 4 * y : 4 * y + 4, :] = parts[
                device, first + 4 * k : first + 4 * k + 4, :
            ]


def restrict_whole(read, rows, dst):
    for k in range(8):
        rows[32 * k : 32 * k + 32, :] = read(2 + 2 * k) + read(3 + 2 * k)
    rows[...] = chosen_dot(rows[...], lane_pairs(128, 128, 64))
    for k in range(8):
        total = (
            rows[pl.ds(32 * k, 16, stride=2), :] + rows[pl.ds(32 * k + 1, 16, stride=2), :]
        )
        dst[1 + k] = 0.125 * total


def coarse_body(
    sc, parts, ax1, ay1, az1, w1, d1, ax2, ay2, az2, w2, d2, rho1, rho2, rows
):
    for ref in (ax1, ay1, az1, w1, d1):
        ref[...] = jnp.zeros(L1, F32)
    for ref in (ax2, ay2, az2, w2, d2, rho2):
        ref[...] = jnp.zeros(L2, F32)
    opens = opens_of(sc)
    whole_plane(parts, 16, rho1)
    coefficients(rho1, opens, 0.25, (ax1, ay1, az1, w1, d1), 2, 18, True)
    restrict_whole(lambda i: rho1[i], rows, rho2)
    coefficients(rho2, opens, 0.0625, (ax2, ay2, az2, w2, d2), 1, 9, True)


def correct(
    sc, parts, coefs1, coefs2, s1, v1, u1, s2, v2, u2, rows, wide_a, wide_b
):
    ax1, ay1, az1, w1, d1 = coefs1
    ax2, ay2, az2, w2, d2 = coefs2
    whole_plane(parts, 0, s1)
    for ref in (v1, u1):
        for k in (0, 1, 18, 19):
            ref[k] = jnp.zeros((32, 128), F32)
    for ref in (v2, u2):
        for k in (0, 9):
            ref[k] = jnp.zeros((16, 128), F32)
    first_sweep(v1, s1, w1, 2, 18)
    sweep(v1, u1, s1, w1, ax1, ay1, az1, 2, 18)
    sweep(u1, v1, s1, w1, ax1, ay1, az1, 2, 18)

    def residue(i):
        centre, total = around(v1, ax1, ay1, az1, i)
        return s1[i] + total - d1[i] * centre

    restrict_whole(residue, rows, s2)
    first_sweep(v2, s2, w2, 1, 9)
    for k in range(5):
        a, b = (v2, u2) if k % 2 == 0 else (u2, v2)
        sweep(a, b, s2, w2, ax2, ay2, az2, 1, 9)
    spread = chosen_dot(
        jnp.concatenate([u2[1 + k] for k in range(8)], axis=0), lane_spread(128, 128)
    )
    rows[pl.ds(0, 128, stride=2), :] = spread
    rows[pl.ds(1, 128, stride=2), :] = spread
    for k in range(8):
        more = rows[32 * k : 32 * k + 32, :]
        v1[2 + 2 * k] = v1[2 + 2 * k] + more
        v1[3 + 2 * k] = v1[3 + 2 * k] + more
    sweep(v1, u1, s1, w1, ax1, ay1, az1, 2, 18)
    sweep(u1, v1, s1, w1, ax1, ay1, az1, 2, 18)
    sweep(v1, u1, s1, w1, ax1, ay1, az1, 2, 18)
    base = sc[0] * 4
    near = jnp.concatenate([u1[base + k] for k in range(8)], axis=0)
    wide = chosen_dot(near, lane_spread(128, 256))
    for lanes, ref in ((slice(0, 128), wide_a), (slice(128, 256), wide_b)):
        for k in range(8):
            ref[80 * k : 80 * k + 8, :] = jnp.zeros((8, 128), F32)
            ref[80 * k + 72 : 80 * k + 80, :] = jnp.zeros((8, 128), F32)
            part = wide[32 * k : 32 * k + 32, lanes]
            ref[pl.ds(80 * k + 8, 32, stride=2), :] = part
            ref[pl.ds(80 * k + 9, 32, stride=2), :] = part


def postsmooth(sc, s, v, coefs, wide_a, wide_b, va, vb):
    ax, ay, az, w = coefs
    row = pl.multiple_of(sc[1] * 8, 8)
    for i in range(3, 19):
        k = (i - 3) // 2
        more = jnp.concatenate(
            [wide_a[pl.ds(80 * k + row, 24), :], wide_b[pl.ds(80 * k + row, 24), :]], axis=1
        )
        va[i] = v[i] + more
    sweep(va, vb, s, w, ax, ay, az, 4, 18)
    sweep(vb, va, s, w, ax, ay, az, 5, 17)


POST_SCRATCH = (
    [pltpu.VMEM(L1, F32)] * 3
    + [pltpu.VMEM(L2, F32)] * 3
    + [pltpu.VMEM((256, 128), F32)]
    + [pltpu.VMEM((640, 128), F32)] * 2
    + [pltpu.VMEM(REGION, F32)] * 2
)


def post_own_body(
    sc, parts, ax1, ay1, az1, w1, d1, ax2, ay2, az2, w2, d2, s, v, ax, ay, az, w, out, *scratch
):
    *inner, wide_a, wide_b, va, vb = scratch
    correct(
        sc,
        parts,
        (ax1, ay1, az1, w1, d1),
        (ax2, ay2, az2, w2, d2),
        *inner,
        wide_a,
        wide_b,
    )
    postsmooth(sc, s, v, (ax, ay, az, w), wide_a, wide_b, va, vb)
    for i in range(8):
        centre, total = around(va, ax, ay, az, i + 7)
        new = 0.2 * centre + w[i + 7] * (s[i + 7] + total)
        out[i] = new[8:16, 0:128]


def post_near_body(
    sc, parts, ax1, ay1, az1, w1, d1, ax2, ay2, az2, w2, d2, s, v, ax, ay, az, w, p, out, *scratch
):
    *inner, wide_a, wide_b, va, vb = scratch
    correct(
        sc,
        parts,
        (ax1, ay1, az1, w1, d1),
        (ax2, ay2, az2, w2, d2),
        *inner,
        wide_a,
        wide_b,
    )
    postsmooth(sc, s, v, (ax, ay, az, w), wide_a, wide_b, va, vb)
    for i in range(10):
        centre, total = around(va, ax, ay, az, i + 6)
        out[i] = p[i + 6] + 0.2 * centre + w[i + 6] * (s[i + 6] + total)


def members(count, groups):
    r = lax.broadcasted_iota(jnp.int32, (count, groups), 0)
    c = lax.broadcasted_iota(jnp.int32, (count, groups), 1)
    return jnp.where(r // 8 == c, F32(1.0), F32(0.0)).astype(BF16)


def same_row(x):
    r = lax.broadcasted_iota(jnp.int32, x.shape, 0)
    c = lax.broadcasted_iota(jnp.int32, x.shape, 1)
    return jnp.where(r % 8 == c % 8, x, F32(0.0)).astype(BF16)


ACROSS = (((1,), (1,)), ((), ()))


def dot_across(a, b, precision=None):
    return lax.dot_general(a, b, ACROSS, precision=precision, preferred_element_type=F32)


def closure_body(
    sc,
    features,
    weight_in,
    bias_in,
    weight_out,
    velocity,
    target,
    flux,
    slope,
    hidden,
    face_x,
    face_y,
    face_z,
    kin,
    bias,
    kout,
):
    units = members(512, 64)
    narrow = dot_across(units, weight_in[...]).astype(BF16)
    kin[...] = same_row(dot_across(narrow, members(128, 16)))
    narrow = dot_across(members(24, 3), weight_out[...]).astype(BF16)
    kout[...] = same_row(dot_across(narrow, units))
    bias[...] = dot_across(
        units.astype(F32), jnp.broadcast_to(bias_in[...], (128, 64)), HIGHEST
    )
    _, high = opens_of(sc)
    high_x = jnp.where(sc[0] == 3, high[0], F32(1.0))
    high_y = jnp.where(sc[1] == 7, high[1], F32(1.0))
    high_z = jnp.where(sc[2] == 7, high[2], F32(1.0))
    row = lax.broadcasted_iota(jnp.int32, (8, 128), 0)
    col = lax.broadcasted_iota(jnp.int32, (8, 128), 1)
    factor_y = jnp.where(row == 7, high_y, F32(1.0))
    factor_z = jnp.where(col == 127, high_z, F32(1.0))

    def one(x):
        columns = features[:, x, :, :].astype(F32).reshape(128, 128).astype(BF16)
        before = jnp.dot(kin[...], columns, preferred_element_type=F32) + bias[...]
        gate = 1.0 / (1.0 + jnp.exp(-before))
        unit = (before * gate).astype(BF16)
        hidden[x] = unit
        slope[x] = gate * (1.0 + before * (1.0 - gate))
        shift = jnp.dot(kout[...], unit, preferred_element_type=F32)
        factor_x = jnp.where(x == 7, high_x, F32(1.0))
        flux[0, x] = (velocity[0, x] + shift[0:8]) * factor_x
        flux[1, x] = (velocity[1, x] + shift[8:16]) * factor_y
        flux[2, x] = (velocity[2, x] + shift[16:24]) * factor_z

    planes(0, 8, one, 1)
    face_x[0] = flux[0, 7]
    face_x[1] = target[0, 7]
    for x in range(8):
        face_y[0, x : x + 1, :] = flux[1, x, 7:8, :]
        face_y[1, x : x + 1, :] = target[1, x, 7:8, :]
    face_z[0] = flux[2]
    face_z[1] = target[2]


def shifted(field, low_x, low_y, low_z, x):
    row = lax.broadcasted_iota(jnp.int32, (8, 128), 0)
    col = lax.broadcasted_iota(jnp.int32, (8, 128), 1)
    before_x = low_x() if x == 0 else field(0, x - 1)
    before_y = jnp.where(row == 0, low_y(x), forth(field(1, x), 0))
    before_z = jnp.where(col == 0, low_z(x), forth(field(2, x), 1))
    return before_x, before_y, before_z


def source_body(sc, flux, low_x, low_y, low_z, out):
    inner = [jnp.where(sc[d] > 0, F32(1.0), F32(0.0)) for d in range(3)]
    for x in range(8):
        bx, by, bz = shifted(
            lambda d, i: flux[d, i],
            lambda: low_x[0] * inner[0],
            lambda i: jnp.broadcast_to(low_y[0, i : i + 1, :] * inner[1], (8, 128)),
            lambda i: forth(low_z[0, i] * inner[2], 1),
            x,
        )
        out[x] = -((flux[0, x] - bx) + (flux[1, x] - by) + (flux[2, x] - bz))


def middle_body(sc, near, flux, target, low_x, low_y, low_z, ax, ay, az, new, misfit, out):
    scale = F32(1.0 / CELLS)
    inner = [jnp.where(sc[d] > 0, F32(1.0), F32(0.0)) for d in range(3)]

    def rises(i):
        p = near[i]
        return p, back(p, 0) - p, back(p, 1) - p

    for x in range(8):
        p, rise_y, rise_z = rises(x + 1)
        rise_x = near[x + 2] - p
        parts = (ax[x + 7] * rise_x, ay[x + 7] * rise_y, az[x + 7] * rise_z)
        for d in range(3):
            value = flux[d, x] - parts[d][8:16, 0:128]
            new[d, x] = value
            misfit[d, x] = (value - target[d, x]) * scale

    def low_weighted_x():
        up = ax[6, 8:16, 0:128]
        rise = (near[1] - near[0])[8:16, 0:128]
        return up * ((low_x[0] - up * rise - low_x[1]) * (scale * inner[0]))

    def low_weighted_y(x):
        up = ay[x + 7, 7:8, 0:128]
        rise = near[x + 1, 8:9, 0:128] - near[x + 1, 7:8, 0:128]
        value = low_y[0, x : x + 1, :] - up * rise - low_y[1, x : x + 1, :]
        return jnp.broadcast_to(up * (value * (scale * inner[1])), (8, 128))

    def low_weighted_z(x):
        p = near[x + 1, 8:16, :]
        rise = (back(p, 1) - p)[:, 128:256]
        up = az[x + 7, 8:16, 128:256]
        value = up * ((low_z[0, x] - up * rise - low_z[1, x]) * (scale * inner[2]))
        return forth(value, 1)

    refs = (ax, ay, az)

    def weighted(d, x):
        return refs[d][x + 7, 8:16, 0:128] * misfit[d, x]

    for x in range(8):
        bx, by, bz = shifted(weighted, low_weighted_x, low_weighted_y, low_weighted_z, x)
        out[x] = (weighted(0, x) - bx) + (weighted(1, x) - by) + (weighted(2, x) - bz)


def gradient_body(
    sc, near, misfit, features, slope, hidden, weight_out, out, acc_in, acc_bias, acc_out, kback
):
    narrow = jnp.dot(members(512, 64), weight_out[...], preferred_element_type=F32).astype(BF16)
    kback[...] = same_row(dot_across(narrow, members(24, 3)))
    _, high = opens_of(sc)
    high_x = jnp.where(sc[0] == 3, high[0], F32(1.0))
    high_y = jnp.where(sc[1] == 7, high[1], F32(1.0))
    high_z = jnp.where(sc[2] == 7, high[2], F32(1.0))
    row = lax.broadcasted_iota(jnp.int32, (8, 128), 0)
    col = lax.broadcasted_iota(jnp.int32, (8, 128), 1)
    factor_y = jnp.where(row == 7, high_y, F32(1.0))
    factor_z = jnp.where(col == 127, high_z, F32(1.0))
    acc_in[...] = jnp.zeros((128, 512), F32)
    acc_bias[...] = jnp.zeros((512, 128), F32)
    acc_out[...] = jnp.zeros((24, 512), F32)
    across = ACROSS

    def one(x):
        p = near[x + 1]
        rise_x = (near[x + 2] - p)[8:16, 0:128]
        rise_y = (back(p, 0) - p)[8:16, 0:128]
        rise_z = (back(p, 1) - p)[8:16, 0:128]
        factor_x = jnp.where(x == 7, high_x, F32(1.0))
        grads = jnp.concatenate(
            [
                (misfit[0, x] + rise_x) * factor_x,
                (misfit[1, x] + rise_y) * factor_y,
                (misfit[2, x] + rise_z) * factor_z,
            ],
            axis=0,
        ).astype(BF16)
        columns = features[:, x, :, :].astype(F32).reshape(128, 128).astype(BF16)
        grad_before = jnp.dot(kback[...], grads, preferred_element_type=F32) * slope[x]
        acc_bias[...] += grad_before
        acc_in[...] += lax.dot_general(
            columns, grad_before.astype(BF16), across, preferred_element_type=F32
        )
        acc_out[...] += lax.dot_general(grads, hidden[x], across, preferred_element_type=F32)

    planes(0, 8, one, 1)

    def same(count):
        r = lax.broadcasted_iota(jnp.int32, (count, 512), 0)
        c = lax.broadcasted_iota(jnp.int32, (count, 512), 1)
        return r % 8 == c % 8

    def grouped(count, groups):
        r = lax.broadcasted_iota(jnp.int32, (groups, count), 0)
        c = lax.broadcasted_iota(jnp.int32, (groups, count), 1)
        return jnp.where(c // 8 == r, F32(1.0), F32(0.0))

    hr = lax.broadcasted_iota(jnp.int32, (512, 64), 0)
    hc = lax.broadcasted_iota(jnp.int32, (512, 64), 1)
    fold = jnp.where(hr // 8 == hc, F32(1.0), F32(0.0))
    in_part = exact_dot(grouped(128, 16), jnp.where(same(128), acc_in[...], F32(0.0)))
    out_part = exact_dot(grouped(24, 8), jnp.where(same(24), acc_out[...], F32(0.0)))
    bias_part = lax.dot_general(
        jnp.ones((8, 128), F32), acc_bias[...], across, precision=HIGHEST, preferred_element_type=F32
    )
    folded = exact_dot(jnp.concatenate([in_part, out_part, bias_part], axis=0), fold)
    out[0:8, 0:64] = folded[0:8]
    out[0:8, 64:128] = folded[8:16]
    out[8:16, 0:64] = folded[16:24]
    out[8:16, 64:128] = folded[24:32]


def neighbours(up, down, axis):
    count = lax.axis_size(axis)
    ups = [(i, (i + 1) % count) for i in range(count)]
    before = lax.ppermute(up, axis, ups)
    after = lax.ppermute(down, axis, [(b, a) for a, b in ups])
    place = lax.axis_index(axis)
    zero = F32(0.0)
    return jnp.where(place > 0, before, zero), jnp.where(place < count - 1, after, zero)


def from_before(face, axis):
    count = lax.axis_size(axis)
    return lax.ppermute(face, axis, [(i, (i + 1) % count) for i in range(count)])


def exchanged(own):
    before, after = neighbours(own, own, "gz")
    lane = lax.broadcasted_iota(jnp.int32, own.shape, 3)
    wide = jnp.concatenate([own, jnp.where(lane < 64, after, before)], axis=3)
    low, high = neighbours(wide[:, 1:8], wide[:, 0:7], "gx")
    wide = jnp.concatenate([low, wide, high], axis=1)
    low, high = neighbours(wide, wide, GY)
    return jnp.concatenate([low, wide, high], axis=2)


def over_plane(part):
    copies = jnp.broadcast_to(part, (32, *part.shape))
    return lax.all_to_all(copies, XY, split_axis=0, concat_axis=0, tiled=True)


def summed(part, axes):
    for axis in axes:
        copies = jnp.broadcast_to(part, (lax.axis_size(axis), *part.shape))
        part = jnp.sum(lax.all_to_all(copies, axis, split_axis=0, concat_axis=0, tiled=True), axis=0)
    return part


def per_device(velocity, features, density, target, weight_in, bias_in, weight_out, open_faces):
    place = jnp.stack([lax.axis_index("gx"), lax.axis_index(GY), lax.axis_index("gz")])
    sc = jnp.concatenate([place.astype(jnp.int32), open_faces])
    block = (8, 8, 128)
    flux, slope, hidden, face_x, face_y, face_z = call(
        closure_body,
        [
            shaped((3, *block)),
            shaped((8, 512, 128)),
            shaped((8, 512, 128), BF16),
            shaped((2, 8, 128)),
            shaped((2, 8, 128)),
            shaped((2, *block)),
        ],
        (sc, features, weight_in, bias_in[None], weight_out, velocity, target),
        [pltpu.VMEM((512, 128), BF16), pltpu.VMEM((512, 128), F32), pltpu.VMEM((24, 512), BF16)],
        smem=(0,),
    )
    low_x = from_before(face_x, "gx")
    low_y = from_before(face_y, GY)
    low_z = from_before(face_z, "gz")
    (source,) = call(
        source_body, [shaped(block)], (sc, flux, low_x, low_y, low_z), smem=(0,)
    )
    both = exchanged(jnp.stack([source, density]))
    region = shaped(REGION)
    one_region = [pltpu.VMEM(REGION, F32), pltpu.VMEM((32, 128), F32)]
    *coefs, v, part = call(
        start_body,
        [region] * 6 + [shaped((32, 128))],
        (sc, both[0], both[1]),
        one_region,
        smem=(0,),
    )
    ax, ay, az, w, d = coefs
    parts = over_plane(part)
    coarse = call(
        coarse_body,
        [shaped(L1)] * 5 + [shaped(L2)] * 5,
        (sc, parts),
        [pltpu.VMEM(L1, F32), pltpu.VMEM(L2, F32), pltpu.VMEM((256, 128), F32)],
        smem=(0,),
    )

    def finish_solve(b, v, parts):
        (own,) = call(
            post_own_body,
            [shaped(block)],
            (sc, parts, *coarse, b, v, ax, ay, az, w),
            POST_SCRATCH,
            smem=(0,),
        )
        p = exchanged(own[None])[0]
        s, v, part = call(
            again_body, [region, region, shaped((16, 128))], (b, p, *coefs), one_region
        )
        (near,) = call(
            post_near_body,
            [shaped((10, NYP, NZP))],
            (sc, over_plane(part), *coarse, s, v, ax, ay, az, w, p),
            POST_SCRATCH,
            smem=(0,),
        )
        return near

    near = finish_solve(both[0], v, parts)
    new_velocity, misfit, grad_pressure = call(
        middle_body,
        [shaped((3, *block)), shaped((3, *block)), shaped(block)],
        (sc, near, flux, target, low_x, low_y, low_z, ax, ay, az),
        smem=(0,),
    )
    b = exchanged(grad_pressure[None])[0]
    v, part = call(pre_body, [region, shaped((16, 128))], (b, *coefs), one_region)
    near = finish_solve(b, v, over_plane(part))
    (packed,) = call(
        gradient_body,
        [shaped((16, 128))],
        (sc, near, misfit, features, slope, hidden, weight_out),
        [
            pltpu.VMEM((128, 512), F32),
            pltpu.VMEM((512, 128), F32),
            pltpu.VMEM((24, 512), F32),
            pltpu.VMEM((512, 24), BF16),
        ],
        smem=(0,),
    )
    total = summed(packed, (XY, "gz"))
    grad_in = jnp.concatenate([total[0:8, 0:64], total[0:8, 64:128]], axis=0)
    return new_velocity, grad_in, total[8, 64:128], total[8:11, 0:64].T


def solution(mesh):
    split = Mesh(
        mesh.devices.reshape(mesh.shape["gx"], 4, 2, mesh.shape["gz"]), ("gx", "gy_0", "gy_1", "gz")
    )
    placed = (
        P(None, "gx", GY, "gz"),
        P(None, "gx", GY, "gz"),
        P("gx", GY, "gz"),
        P(None, "gx", GY, "gz"),
        P(),
        P(),
        P(),
        P(),
    )
    return jax.shard_map(
        per_device,
        mesh=split,
        in_specs=placed,
        out_specs=(P(None, "gx", GY, "gz"), P(), P(), P()),
        check_vma=False,
    )
```

```python
import jax
import jax.numpy as jnp
from jax import lax
from jax.experimental import pallas as pl
from jax.experimental.pallas import tpu as pltpu
from jax.sharding import Mesh
from jax.sharding import PartitionSpec as P

GY = ("gy_0", "gy_1")
GRANT = 12
XY = ("gx", "gy_0", "gy_1")
ALL = ("gx", "gy_0", "gy_1", "gz")
F32 = jnp.float32
BF16 = jnp.bfloat16
HIGHEST = lax.Precision.HIGHEST
MASS_SHIFT = 0.05
CELLS = 2097152.0

NXP, NYP, NZP = 22, 24, 256
REGION = (NXP, NYP, NZP)
L1 = (20, 32, 128)
L2 = (10, 16, 128)
UNROLL = {24: 2, 32: 8, 16: 8}


def shaped(shape, dtype=F32):
    return jax.ShapeDtypeStruct(shape, dtype)


def call(body, outs, args, scratch=(), smem=(), left=(), grant=12):
    spaces = [
        pltpu.SMEM if i in smem else pltpu.HBM if i in left else pltpu.VMEM for i in range(len(args))
    ]
    specs = [pl.BlockSpec(memory_space=space) for space in spaces]
    return pl.pallas_call(
        body,
        out_shape=outs,
        in_specs=specs,
        out_specs=[pl.BlockSpec(memory_space=pltpu.VMEM)] * len(outs),
        scratch_shapes=list(scratch),
        compiler_params=pltpu.CompilerParams(vmem_limit_bytes=grant << 20),
    )(*args)


def back(x, axis):
    return pltpu.roll(x, x.shape[axis] - 1, axis)


def forth(x, axis):
    return pltpu.roll(x, 1, axis)


def exact_dot(a, b):
    return jnp.dot(a, b, precision=HIGHEST, preferred_element_type=F32)


def chosen_dot(a, b):
    high = a.astype(BF16)
    rest = a - high.astype(F32)
    middle = rest.astype(BF16)
    low = (rest - middle.astype(F32)).astype(BF16)
    count = a.shape[0]
    parts = jnp.dot(
        jnp.concatenate([high, middle, low], axis=0), b.astype(BF16), preferred_element_type=F32
    )
    return (parts[2 * count :] + parts[count : 2 * count]) + parts[:count]


def planes(lo, hi, body, unroll=2):
    def step(i, carry):
        body(i)
        return carry

    lax.fori_loop(lo, hi, step, 0, unroll=unroll)


def around(src, ax, ay, az, i):
    v = src[i]
    y, z = ay[i], az[i]
    total = ax[i] * src[i + 1] + ax[i - 1] * src[i - 1]
    total = total + (y * back(v, 0) + forth(y * v, 0))
    return v, total + (z * back(v, 1) + forth(z * v, 1))


def sweep(src, dst, s, w, ax, ay, az, lo, hi):
    def one(i):
        v, total = around(src, ax, ay, az, i)
        dst[i] = 0.2 * v + w[i] * (s[i] + total)

    planes(lo, hi, one, UNROLL[src.shape[1]])


def first_sweep(dst, s, w, lo, hi):
    def one(i):
        dst[i] = w[i] * s[i]

    planes(lo, hi, one, UNROLL[s.shape[1]])


def face(here, there, weight, low, high):
    has, next_has = here > 0.0, there > 0.0
    factor = jnp.where(
        has, jnp.where(next_has, F32(1.0), high), jnp.where(next_has, low, F32(0.0))
    )
    total = jnp.where(has | next_has, here + there, F32(1.0))
    return weight * 2.0 / total * factor


def coefficients(rho, opens, weight, refs, lo, hi, whole_y):
    ax, ay, az, w, d = refs
    low, high = opens
    count = rho.shape[1]

    def one_face(i):
        ax[i] = face(rho[i], rho[i + 1], weight, low[0], high[0])

    planes(lo - 1, hi, one_face, 2)

    def one(i):
        r = rho[i]
        after = back(r, 0)
        row = lax.broadcasted_iota(jnp.int32, r.shape, 0)
        if whole_y:
            after = jnp.where(row == count - 1, F32(0.0), after)
        up_y = face(r, after, weight, low[1], high[1])
        if whole_y:
            first = jnp.where(r > 0.0, weight * 2.0 / jnp.where(r > 0.0, r, F32(1.0)), F32(0.0))
            down_y = jnp.where(row == 0, first * low[1], forth(up_y, 0))
        else:
            down_y = forth(up_y, 0)
        up_z = face(r, back(r, 1), weight, low[2], high[2])
        diagonal = MASS_SHIFT + ax[i] + ax[i - 1] + up_y + down_y + up_z + forth(up_z, 1)
        ay[i] = jnp.where(row == count - 1, F32(0.0), up_y) if whole_y else up_y
        az[i] = up_z
        d[i] = diagonal
        w[i] = jnp.where(r > 0.0, 0.8 / diagonal, F32(0.0))

    planes(lo, hi, one, 2)


def lane_pairs(cells, kept, repeat):
    row = lax.broadcasted_iota(jnp.int32, (cells, kept), 0)
    col = lax.broadcasted_iota(jnp.int32, (cells, kept), 1)
    return jnp.where(row // 2 == col % repeat, F32(1.0), F32(0.0))


def lane_spread(cells, kept):
    row = lax.broadcasted_iota(jnp.int32, (cells, kept), 0)
    col = lax.broadcasted_iota(jnp.int32, (cells, kept), 1)
    return jnp.where(col // 2 == row, F32(1.0), F32(0.0))


def block_means(read, rows, out, out_row):
    pairs = [read(7 + 2 * k) + read(8 + 2 * k) for k in range(4)]
    rows[...] = chosen_dot(jnp.concatenate(pairs, axis=0), lane_pairs(256, 128, 128))
    total = 0.125 * (rows[pl.ds(0, 16, stride=2), :] + rows[pl.ds(1, 16, stride=2), :])
    for k in range(32):
        out[k, out_row : out_row + 16, :] = total


def presmooth(s, v, va, coefs, rows, out):
    ax, ay, az, w, d = coefs
    first_sweep(v, s, w, 1, 21)
    sweep(v, va, s, w, ax, ay, az, 2, 20)
    sweep(va, v, s, w, ax, ay, az, 3, 19)

    def residue(i):
        centre, total = around(v, ax, ay, az, i)
        return (s[i] + total - d[i] * centre)[8:16]

    block_means(residue, rows, out, 0)


def opens_of(sc):
    values = [sc[3 + k].astype(F32) for k in range(6)]
    return values[0::2], values[1::2]


def start_body(
    sc, own, low, high, b, ax, ay, az, w, d, v, out, low_faces, rho, va, rows
):
    along_y(sc, own, low, high, b, rho, low_faces)
    coefs = (ax, ay, az, w, d)
    for ref in (ax, ay, az, w, d, v):
        ref[0] = jnp.zeros((NYP, NZP), F32)
        ref[21] = jnp.zeros((NYP, NZP), F32)
    coefficients(rho, opens_of(sc), 1.0, coefs, 1, 21, False)
    presmooth(b, v, va, coefs, rows, out)
    block_means(lambda i: rho[i, 8:16, :], rows, out, 16)


def pre_body(b, ax, ay, az, w, d, v, out, va, rows):
    v[0] = jnp.zeros((NYP, NZP), F32)
    v[21] = jnp.zeros((NYP, NZP), F32)
    presmooth(b, v, va, (ax, ay, az, w, d), rows, out)


def again_body(b, p, ax, ay, az, w, d, s, v, out, va, rows):
    for ref in (s, v):
        ref[0] = jnp.zeros((NYP, NZP), F32)
        ref[21] = jnp.zeros((NYP, NZP), F32)

    def one(i):
        centre, total = around(p, ax, ay, az, i)
        s[i] = b[i] + total - d[i] * centre

    planes(1, 21, one)
    presmooth(s, v, va, (ax, ay, az, w, d), rows, out)


def whole_plane(parts, first, dst):
    for k in range(2):
        dst[k] = jnp.zeros((32, 128), F32)
        dst[18 + k] = jnp.zeros((32, 128), F32)
    for device in range(32):
        x, y = divmod(device, 8)
        for k in range(4):
            dst[2 + 4 * x + k, 4 * y : 4 * y + 4, :] = parts[
                device, first + 4 * k : first + 4 * k + 4, :
            ]


def restrict_whole(read, rows, dst):
    for k in range(8):
        rows[32 * k : 32 * k + 32, :] = read(2 + 2 * k) + read(3 + 2 * k)
    rows[...] = chosen_dot(rows[...], lane_pairs(128, 128, 64))
    for k in range(8):
        total = (
            rows[pl.ds(32 * k, 16, stride=2), :] + rows[pl.ds(32 * k + 1, 16, stride=2), :]
        )
        dst[1 + k] = 0.125 * total


def coarse_body(
    sc, parts, ax1, ay1, az1, w1, d1, ax2, ay2, az2, w2, d2, rho1, rho2, rows
):
    for ref in (ax1, ay1, az1, w1, d1):
        ref[...] = jnp.zeros(L1, F32)
    for ref in (ax2, ay2, az2, w2, d2, rho2):
        ref[...] = jnp.zeros(L2, F32)
    opens = opens_of(sc)
    whole_plane(parts, 16, rho1)
    coefficients(rho1, opens, 0.25, (ax1, ay1, az1, w1, d1), 2, 18, True)
    restrict_whole(lambda i: rho1[i], rows, rho2)
    coefficients(rho2, opens, 0.0625, (ax2, ay2, az2, w2, d2), 1, 9, True)


def correct(
    sc, parts, coefs1, coefs2, s1, v1, u1, s2, v2, u2, rows, wide_a, wide_b
):
    ax1, ay1, az1, w1, d1 = coefs1
    ax2, ay2, az2, w2, d2 = coefs2
    whole_plane(parts, 0, s1)
    for ref in (v1, u1):
        for k in (0, 1, 18, 19):
            ref[k] = jnp.zeros((32, 128), F32)
    for ref in (v2, u2):
        for k in (0, 9):
            ref[k] = jnp.zeros((16, 128), F32)
    first_sweep(v1, s1, w1, 2, 18)
    sweep(v1, u1, s1, w1, ax1, ay1, az1, 2, 18)
    sweep(u1, v1, s1, w1, ax1, ay1, az1, 2, 18)

    def residue(i):
        centre, total = around(v1, ax1, ay1, az1, i)
        return s1[i] + total - d1[i] * centre

    restrict_whole(residue, rows, s2)
    first_sweep(v2, s2, w2, 1, 9)
    for k in range(5):
        a, b = (v2, u2) if k % 2 == 0 else (u2, v2)
        sweep(a, b, s2, w2, ax2, ay2, az2, 1, 9)
    spread = chosen_dot(
        jnp.concatenate([u2[1 + k] for k in range(8)], axis=0), lane_spread(128, 128)
    )
    rows[pl.ds(0, 128, stride=2), :] = spread
    rows[pl.ds(1, 128, stride=2), :] = spread
    for k in range(8):
        more = rows[32 * k : 32 * k + 32, :]
        v1[2 + 2 * k] = v1[2 + 2 * k] + more
        v1[3 + 2 * k] = v1[3 + 2 * k] + more
    sweep(v1, u1, s1, w1, ax1, ay1, az1, 2, 18)
    sweep(u1, v1, s1, w1, ax1, ay1, az1, 2, 18)
    sweep(v1, u1, s1, w1, ax1, ay1, az1, 2, 18)
    base = sc[0] * 4
    near = jnp.concatenate([u1[base + k] for k in range(8)], axis=0)
    wide = chosen_dot(near, lane_spread(128, 256))
    for lanes, ref in ((slice(0, 128), wide_a), (slice(128, 256), wide_b)):
        for k in range(8):
            ref[80 * k : 80 * k + 8, :] = jnp.zeros((8, 128), F32)
            ref[80 * k + 72 : 80 * k + 80, :] = jnp.zeros((8, 128), F32)
            part = wide[32 * k : 32 * k + 32, lanes]
            ref[pl.ds(80 * k + 8, 32, stride=2), :] = part
            ref[pl.ds(80 * k + 9, 32, stride=2), :] = part


def postsmooth(sc, s, v, coefs, wide_a, wide_b, va, vb):
    ax, ay, az, w = coefs
    row = pl.multiple_of(sc[1] * 8, 8)
    for i in range(3, 19):
        k = (i - 3) // 2
        more = jnp.concatenate(
            [wide_a[pl.ds(80 * k + row, 24), :], wide_b[pl.ds(80 * k + row, 24), :]], axis=1
        )
        va[i] = v[i] + more
    sweep(va, vb, s, w, ax, ay, az, 4, 18)
    sweep(vb, va, s, w, ax, ay, az, 5, 17)


POST_SCRATCH = (
    [pltpu.VMEM(L1, F32)] * 3
    + [pltpu.VMEM(L2, F32)] * 3
    + [pltpu.VMEM((256, 128), F32)]
    + [pltpu.VMEM((640, 128), F32)] * 2
    + [pltpu.VMEM(REGION, F32)] * 2
)


def post_own_body(
    sc, parts, ax1, ay1, az1, w1, d1, ax2, ay2, az2, w2, d2, s, v, ax, ay, az, w, out, *scratch
):
    *inner, wide_a, wide_b, va, vb = scratch
    correct(
        sc,
        parts,
        (ax1, ay1, az1, w1, d1),
        (ax2, ay2, az2, w2, d2),
        *inner,
        wide_a,
        wide_b,
    )
    postsmooth(sc, s, v, (ax, ay, az, w), wide_a, wide_b, va, vb)
    for i in range(8):
        centre, total = around(va, ax, ay, az, i + 7)
        new = 0.2 * centre + w[i + 7] * (s[i + 7] + total)
        out[i] = new[8:16, 0:128]


def post_near_body(
    sc, parts, ax1, ay1, az1, w1, d1, ax2, ay2, az2, w2, d2, s, v, ax, ay, az, w, p, out, *scratch
):
    *inner, wide_a, wide_b, va, vb = scratch
    correct(
        sc,
        parts,
        (ax1, ay1, az1, w1, d1),
        (ax2, ay2, az2, w2, d2),
        *inner,
        wide_a,
        wide_b,
    )
    postsmooth(sc, s, v, (ax, ay, az, w), wide_a, wide_b, va, vb)
    for i in range(10):
        centre, total = around(va, ax, ay, az, i + 6)
        out[i] = p[i + 6] + 0.2 * centre + w[i + 6] * (s[i + 6] + total)


def members(count, groups):
    r = lax.broadcasted_iota(jnp.int32, (count, groups), 0)
    c = lax.broadcasted_iota(jnp.int32, (count, groups), 1)
    return jnp.where(r // 8 == c, F32(1.0), F32(0.0)).astype(BF16)


def same_row(x):
    r = lax.broadcasted_iota(jnp.int32, x.shape, 0)
    c = lax.broadcasted_iota(jnp.int32, x.shape, 1)
    return jnp.where(r % 8 == c % 8, x, F32(0.0)).astype(BF16)


ACROSS = (((1,), (1,)), ((), ()))


def dot_across(a, b, precision=None):
    return lax.dot_general(a, b, ACROSS, precision=precision, preferred_element_type=F32)


def closure_body(
    sc,
    features_far,
    velocity_far,
    target_far,
    density_far,
    weight_in,
    bias_in,
    weight_out,
    flux,
    slope,
    hidden,
    message,
    target_faces,
    marks,
    features,
    velocity,
    target,
    kin,
    bias,
    kout,
    sems,
):
    copies = [
        pltpu.make_async_copy(source, place, sems.at[k])
        for k, (source, place) in enumerate(
            (
                (features_far, features),
                (velocity_far, velocity),
                (target_far, target),
                (density_far, message.at[8:16]),
            )
        )
    ]
    for copy in copies:
        copy.start()
    units = members(512, 64)
    narrow = dot_across(units, weight_in[...]).astype(BF16)
    kin[...] = same_row(dot_across(narrow, members(128, 16)))
    narrow = jnp.dot(members(24, 3), weight_out[...], preferred_element_type=F32).astype(BF16)
    kout[...] = same_row(dot_across(narrow, units))
    bias[...] = dot_across(
        units.astype(F32), jnp.broadcast_to(bias_in[...], (128, 64)), HIGHEST
    )
    _, high = opens_of(sc)
    high_x = jnp.where(sc[0] == 3, high[0], F32(1.0))
    high_y = jnp.where(sc[1] == 7, high[1], F32(1.0))
    high_z = jnp.where(sc[2] == 7, high[2], F32(1.0))
    row = lax.broadcasted_iota(jnp.int32, (8, 128), 0)
    col = lax.broadcasted_iota(jnp.int32, (8, 128), 1)
    factor_y = jnp.where(row == 7, high_y, F32(1.0))
    factor_z = jnp.where(col == 127, high_z, F32(1.0))
    for copy in copies:
        copy.wait()

    def one(x):
        columns = features[:, x, :, :].astype(F32).reshape(128, 128).astype(BF16)
        before = jnp.dot(kin[...], columns, preferred_element_type=F32) + bias[...]
        gate = 1.0 / (1.0 + jnp.exp(-before))
        unit = (before * gate).astype(BF16)
        hidden[x] = unit
        slope[x] = gate * (1.0 + before * (1.0 - gate))
        shift = jnp.dot(kout[...], unit, preferred_element_type=F32)
        factor_x = jnp.where(x == 7, high_x, F32(1.0))
        flux[0, x] = (velocity[0, x] + shift[0:8]) * factor_x
        flux[1, x] = (velocity[1, x] + shift[8:16]) * factor_y
        flux[2, x] = (velocity[2, x] + shift[16:24]) * factor_z

    planes(0, 8, one, 1)
    zero = jnp.zeros((8, 128), F32)
    ends = zero
    for x in range(8):
        bx, by, bz = shifted(
            lambda d, i: flux[d, i], lambda: zero, lambda i: zero, lambda i: zero, x
        )
        message[x] = -((flux[0, x] - bx) + (flux[1, x] - by) + (flux[2, x] - bz))
        message[17, x : x + 1, :] = flux[1, x, 7:8, :]
        target_faces[1, x : x + 1, :] = target[1, x, 7:8, :]
        ends = jnp.where(col == x, pltpu.roll(flux[2, x], x + 1, 1), ends)
        ends = jnp.where(col == x + 8, pltpu.roll(target[2, x], x + 9, 1), ends)
    message[16] = flux[0, 7]
    message[18] = ends
    target_faces[0] = target[0, 7]
    inside = inside_of(sc)
    wide_col = lax.broadcasted_iota(jnp.int32, (1, 256), 1)
    one_row = jnp.ones((1, 256), F32)
    marks[0:1, :] = jnp.where(wide_col < 64, inside[2][1], F32(0.0))
    marks[1:2, :] = jnp.where(wide_col < 64, F32(0.0), inside[2][0])
    for d in range(2):
        marks[2 + 2 * d : 3 + 2 * d, :] = one_row * inside[d][0]
        marks[3 + 2 * d : 4 + 2 * d, :] = one_row * inside[d][1]
    marks[6:8, :] = jnp.zeros((2, 256), F32)


def shifted(field, low_x, low_y, low_z, x):
    row = lax.broadcasted_iota(jnp.int32, (8, 128), 0)
    col = lax.broadcasted_iota(jnp.int32, (8, 128), 1)
    before_x = low_x() if x == 0 else field(0, x - 1)
    before_y = jnp.where(row == 0, low_y(x), forth(field(1, x), 0))
    before_z = jnp.where(col == 0, low_z(x), forth(field(2, x), 1))
    return before_x, before_y, before_z


def inside_of(sc):
    last = (3, 7, 7)
    return [
        (
            jnp.where(sc[d] > 0, F32(1.0), F32(0.0)),
            jnp.where(sc[d] < last[d], F32(1.0), F32(0.0)),
        )
        for d in range(3)
    ]


def along_z_body(sc, own, before, after, target_faces, wide, up, down):
    has_before, has_after = inside_of(sc)[2]
    col = lax.broadcasted_iota(jnp.int32, (8, 128), 1)

    def around_z(k):
        return jnp.where(col < 64, after[k] * has_after, before[k] * has_before)

    for k in range(18):
        here, there = own[k], around_z(k)
        if k < 8:
            turn = (128 - k) % 128
            low = pltpu.roll(before[18], turn, 1) if turn else before[18]
            high = pltpu.roll(own[18], turn, 1) if turn else own[18]
            here = jnp.where(col == 0, here + low * has_before, here)
            there = jnp.where(col == 0, there + high * has_after, there)
        wide[k, :, 0:128] = here
        wide[k, :, 128:256] = there
    for k in range(7):
        up[k] = wide[k + 1]
        up[k + 7] = wide[k + 9]
        down[k] = wide[k]
        down[k + 7] = wide[k + 8]
    up[14] = wide[17]
    down[14] = wide[17]
    up[15] = wide[16]
    up[16, :, 0:128] = target_faces[0]
    up[16, :, 128:256] = jnp.zeros((8, 128), F32)


def along_x_body(sc, wide, low, high, target_faces, out):
    has_before, has_after = inside_of(sc)[0]
    for k in range(7):
        out[k] = low[k] * has_before
        out[k + 22] = low[k + 7] * has_before
        more = wide[16] if k == 0 else jnp.zeros((8, 256), F32)
        out[k + 15] = (high[k] + more) * has_after
        out[k + 37] = high[k + 7] * has_after
    for k in range(8):
        out[k + 7] = wide[k] + low[15] * has_before if k == 0 else wide[k]
        out[k + 29] = wide[k + 8]
    out[44] = low[14] * has_before
    out[45] = wide[17]
    out[46] = high[14] * has_after
    out[47, :, 0:128] = target_faces[1]
    out[47, :, 128:256] = jnp.zeros((8, 128), F32)


def along_y(sc, own, low, high, b, rho, low_faces):
    has_before, has_after = inside_of(sc)[1]
    row = lax.broadcasted_iota(jnp.int32, (8, 256), 0)
    for i in range(22):
        k, r = divmod(i + 1, 8)
        more = jnp.broadcast_to(low[44 + k, r : r + 1, :] * has_before, (8, 256))
        next_more = jnp.broadcast_to(own[44 + k, r : r + 1, :], (8, 256))
        b[i, 0:8, :] = low[i] * has_before
        b[i, 8:16, :] = jnp.where(row == 0, own[i] + more, own[i])
        b[i, 16:24, :] = jnp.where(row == 0, high[i] + next_more, high[i]) * has_after
        rho[i, 0:8, :] = low[i + 22] * has_before
        rho[i, 8:16, :] = own[i + 22]
        rho[i, 16:24, :] = high[i + 22] * has_after
    low_faces[0] = low[45, :, 0:128]
    low_faces[1] = low[47, :, 0:128]


def middle_body(sc, near, flux, target, from_x, low_y, from_z, ax, ay, az, new, misfit, out):
    scale = F32(1.0 / CELLS)
    inner = [jnp.where(sc[d] > 0, F32(1.0), F32(0.0)) for d in range(3)]

    def rises(i):
        p = near[i]
        return p, back(p, 0) - p, back(p, 1) - p

    for x in range(8):
        p, rise_y, rise_z = rises(x + 1)
        rise_x = near[x + 2] - p
        parts = (ax[x + 7] * rise_x, ay[x + 7] * rise_y, az[x + 7] * rise_z)
        for d in range(3):
            value = flux[d, x] - parts[d][8:16, 0:128]
            new[d, x] = value
            misfit[d, x] = (value - target[d, x]) * scale

    def low_weighted_x():
        up = ax[6, 8:16, 0:128]
        rise = (near[1] - near[0])[8:16, 0:128]
        value = from_x[15, :, 0:128] - up * rise - from_x[16, :, 0:128]
        return up * (value * (scale * inner[0]))

    def low_weighted_y(x):
        up = ay[x + 7, 7:8, 0:128]
        rise = near[x + 1, 8:9, 0:128] - near[x + 1, 7:8, 0:128]
        value = low_y[0, x : x + 1, :] - up * rise - low_y[1, x : x + 1, :]
        return jnp.broadcast_to(up * (value * (scale * inner[1])), (8, 128))

    def low_weighted_z(x):
        p = near[x + 1, 8:16, :]
        rise = (back(p, 1) - p)[:, 128:256]
        up = az[x + 7, 8:16, 128:256]
        low_flux = pltpu.roll(from_z[18], 127 - x, 1)
        low_target = pltpu.roll(from_z[18], 119 - x, 1)
        value = up * ((low_flux - up * rise - low_target) * (scale * inner[2]))
        return forth(value, 1)

    refs = (ax, ay, az)

    def weighted(d, x):
        return refs[d][x + 7, 8:16, 0:128] * misfit[d, x]

    for x in range(8):
        bx, by, bz = shifted(weighted, low_weighted_x, low_weighted_y, low_weighted_z, x)
        out[x] = (weighted(0, x) - bx) + (weighted(1, x) - by) + (weighted(2, x) - bz)


def gradient_body(
    sc, near, misfit, features, slope, hidden, weight_out, out, acc_in, acc_bias, acc_out, kback
):
    narrow = dot_across(members(512, 64), weight_out[...]).astype(BF16)
    kback[...] = same_row(dot_across(narrow, members(24, 3)))
    _, high = opens_of(sc)
    high_x = jnp.where(sc[0] == 3, high[0], F32(1.0))
    high_y = jnp.where(sc[1] == 7, high[1], F32(1.0))
    high_z = jnp.where(sc[2] == 7, high[2], F32(1.0))
    row = lax.broadcasted_iota(jnp.int32, (8, 128), 0)
    col = lax.broadcasted_iota(jnp.int32, (8, 128), 1)
    factor_y = jnp.where(row == 7, high_y, F32(1.0))
    factor_z = jnp.where(col == 127, high_z, F32(1.0))
    acc_in[...] = jnp.zeros((128, 512), F32)
    acc_bias[...] = jnp.zeros((512, 128), F32)
    acc_out[...] = jnp.zeros((24, 512), F32)
    across = ACROSS

    def one(x):
        p = near[x + 1]
        rise_x = (near[x + 2] - p)[8:16, 0:128]
        rise_y = (back(p, 0) - p)[8:16, 0:128]
        rise_z = (back(p, 1) - p)[8:16, 0:128]
        factor_x = jnp.where(x == 7, high_x, F32(1.0))
        grads = jnp.concatenate(
            [
                (misfit[0, x] + rise_x) * factor_x,
                (misfit[1, x] + rise_y) * factor_y,
                (misfit[2, x] + rise_z) * factor_z,
            ],
            axis=0,
        ).astype(BF16)
        columns = features[:, x, :, :].astype(F32).reshape(128, 128).astype(BF16)
        grad_before = jnp.dot(kback[...], grads, preferred_element_type=F32) * slope[x]
        acc_bias[...] += grad_before
        acc_in[...] += lax.dot_general(
            columns, grad_before.astype(BF16), across, preferred_element_type=F32
        )
        acc_out[...] += lax.dot_general(grads, hidden[x], across, preferred_element_type=F32)

    planes(0, 8, one, 1)

    def same(count):
        r = lax.broadcasted_iota(jnp.int32, (count, 512), 0)
        c = lax.broadcasted_iota(jnp.int32, (count, 512), 1)
        return r % 8 == c % 8

    def grouped(count, groups):
        r = lax.broadcasted_iota(jnp.int32, (groups, count), 0)
        c = lax.broadcasted_iota(jnp.int32, (groups, count), 1)
        return jnp.where(c // 8 == r, F32(1.0), F32(0.0))

    hr = lax.broadcasted_iota(jnp.int32, (512, 64), 0)
    hc = lax.broadcasted_iota(jnp.int32, (512, 64), 1)
    fold = jnp.where(hr // 8 == hc, F32(1.0), F32(0.0))
    in_part = exact_dot(grouped(128, 16), jnp.where(same(128), acc_in[...], F32(0.0)))
    out_part = exact_dot(grouped(24, 8), jnp.where(same(24), acc_out[...], F32(0.0)))
    bias_part = lax.dot_general(
        jnp.ones((8, 128), F32), acc_bias[...], across, precision=HIGHEST, preferred_element_type=F32
    )
    folded = exact_dot(jnp.concatenate([in_part, out_part, bias_part], axis=0), fold)
    packed = jnp.concatenate(
        [
            jnp.concatenate([folded[0:8], folded[8:16]], axis=1),
            jnp.concatenate([folded[16:24], folded[24:32]], axis=1),
        ],
        axis=0,
    )
    for k in range(32):
        out[k] = packed


def plane_sum_body(parts, out):
    total = parts[0]
    for k in range(1, 32):
        total = total + parts[k]
    for k in range(8):
        out[k] = total


def ring(up, down, axis):
    count = lax.axis_size(axis)
    ups = [(i, (i + 1) % count) for i in range(count)]
    return lax.ppermute(up, axis, ups), lax.ppermute(down, axis, [(b, a) for a, b in ups])


def exchanged(own, marks):
    before, after = ring(own, own, "gz")
    wide = jnp.concatenate([own, after * marks[0, :128] + before * marks[1, :128]], axis=2)
    low, high = ring(wide[1:8], wide[0:7], "gx")
    wide = jnp.concatenate([low * marks[2], wide, high * marks[3]], axis=0)
    low, high = ring(wide, wide, GY)
    return jnp.concatenate([low * marks[4], wide, high * marks[5]], axis=1)


def unpack_body(parts, grad_in, grad_bias, grad_out):
    total = parts[0]
    for k in range(1, 8):
        total = total + parts[k]
    grad_in[0:8, :] = total[0:8, 0:64]
    grad_in[8:16, :] = total[0:8, 64:128]
    grad_bias[...] = total[8:9, 64:128]
    grad_out[...] = total[8:11, 0:64]


def sent_to_all(copies, axis):
    return lax.all_to_all(copies, axis, split_axis=0, concat_axis=0, tiled=True)


def per_device(velocity, features, density, target, weight_in, bias_in, weight_out, open_faces):
    place = jnp.stack([lax.axis_index("gx"), lax.axis_index(GY), lax.axis_index("gz")])
    sc = jnp.concatenate([place.astype(jnp.int32), open_faces])
    block = (8, 8, 128)
    narrow_out = weight_out.T
    flux, slope, hidden, message, target_faces, marks = call(
        closure_body,
        [
            shaped((3, *block)),
            shaped((8, 512, 128)),
            shaped((8, 512, 128), BF16),
            shaped((19, 8, 128)),
            shaped((2, 8, 128)),
            shaped((8, 256)),
        ],
        (sc, features, velocity, target, density, weight_in, bias_in[None], narrow_out),
        [
            pltpu.VMEM((16, *block), BF16),
            pltpu.VMEM((3, *block), F32),
            pltpu.VMEM((3, *block), F32),
            pltpu.VMEM((512, 128), BF16),
            pltpu.VMEM((512, 128), F32),
            pltpu.VMEM((24, 512), BF16),
            pltpu.SemaphoreType.DMA((4,)),
        ],
        smem=(0,),
        left=(1, 2, 3, 4),
        grant=GRANT,
    )
    from_z, after = ring(message, message, "gz")
    wide, up, down = call(
        along_z_body,
        [shaped((18, 8, 256)), shaped((17, 8, 256)), shaped((15, 8, 256))],
        (sc, message, from_z, after, target_faces),
        smem=(0,),
    )
    from_x, after = ring(up, down, "gx")
    (message,) = call(
        along_x_body, [shaped((48, 8, 256))], (sc, wide, from_x, after, target_faces), smem=(0,)
    )
    before, after = ring(message, message, GY)
    region, to_plane = shaped(REGION), shaped((32, 16, 128))
    one_region = [pltpu.VMEM(REGION, F32), pltpu.VMEM((32, 128), F32)]
    source, *coefs, v, part, low_y = call(
        start_body,
        [region] * 7 + [shaped((32, 32, 128)), shaped((2, 8, 128))],
        (sc, message, before, after),
        [pltpu.VMEM(REGION, F32), *one_region],
        smem=(0,),
    )
    ax, ay, az, w, d = coefs
    parts = sent_to_all(part, XY)
    coarse = call(
        coarse_body,
        [shaped(L1)] * 5 + [shaped(L2)] * 5,
        (sc, parts),
        [pltpu.VMEM(L1, F32), pltpu.VMEM(L2, F32), pltpu.VMEM((256, 128), F32)],
        smem=(0,),
    )

    def finish_solve(b, v, parts):
        (own,) = call(
            post_own_body,
            [shaped(block)],
            (sc, parts, *coarse, b, v, ax, ay, az, w),
            POST_SCRATCH,
            smem=(0,),
        )
        p = exchanged(own, marks)
        s, v, part = call(
            again_body, [region, region, to_plane], (b, p, *coefs), one_region
        )
        (near,) = call(
            post_near_body,
            [shaped((10, NYP, NZP))],
            (sc, sent_to_all(part, XY), *coarse, s, v, ax, ay, az, w, p),
            POST_SCRATCH,
            smem=(0,),
        )
        return near

    near = finish_solve(source, v, parts)
    new_velocity, misfit, grad_pressure = call(
        middle_body,
        [shaped((3, *block)), shaped((3, *block)), shaped(block)],
        (sc, near, flux, target, from_x, low_y, from_z, ax, ay, az),
        smem=(0,),
    )
    b = exchanged(grad_pressure, marks)
    v, part = call(pre_body, [region, to_plane], (b, *coefs), one_region)
    near = finish_solve(b, v, sent_to_all(part, XY))
    (packed,) = call(
        gradient_body,
        [to_plane],
        (sc, near, misfit, features, slope, hidden, narrow_out),
        [
            pltpu.VMEM((128, 512), F32),
            pltpu.VMEM((512, 128), F32),
            pltpu.VMEM((24, 512), F32),
            pltpu.VMEM((512, 24), BF16),
        ],
        smem=(0,),
    )
    (plane,) = call(plane_sum_body, [shaped((8, 16, 128))], (sent_to_all(packed, XY),))
    grad_in, grad_bias, grad_out = call(
        unpack_body,
        [shaped((16, 64)), shaped((1, 64)), shaped((3, 64))],
        (sent_to_all(plane, "gz"),),
    )
    return new_velocity, grad_in, grad_bias[0], grad_out.T


def solution(mesh):
    split = Mesh(
        mesh.devices.reshape(mesh.shape["gx"], 4, 2, mesh.shape["gz"]), ("gx", "gy_0", "gy_1", "gz")
    )
    placed = (
        P(None, "gx", GY, "gz"),
        P(None, "gx", GY, "gz"),
        P("gx", GY, "gz"),
        P(None, "gx", GY, "gz"),
        P(),
        P(),
        P(),
        P(),
    )
    return jax.shard_map(
        per_device,
        mesh=split,
        in_specs=placed,
        out_specs=(P(None, "gx", GY, "gz"), P(), P(), P()),
        check_vma=False,
    )
```

```python
import jax
import jax.numpy as jnp
from jax import lax
from jax.experimental import pallas as pl
from jax.experimental.pallas import tpu as pltpu
from jax.sharding import Mesh
from jax.sharding import PartitionSpec as P

GY = ("gy_0", "gy_1")
CLOSURE = 4
XY = ("gx", "gy_0", "gy_1")
ALL = ("gx", "gy_0", "gy_1", "gz")
F32 = jnp.float32
BF16 = jnp.bfloat16
HIGHEST = lax.Precision.HIGHEST
MASS_SHIFT = 0.05
CELLS = 2097152.0

NXP, NYP, NZP = 22, 24, 256
REGION = (NXP, NYP, NZP)
L1 = (20, 32, 128)
L2 = (10, 16, 128)
MOST = {24: 7, 32: 8, 16: 8}


def shaped(shape, dtype=F32):
    return jax.ShapeDtypeStruct(shape, dtype)


def call(body, outs, args, scratch=(), smem=()):
    spaces = [
        pltpu.SMEM if i in smem else pltpu.VMEM for i in range(len(args))
    ]
    specs = [pl.BlockSpec(memory_space=space) for space in spaces]
    return pl.pallas_call(
        body,
        out_shape=outs,
        in_specs=specs,
        out_specs=[pl.BlockSpec(memory_space=pltpu.VMEM)] * len(outs),
        scratch_shapes=list(scratch),
        compiler_params=pltpu.CompilerParams(vmem_limit_bytes=12 << 20),
    )(*args)


def back(x, axis):
    return pltpu.roll(x, x.shape[axis] - 1, axis)


def forth(x, axis):
    return pltpu.roll(x, 1, axis)


def exact_dot(a, b):
    return jnp.dot(a, b, precision=HIGHEST, preferred_element_type=F32)


def chosen_dot(a, b):
    high = a.astype(BF16)
    rest = a - high.astype(F32)
    middle = rest.astype(BF16)
    low = (rest - middle.astype(F32)).astype(BF16)
    count = a.shape[0]
    parts = jnp.dot(
        jnp.concatenate([high, middle, low], axis=0), b.astype(BF16), preferred_element_type=F32
    )
    return (parts[2 * count :] + parts[count : 2 * count]) + parts[:count]


def steps(count, rows):
    return max(k for k in range(1, MOST[rows] + 1) if count % k == 0)


def planes(lo, hi, body, unroll=2):
    def step(i, carry):
        body(i)
        return carry

    lax.fori_loop(lo, hi, step, 0, unroll=unroll)


def around(src, ax, ay, az, i):
    v = src[i]
    y, z = ay[i], az[i]
    total = ax[i] * src[i + 1] + ax[i - 1] * src[i - 1]
    total = total + (y * back(v, 0) + forth(y * v, 0))
    return v, total + (z * back(v, 1) + forth(z * v, 1))


def sweep(src, dst, s, w, ax, ay, az, lo, hi):
    def one(i):
        v, total = around(src, ax, ay, az, i)
        dst[i] = 0.2 * v + w[i] * (s[i] + total)

    planes(lo, hi, one, steps(hi - lo, src.shape[1]))


def first_sweep(dst, s, w, lo, hi):
    def one(i):
        dst[i] = w[i] * s[i]

    planes(lo, hi, one, steps(hi - lo, s.shape[1]))


def face(here, there, weight, low, high):
    has, next_has = here > 0.0, there > 0.0
    factor = jnp.where(
        has, jnp.where(next_has, F32(1.0), high), jnp.where(next_has, low, F32(0.0))
    )
    total = jnp.where(has | next_has, here + there, F32(1.0))
    return weight * 2.0 / total * factor


def coefficients(rho, opens, weight, refs, lo, hi, whole_y):
    ax, ay, az, w, d = refs
    low, high = opens
    count = rho.shape[1]

    def one_face(i):
        ax[i] = face(rho[i], rho[i + 1], weight, low[0], high[0])

    planes(lo - 1, hi, one_face, 2)

    def one(i):
        r = rho[i]
        after = back(r, 0)
        row = lax.broadcasted_iota(jnp.int32, r.shape, 0)
        if whole_y:
            after = jnp.where(row == count - 1, F32(0.0), after)
        up_y = face(r, after, weight, low[1], high[1])
        if whole_y:
            first = jnp.where(r > 0.0, weight * 2.0 / jnp.where(r > 0.0, r, F32(1.0)), F32(0.0))
            down_y = jnp.where(row == 0, first * low[1], forth(up_y, 0))
        else:
            down_y = forth(up_y, 0)
        up_z = face(r, back(r, 1), weight, low[2], high[2])
        diagonal = MASS_SHIFT + ax[i] + ax[i - 1] + up_y + down_y + up_z + forth(up_z, 1)
        ay[i] = jnp.where(row == count - 1, F32(0.0), up_y) if whole_y else up_y
        az[i] = up_z
        d[i] = diagonal
        w[i] = jnp.where(r > 0.0, 0.8 / diagonal, F32(0.0))

    planes(lo, hi, one, 2)


def lane_pairs(cells, kept, repeat):
    row = lax.broadcasted_iota(jnp.int32, (cells, kept), 0)
    col = lax.broadcasted_iota(jnp.int32, (cells, kept), 1)
    return jnp.where(row // 2 == col % repeat, F32(1.0), F32(0.0))


def lane_spread(cells, kept):
    row = lax.broadcasted_iota(jnp.int32, (cells, kept), 0)
    col = lax.broadcasted_iota(jnp.int32, (cells, kept), 1)
    return jnp.where(col // 2 == row, F32(1.0), F32(0.0))


def block_means(read, rows, out, out_row):
    pairs = [read(7 + 2 * k) + read(8 + 2 * k) for k in range(4)]
    rows[...] = chosen_dot(jnp.concatenate(pairs, axis=0), lane_pairs(256, 128, 128))
    total = 0.125 * (rows[pl.ds(0, 16, stride=2), :] + rows[pl.ds(1, 16, stride=2), :])
    for k in range(32):
        out[k, out_row : out_row + 16, :] = total


def presmooth(s, v, va, coefs, rows, out):
    ax, ay, az, w, d = coefs
    first_sweep(v, s, w, 1, 21)
    sweep(v, va, s, w, ax, ay, az, 2, 20)
    sweep(va, v, s, w, ax, ay, az, 3, 19)

    def residue(i):
        centre, total = around(v, ax, ay, az, i)
        return (s[i] + total - d[i] * centre)[8:16]

    block_means(residue, rows, out, 0)


def opens_of(sc):
    values = [sc[3 + k].astype(F32) for k in range(6)]
    return values[0::2], values[1::2]


def start_body(
    sc, own, low, high, b, ax, ay, az, w, d, v, out, low_faces, rho, va, rows
):
    along_y(sc, own, low, high, b, rho, low_faces)
    coefs = (ax, ay, az, w, d)
    for ref in (ax, ay, az, w, d, v):
        ref[0] = jnp.zeros((NYP, NZP), F32)
        ref[21] = jnp.zeros((NYP, NZP), F32)
    coefficients(rho, opens_of(sc), 1.0, coefs, 1, 21, False)
    presmooth(b, v, va, coefs, rows, out)
    block_means(lambda i: rho[i, 8:16, :], rows, out, 16)


def pre_body(b, ax, ay, az, w, d, v, out, va, rows):
    v[0] = jnp.zeros((NYP, NZP), F32)
    v[21] = jnp.zeros((NYP, NZP), F32)
    presmooth(b, v, va, (ax, ay, az, w, d), rows, out)


def again_body(b, p, ax, ay, az, w, d, s, v, out, va, rows):
    for ref in (s, v):
        ref[0] = jnp.zeros((NYP, NZP), F32)
        ref[21] = jnp.zeros((NYP, NZP), F32)

    def one(i):
        centre, total = around(p, ax, ay, az, i)
        s[i] = b[i] + total - d[i] * centre

    planes(1, 21, one, 5)
    presmooth(s, v, va, (ax, ay, az, w, d), rows, out)


def whole_plane(parts, first, dst):
    for k in range(2):
        dst[k] = jnp.zeros((32, 128), F32)
        dst[18 + k] = jnp.zeros((32, 128), F32)
    for device in range(32):
        x, y = divmod(device, 8)
        for k in range(4):
            dst[2 + 4 * x + k, 4 * y : 4 * y + 4, :] = parts[
                device, first + 4 * k : first + 4 * k + 4, :
            ]


def restrict_whole(read, rows, dst):
    for k in range(8):
        rows[32 * k : 32 * k + 32, :] = read(2 + 2 * k) + read(3 + 2 * k)
    rows[...] = chosen_dot(rows[...], lane_pairs(128, 128, 64))
    for k in range(8):
        total = (
            rows[pl.ds(32 * k, 16, stride=2), :] + rows[pl.ds(32 * k + 1, 16, stride=2), :]
        )
        dst[1 + k] = 0.125 * total


def coarse_body(
    sc, parts, ax1, ay1, az1, w1, d1, ax2, ay2, az2, w2, d2, rho1, rho2, rows
):
    for ref in (ax1, ay1, az1, w1, d1):
        ref[...] = jnp.zeros(L1, F32)
    for ref in (ax2, ay2, az2, w2, d2, rho2):
        ref[...] = jnp.zeros(L2, F32)
    opens = opens_of(sc)
    whole_plane(parts, 16, rho1)
    coefficients(rho1, opens, 0.25, (ax1, ay1, az1, w1, d1), 2, 18, True)
    restrict_whole(lambda i: rho1[i], rows, rho2)
    coefficients(rho2, opens, 0.0625, (ax2, ay2, az2, w2, d2), 1, 9, True)


def correct(
    sc, parts, coefs1, coefs2, s1, v1, u1, s2, v2, u2, rows, wide_a, wide_b
):
    ax1, ay1, az1, w1, d1 = coefs1
    ax2, ay2, az2, w2, d2 = coefs2
    whole_plane(parts, 0, s1)
    for ref in (v1, u1):
        for k in (0, 1, 18, 19):
            ref[k] = jnp.zeros((32, 128), F32)
    for ref in (v2, u2):
        for k in (0, 9):
            ref[k] = jnp.zeros((16, 128), F32)
    first_sweep(v1, s1, w1, 2, 18)
    sweep(v1, u1, s1, w1, ax1, ay1, az1, 2, 18)
    sweep(u1, v1, s1, w1, ax1, ay1, az1, 2, 18)

    def residue(i):
        centre, total = around(v1, ax1, ay1, az1, i)
        return s1[i] + total - d1[i] * centre

    restrict_whole(residue, rows, s2)
    first_sweep(v2, s2, w2, 1, 9)
    for k in range(5):
        a, b = (v2, u2) if k % 2 == 0 else (u2, v2)
        sweep(a, b, s2, w2, ax2, ay2, az2, 1, 9)
    spread = chosen_dot(
        jnp.concatenate([u2[1 + k] for k in range(8)], axis=0), lane_spread(128, 128)
    )
    rows[pl.ds(0, 128, stride=2), :] = spread
    rows[pl.ds(1, 128, stride=2), :] = spread
    for k in range(8):
        more = rows[32 * k : 32 * k + 32, :]
        v1[2 + 2 * k] = v1[2 + 2 * k] + more
        v1[3 + 2 * k] = v1[3 + 2 * k] + more
    sweep(v1, u1, s1, w1, ax1, ay1, az1, 2, 18)
    sweep(u1, v1, s1, w1, ax1, ay1, az1, 2, 18)
    sweep(v1, u1, s1, w1, ax1, ay1, az1, 2, 18)
    base = sc[0] * 4
    near = jnp.concatenate([u1[base + k] for k in range(8)], axis=0)
    wide = chosen_dot(near, lane_spread(128, 256))
    for lanes, ref in ((slice(0, 128), wide_a), (slice(128, 256), wide_b)):
        for k in range(8):
            ref[80 * k : 80 * k + 8, :] = jnp.zeros((8, 128), F32)
            ref[80 * k + 72 : 80 * k + 80, :] = jnp.zeros((8, 128), F32)
            part = wide[32 * k : 32 * k + 32, lanes]
            ref[pl.ds(80 * k + 8, 32, stride=2), :] = part
            ref[pl.ds(80 * k + 9, 32, stride=2), :] = part


def postsmooth(sc, s, v, coefs, wide_a, wide_b, va, vb):
    ax, ay, az, w = coefs
    row = pl.multiple_of(sc[1] * 8, 8)
    for i in range(3, 19):
        k = (i - 3) // 2
        more = jnp.concatenate(
            [wide_a[pl.ds(80 * k + row, 24), :], wide_b[pl.ds(80 * k + row, 24), :]], axis=1
        )
        va[i] = v[i] + more
    sweep(va, vb, s, w, ax, ay, az, 4, 18)
    sweep(vb, va, s, w, ax, ay, az, 5, 17)


POST_SCRATCH = (
    [pltpu.VMEM(L1, F32)] * 3
    + [pltpu.VMEM(L2, F32)] * 3
    + [pltpu.VMEM((256, 128), F32)]
    + [pltpu.VMEM((640, 128), F32)] * 2
    + [pltpu.VMEM(REGION, F32)] * 2
)


def post_own_body(
    sc, parts, ax1, ay1, az1, w1, d1, ax2, ay2, az2, w2, d2, s, v, ax, ay, az, w, out, *scratch
):
    *inner, wide_a, wide_b, va, vb = scratch
    correct(
        sc,
        parts,
        (ax1, ay1, az1, w1, d1),
        (ax2, ay2, az2, w2, d2),
        *inner,
        wide_a,
        wide_b,
    )
    postsmooth(sc, s, v, (ax, ay, az, w), wide_a, wide_b, va, vb)
    for i in range(8):
        centre, total = around(va, ax, ay, az, i + 7)
        new = 0.2 * centre + w[i + 7] * (s[i + 7] + total)
        out[i] = new[8:16, 0:128]


def post_near_body(
    sc, parts, ax1, ay1, az1, w1, d1, ax2, ay2, az2, w2, d2, s, v, ax, ay, az, w, p, out, *scratch
):
    *inner, wide_a, wide_b, va, vb = scratch
    correct(
        sc,
        parts,
        (ax1, ay1, az1, w1, d1),
        (ax2, ay2, az2, w2, d2),
        *inner,
        wide_a,
        wide_b,
    )
    postsmooth(sc, s, v, (ax, ay, az, w), wide_a, wide_b, va, vb)
    for i in range(10):
        centre, total = around(va, ax, ay, az, i + 6)
        out[i] = p[i + 6] + 0.2 * centre + w[i + 6] * (s[i + 6] + total)


def members(count, groups):
    r = lax.broadcasted_iota(jnp.int32, (count, groups), 0)
    c = lax.broadcasted_iota(jnp.int32, (count, groups), 1)
    return jnp.where(r // 8 == c, F32(1.0), F32(0.0)).astype(BF16)


def same_row(x):
    r = lax.broadcasted_iota(jnp.int32, x.shape, 0)
    c = lax.broadcasted_iota(jnp.int32, x.shape, 1)
    return jnp.where(r % 8 == c % 8, x, F32(0.0)).astype(BF16)


ACROSS = (((1,), (1,)), ((), ()))


def dot_across(a, b, precision=None):
    return lax.dot_general(a, b, ACROSS, precision=precision, preferred_element_type=F32)


def closure_body(
    sc,
    features,
    fields,
    weights,
    flux,
    slope,
    hidden,
    message,
    target_faces,
    marks,
    kin,
    bias,
    kout,
):
    velocity, target = fields.at[0:3], fields.at[3:6]
    message[8:16] = fields[6]
    weight_in = weights[0:16, :].astype(BF16)
    weight_out = weights[24:27, :].astype(BF16)
    units = members(512, 64)
    narrow = dot_across(units, weight_in).astype(BF16)
    kin[...] = same_row(dot_across(narrow, members(128, 16)))
    narrow = jnp.dot(members(24, 3), weight_out, preferred_element_type=F32).astype(BF16)
    kout[...] = same_row(dot_across(narrow, units))
    bias[...] = dot_across(
        units.astype(F32), jnp.broadcast_to(weights[16:17, :], (128, 64)), HIGHEST
    )
    _, high = opens_of(sc)
    high_x = jnp.where(sc[0] == 3, high[0], F32(1.0))
    high_y = jnp.where(sc[1] == 7, high[1], F32(1.0))
    high_z = jnp.where(sc[2] == 7, high[2], F32(1.0))
    row = lax.broadcasted_iota(jnp.int32, (8, 128), 0)
    col = lax.broadcasted_iota(jnp.int32, (8, 128), 1)
    factor_y = jnp.where(row == 7, high_y, F32(1.0))
    factor_z = jnp.where(col == 127, high_z, F32(1.0))
    def one(x):
        columns = features[:, x, :, :].astype(F32).reshape(128, 128).astype(BF16)
        before = jnp.dot(kin[...], columns, preferred_element_type=F32) + bias[...]
        gate = 1.0 / (1.0 + jnp.exp(-before))
        unit = (before * gate).astype(BF16)
        hidden[x] = unit
        slope[x] = gate * (1.0 + before * (1.0 - gate))
        shift = jnp.dot(kout[...], unit, preferred_element_type=F32)
        factor_x = jnp.where(x == 7, high_x, F32(1.0))
        flux[0, x] = (velocity[0, x] + shift[0:8]) * factor_x
        flux[1, x] = (velocity[1, x] + shift[8:16]) * factor_y
        flux[2, x] = (velocity[2, x] + shift[16:24]) * factor_z

    planes(0, 8, one, CLOSURE)
    zero = jnp.zeros((8, 128), F32)
    ends = zero
    for x in range(8):
        bx, by, bz = shifted(
            lambda d, i: flux[d, i], lambda: zero, lambda i: zero, lambda i: zero, x
        )
        message[x] = -((flux[0, x] - bx) + (flux[1, x] - by) + (flux[2, x] - bz))
        message[17, x : x + 1, :] = flux[1, x, 7:8, :]
        target_faces[1, x : x + 1, :] = target[1, x, 7:8, :]
        ends = jnp.where(col == x, pltpu.roll(flux[2, x], x + 1, 1), ends)
        ends = jnp.where(col == x + 8, pltpu.roll(target[2, x], x + 9, 1), ends)
    message[16] = flux[0, 7]
    message[18] = ends
    target_faces[0] = target[0, 7]
    inside = inside_of(sc)
    wide_col = lax.broadcasted_iota(jnp.int32, (1, 256), 1)
    one_row = jnp.ones((1, 256), F32)
    marks[0:1, :] = jnp.where(wide_col < 64, inside[2][1], F32(0.0))
    marks[1:2, :] = jnp.where(wide_col < 64, F32(0.0), inside[2][0])
    for d in range(2):
        marks[2 + 2 * d : 3 + 2 * d, :] = one_row * inside[d][0]
        marks[3 + 2 * d : 4 + 2 * d, :] = one_row * inside[d][1]
    marks[6:8, :] = jnp.zeros((2, 256), F32)


def shifted(field, low_x, low_y, low_z, x):
    row = lax.broadcasted_iota(jnp.int32, (8, 128), 0)
    col = lax.broadcasted_iota(jnp.int32, (8, 128), 1)
    before_x = low_x() if x == 0 else field(0, x - 1)
    before_y = jnp.where(row == 0, low_y(x), forth(field(1, x), 0))
    before_z = jnp.where(col == 0, low_z(x), forth(field(2, x), 1))
    return before_x, before_y, before_z


def inside_of(sc):
    last = (3, 7, 7)
    return [
        (
            jnp.where(sc[d] > 0, F32(1.0), F32(0.0)),
            jnp.where(sc[d] < last[d], F32(1.0), F32(0.0)),
        )
        for d in range(3)
    ]


def along_z_body(sc, own, before, after, target_faces, wide, up, down):
    has_before, has_after = inside_of(sc)[2]
    col = lax.broadcasted_iota(jnp.int32, (8, 128), 1)

    def around_z(k):
        return jnp.where(col < 64, after[k] * has_after, before[k] * has_before)

    for k in range(18):
        here, there = own[k], around_z(k)
        if k < 8:
            turn = (128 - k) % 128
            low = pltpu.roll(before[18], turn, 1) if turn else before[18]
            high = pltpu.roll(own[18], turn, 1) if turn else own[18]
            here = jnp.where(col == 0, here + low * has_before, here)
            there = jnp.where(col == 0, there + high * has_after, there)
        wide[k, :, 0:128] = here
        wide[k, :, 128:256] = there
    for k in range(7):
        up[k] = wide[k + 1]
        up[k + 7] = wide[k + 9]
        down[k] = wide[k]
        down[k + 7] = wide[k + 8]
    up[14] = wide[17]
    down[14] = wide[17]
    up[15] = wide[16]
    up[16, :, 0:128] = target_faces[0]
    up[16, :, 128:256] = jnp.zeros((8, 128), F32)


def along_x_body(sc, wide, low, high, target_faces, out):
    has_before, has_after = inside_of(sc)[0]
    for k in range(7):
        out[k] = low[k] * has_before
        out[k + 22] = low[k + 7] * has_before
        more = wide[16] if k == 0 else jnp.zeros((8, 256), F32)
        out[k + 15] = (high[k] + more) * has_after
        out[k + 37] = high[k + 7] * has_after
    for k in range(8):
        out[k + 7] = wide[k] + low[15] * has_before if k == 0 else wide[k]
        out[k + 29] = wide[k + 8]
    out[44] = low[14] * has_before
    out[45] = wide[17]
    out[46] = high[14] * has_after
    out[47, :, 0:128] = target_faces[1]
    out[47, :, 128:256] = jnp.zeros((8, 128), F32)


def along_y(sc, own, low, high, b, rho, low_faces):
    has_before, has_after = inside_of(sc)[1]
    row = lax.broadcasted_iota(jnp.int32, (8, 256), 0)
    for i in range(22):
        k, r = divmod(i + 1, 8)
        more = jnp.broadcast_to(low[44 + k, r : r + 1, :] * has_before, (8, 256))
        next_more = jnp.broadcast_to(own[44 + k, r : r + 1, :], (8, 256))
        b[i, 0:8, :] = low[i] * has_before
        b[i, 8:16, :] = jnp.where(row == 0, own[i] + more, own[i])
        b[i, 16:24, :] = jnp.where(row == 0, high[i] + next_more, high[i]) * has_after
        rho[i, 0:8, :] = low[i + 22] * has_before
        rho[i, 8:16, :] = own[i + 22]
        rho[i, 16:24, :] = high[i + 22] * has_after
    low_faces[0] = low[45, :, 0:128]
    low_faces[1] = low[47, :, 0:128]


def middle_body(sc, near, flux, fields, from_x, low_y, from_z, ax, ay, az, new, misfit, out):
    scale = F32(1.0 / CELLS)
    target = fields.at[3:6]
    inner = [jnp.where(sc[d] > 0, F32(1.0), F32(0.0)) for d in range(3)]

    def rises(i):
        p = near[i]
        return p, back(p, 0) - p, back(p, 1) - p

    for x in range(8):
        p, rise_y, rise_z = rises(x + 1)
        rise_x = near[x + 2] - p
        parts = (ax[x + 7] * rise_x, ay[x + 7] * rise_y, az[x + 7] * rise_z)
        for d in range(3):
            value = flux[d, x] - parts[d][8:16, 0:128]
            new[d, x] = value
            misfit[d, x] = (value - target[d, x]) * scale

    def low_weighted_x():
        up = ax[6, 8:16, 0:128]
        rise = (near[1] - near[0])[8:16, 0:128]
        value = from_x[15, :, 0:128] - up * rise - from_x[16, :, 0:128]
        return up * (value * (scale * inner[0]))

    def low_weighted_y(x):
        up = ay[x + 7, 7:8, 0:128]
        rise = near[x + 1, 8:9, 0:128] - near[x + 1, 7:8, 0:128]
        value = low_y[0, x : x + 1, :] - up * rise - low_y[1, x : x + 1, :]
        return jnp.broadcast_to(up * (value * (scale * inner[1])), (8, 128))

    def low_weighted_z(x):
        p = near[x + 1, 8:16, :]
        rise = (back(p, 1) - p)[:, 128:256]
        up = az[x + 7, 8:16, 128:256]
        low_flux = pltpu.roll(from_z[18], 127 - x, 1)
        low_target = pltpu.roll(from_z[18], 119 - x, 1)
        value = up * ((low_flux - up * rise - low_target) * (scale * inner[2]))
        return forth(value, 1)

    refs = (ax, ay, az)

    def weighted(d, x):
        return refs[d][x + 7, 8:16, 0:128] * misfit[d, x]

    for x in range(8):
        bx, by, bz = shifted(weighted, low_weighted_x, low_weighted_y, low_weighted_z, x)
        out[x] = (weighted(0, x) - bx) + (weighted(1, x) - by) + (weighted(2, x) - bz)


def gradient_body(
    sc, near, misfit, features, slope, hidden, weights, out, acc_in, acc_bias, acc_out, kback
):
    narrow = dot_across(members(512, 64), weights[24:27, :].astype(BF16)).astype(BF16)
    kback[...] = same_row(dot_across(narrow, members(24, 3)))
    _, high = opens_of(sc)
    high_x = jnp.where(sc[0] == 3, high[0], F32(1.0))
    high_y = jnp.where(sc[1] == 7, high[1], F32(1.0))
    high_z = jnp.where(sc[2] == 7, high[2], F32(1.0))
    row = lax.broadcasted_iota(jnp.int32, (8, 128), 0)
    col = lax.broadcasted_iota(jnp.int32, (8, 128), 1)
    factor_y = jnp.where(row == 7, high_y, F32(1.0))
    factor_z = jnp.where(col == 127, high_z, F32(1.0))
    acc_in[...] = jnp.zeros((128, 512), F32)
    acc_bias[...] = jnp.zeros((512, 128), F32)
    acc_out[...] = jnp.zeros((24, 512), F32)
    across = ACROSS

    def one(x):
        p = near[x + 1]
        rise_x = (near[x + 2] - p)[8:16, 0:128]
        rise_y = (back(p, 0) - p)[8:16, 0:128]
        rise_z = (back(p, 1) - p)[8:16, 0:128]
        factor_x = jnp.where(x == 7, high_x, F32(1.0))
        grads = jnp.concatenate(
            [
                (misfit[0, x] + rise_x) * factor_x,
                (misfit[1, x] + rise_y) * factor_y,
                (misfit[2, x] + rise_z) * factor_z,
            ],
            axis=0,
        ).astype(BF16)
        columns = features[:, x, :, :].astype(F32).reshape(128, 128).astype(BF16)
        grad_before = jnp.dot(kback[...], grads, preferred_element_type=F32) * slope[x]
        acc_bias[...] += grad_before
        acc_in[...] += lax.dot_general(
            columns, grad_before.astype(BF16), across, preferred_element_type=F32
        )
        acc_out[...] += lax.dot_general(grads, hidden[x], across, preferred_element_type=F32)

    planes(0, 8, one, CLOSURE)

    def same(count):
        r = lax.broadcasted_iota(jnp.int32, (count, 512), 0)
        c = lax.broadcasted_iota(jnp.int32, (count, 512), 1)
        return r % 8 == c % 8

    def grouped(count, groups):
        r = lax.broadcasted_iota(jnp.int32, (groups, count), 0)
        c = lax.broadcasted_iota(jnp.int32, (groups, count), 1)
        return jnp.where(c // 8 == r, F32(1.0), F32(0.0))

    hr = lax.broadcasted_iota(jnp.int32, (512, 64), 0)
    hc = lax.broadcasted_iota(jnp.int32, (512, 64), 1)
    fold = jnp.where(hr // 8 == hc, F32(1.0), F32(0.0))
    in_part = exact_dot(grouped(128, 16), jnp.where(same(128), acc_in[...], F32(0.0)))
    out_part = exact_dot(grouped(24, 8), jnp.where(same(24), acc_out[...], F32(0.0)))
    bias_part = lax.dot_general(
        jnp.ones((8, 128), F32), acc_bias[...], across, precision=HIGHEST, preferred_element_type=F32
    )
    folded = exact_dot(jnp.concatenate([in_part, out_part, bias_part], axis=0), fold)
    packed = jnp.concatenate(
        [
            jnp.concatenate([folded[0:8], folded[8:16]], axis=1),
            jnp.concatenate([folded[16:24], folded[24:32]], axis=1),
        ],
        axis=0,
    )
    for k in range(32):
        out[k] = packed


def plane_sum_body(parts, out):
    total = parts[0]
    for k in range(1, 32):
        total = total + parts[k]
    for k in range(8):
        out[k] = total


def ring(up, down, axis):
    count = lax.axis_size(axis)
    ups = [(i, (i + 1) % count) for i in range(count)]
    return lax.ppermute(up, axis, ups), lax.ppermute(down, axis, [(b, a) for a, b in ups])


def exchanged(own, marks):
    before, after = ring(own, own, "gz")
    wide = jnp.concatenate([own, after * marks[0, :128] + before * marks[1, :128]], axis=2)
    low, high = ring(wide[1:8], wide[0:7], "gx")
    wide = jnp.concatenate([low * marks[2], wide, high * marks[3]], axis=0)
    low, high = ring(wide, wide, GY)
    return jnp.concatenate([low * marks[4], wide, high * marks[5]], axis=1)


def unpack_body(parts, grad_in, grad_bias, grad_out):
    total = parts[0]
    for k in range(1, 8):
        total = total + parts[k]
    grad_in[0:8, :] = total[0:8, 0:64]
    grad_in[8:16, :] = total[0:8, 64:128]
    grad_bias[...] = total[8:9, 64:128]
    grad_out[...] = total[8:11, 0:64]


def sent_to_all(copies, axis):
    return lax.all_to_all(copies, axis, split_axis=0, concat_axis=0, tiled=True)


def per_device(velocity, features, density, target, weight_in, bias_in, weight_out, open_faces):
    place = jnp.stack([lax.axis_index("gx"), lax.axis_index(GY), lax.axis_index("gz")])
    sc = jnp.concatenate([place.astype(jnp.int32), open_faces])
    block = (8, 8, 128)
    weights = jnp.concatenate(
        [
            weight_in.astype(F32),
            jnp.broadcast_to(bias_in[None], (8, 64)),
            jnp.pad(weight_out.T.astype(F32), ((0, 5), (0, 0))),
        ],
        axis=0,
    )
    fields = jnp.concatenate([velocity, target, density[None]], axis=0)
    flux, slope, hidden, message, target_faces, marks = call(
        closure_body,
        [
            shaped((3, *block)),
            shaped((8, 512, 128)),
            shaped((8, 512, 128), BF16),
            shaped((19, 8, 128)),
            shaped((2, 8, 128)),
            shaped((8, 256)),
        ],
        (sc, features, fields, weights),
        [
            pltpu.VMEM((512, 128), BF16),
            pltpu.VMEM((512, 128), F32),
            pltpu.VMEM((24, 512), BF16),
        ],
        smem=(0,),
    )
    from_z, after = ring(message, message, "gz")
    wide, up, down = call(
        along_z_body,
        [shaped((18, 8, 256)), shaped((17, 8, 256)), shaped((15, 8, 256))],
        (sc, message, from_z, after, target_faces),
        smem=(0,),
    )
    from_x, after = ring(up, down, "gx")
    (message,) = call(
        along_x_body, [shaped((48, 8, 256))], (sc, wide, from_x, after, target_faces), smem=(0,)
    )
    before, after = ring(message, message, GY)
    region, to_plane = shaped(REGION), shaped((32, 16, 128))
    one_region = [pltpu.VMEM(REGION, F32), pltpu.VMEM((32, 128), F32)]
    source, *coefs, v, part, low_y = call(
        start_body,
        [region] * 7 + [shaped((32, 32, 128)), shaped((2, 8, 128))],
        (sc, message, before, after),
        [pltpu.VMEM(REGION, F32), *one_region],
        smem=(0,),
    )
    ax, ay, az, w, d = coefs
    parts = sent_to_all(part, XY)
    coarse = call(
        coarse_body,
        [shaped(L1)] * 5 + [shaped(L2)] * 5,
        (sc, parts),
        [pltpu.VMEM(L1, F32), pltpu.VMEM(L2, F32), pltpu.VMEM((256, 128), F32)],
        smem=(0,),
    )

    def finish_solve(b, v, parts):
        (own,) = call(
            post_own_body,
            [shaped(block)],
            (sc, parts, *coarse, b, v, ax, ay, az, w),
            POST_SCRATCH,
            smem=(0,),
        )
        p = exchanged(own, marks)
        s, v, part = call(
            again_body, [region, region, to_plane], (b, p, *coefs), one_region
        )
        (near,) = call(
            post_near_body,
            [shaped((10, NYP, NZP))],
            (sc, sent_to_all(part, XY), *coarse, s, v, ax, ay, az, w, p),
            POST_SCRATCH,
            smem=(0,),
        )
        return near

    near = finish_solve(source, v, parts)
    new_velocity, misfit, grad_pressure = call(
        middle_body,
        [shaped((3, *block)), shaped((3, *block)), shaped(block)],
        (sc, near, flux, fields, from_x, low_y, from_z, ax, ay, az),
        smem=(0,),
    )
    b = exchanged(grad_pressure, marks)
    v, part = call(pre_body, [region, to_plane], (b, *coefs), one_region)
    near = finish_solve(b, v, sent_to_all(part, XY))
    (packed,) = call(
        gradient_body,
        [to_plane],
        (sc, near, misfit, features, slope, hidden, weights),
        [
            pltpu.VMEM((128, 512), F32),
            pltpu.VMEM((512, 128), F32),
            pltpu.VMEM((24, 512), F32),
            pltpu.VMEM((512, 24), BF16),
        ],
        smem=(0,),
    )
    (plane,) = call(plane_sum_body, [shaped((8, 16, 128))], (sent_to_all(packed, XY),))
    grad_in, grad_bias, grad_out = call(
        unpack_body,
        [shaped((16, 64)), shaped((1, 64)), shaped((3, 64))],
        (sent_to_all(plane, "gz"),),
    )
    return new_velocity, grad_in, grad_bias[0], grad_out.T


def solution(mesh):
    split = Mesh(
        mesh.devices.reshape(mesh.shape["gx"], 4, 2, mesh.shape["gz"]), ("gx", "gy_0", "gy_1", "gz")
    )
    placed = (
        P(None, "gx", GY, "gz"),
        P(None, "gx", GY, "gz"),
        P("gx", GY, "gz"),
        P(None, "gx", GY, "gz"),
        P(),
        P(),
        P(),
        P(),
    )
    return jax.shard_map(
        per_device,
        mesh=split,
        in_specs=placed,
        out_specs=(P(None, "gx", GY, "gz"), P(), P(), P()),
        check_vma=False,
    )
```

```python
import jax
import jax.numpy as jnp
from jax import lax
from jax.experimental import pallas as pl
from jax.experimental.pallas import tpu as pltpu
from jax.sharding import Mesh
from jax.sharding import PartitionSpec as P

GY = ("gy_0", "gy_1")
CLOSURE = 8
XY = ("gx", "gy_0", "gy_1")
ALL = ("gx", "gy_0", "gy_1", "gz")
F32 = jnp.float32
BF16 = jnp.bfloat16
HIGHEST = lax.Precision.HIGHEST
MASS_SHIFT = 0.05
CELLS = 2097152.0

NXP, NYP, NZP = 22, 24, 256
REGION = (NXP, NYP, NZP)
L1 = (20, 32, 128)
L2 = (10, 16, 128)
MOST = {24: 7, 32: 16, 16: 8}


def shaped(shape, dtype=F32):
    return jax.ShapeDtypeStruct(shape, dtype)


def call(body, outs, args, scratch=(), smem=()):
    spaces = [
        pltpu.SMEM if i in smem else pltpu.VMEM for i in range(len(args))
    ]
    specs = [pl.BlockSpec(memory_space=space) for space in spaces]
    return pl.pallas_call(
        body,
        out_shape=outs,
        in_specs=specs,
        out_specs=[pl.BlockSpec(memory_space=pltpu.VMEM)] * len(outs),
        scratch_shapes=list(scratch),
        compiler_params=pltpu.CompilerParams(vmem_limit_bytes=12 << 20),
    )(*args)


def back(x, axis):
    return pltpu.roll(x, x.shape[axis] - 1, axis)


def forth(x, axis):
    return pltpu.roll(x, 1, axis)


def exact_dot(a, b):
    return jnp.dot(a, b, precision=HIGHEST, preferred_element_type=F32)


def chosen_dot(a, b):
    high = a.astype(BF16)
    rest = a - high.astype(F32)
    middle = rest.astype(BF16)
    low = (rest - middle.astype(F32)).astype(BF16)
    count = a.shape[0]
    parts = jnp.dot(
        jnp.concatenate([high, middle, low], axis=0), b.astype(BF16), preferred_element_type=F32
    )
    return (parts[2 * count :] + parts[count : 2 * count]) + parts[:count]


def steps(count, rows):
    return max(k for k in range(1, MOST[rows] + 1) if count % k == 0)


def planes(lo, hi, body, unroll=2):
    def step(i, carry):
        body(i)
        return carry

    lax.fori_loop(lo, hi, step, 0, unroll=unroll)


def around(src, ax, ay, az, i):
    v = src[i]
    y, z = ay[i], az[i]
    total = ax[i] * src[i + 1] + ax[i - 1] * src[i - 1]
    total = total + (y * back(v, 0) + forth(y * v, 0))
    return v, total + (z * back(v, 1) + forth(z * v, 1))


def sweep(src, dst, s, w, ax, ay, az, lo, hi):
    def one(i):
        v, total = around(src, ax, ay, az, i)
        dst[i] = 0.2 * v + w[i] * (s[i] + total)

    planes(lo, hi, one, steps(hi - lo, src.shape[1]))


def first_sweep(dst, s, w, lo, hi):
    def one(i):
        dst[i] = w[i] * s[i]

    planes(lo, hi, one, steps(hi - lo, s.shape[1]))


def face(here, there, weight, low, high):
    has, next_has = here > 0.0, there > 0.0
    factor = jnp.where(
        has, jnp.where(next_has, F32(1.0), high), jnp.where(next_has, low, F32(0.0))
    )
    total = jnp.where(has | next_has, here + there, F32(1.0))
    return weight * 2.0 / total * factor


def coefficients(rho, opens, weight, refs, lo, hi, whole_y):
    ax, ay, az, w, d = refs
    low, high = opens
    count = rho.shape[1]

    def one_face(i):
        ax[i] = face(rho[i], rho[i + 1], weight, low[0], high[0])

    planes(lo - 1, hi, one_face, 7 if count == 24 else 1)

    def one(i):
        r = rho[i]
        after = back(r, 0)
        row = lax.broadcasted_iota(jnp.int32, r.shape, 0)
        if whole_y:
            after = jnp.where(row == count - 1, F32(0.0), after)
        up_y = face(r, after, weight, low[1], high[1])
        if whole_y:
            first = jnp.where(r > 0.0, weight * 2.0 / jnp.where(r > 0.0, r, F32(1.0)), F32(0.0))
            down_y = jnp.where(row == 0, first * low[1], forth(up_y, 0))
        else:
            down_y = forth(up_y, 0)
        up_z = face(r, back(r, 1), weight, low[2], high[2])
        diagonal = MASS_SHIFT + ax[i] + ax[i - 1] + up_y + down_y + up_z + forth(up_z, 1)
        ay[i] = jnp.where(row == count - 1, F32(0.0), up_y) if whole_y else up_y
        az[i] = up_z
        d[i] = diagonal
        w[i] = jnp.where(r > 0.0, 0.8 / diagonal, F32(0.0))

    planes(lo, hi, one, 4)


def lane_pairs(cells, kept, repeat):
    row = lax.broadcasted_iota(jnp.int32, (cells, kept), 0)
    col = lax.broadcasted_iota(jnp.int32, (cells, kept), 1)
    return jnp.where(row // 2 == col % repeat, F32(1.0), F32(0.0))


def lane_spread(cells, kept):
    row = lax.broadcasted_iota(jnp.int32, (cells, kept), 0)
    col = lax.broadcasted_iota(jnp.int32, (cells, kept), 1)
    return jnp.where(col // 2 == row, F32(1.0), F32(0.0))


def block_means(read, rows, out, out_row):
    pairs = [read(7 + 2 * k) + read(8 + 2 * k) for k in range(4)]
    rows[...] = chosen_dot(jnp.concatenate(pairs, axis=0), lane_pairs(256, 128, 128))
    total = 0.125 * (rows[pl.ds(0, 16, stride=2), :] + rows[pl.ds(1, 16, stride=2), :])
    for k in range(32):
        out[k, out_row : out_row + 16, :] = total


def presmooth(s, v, va, coefs, rows, out):
    ax, ay, az, w, d = coefs
    first_sweep(v, s, w, 1, 21)
    sweep(v, va, s, w, ax, ay, az, 2, 20)
    sweep(va, v, s, w, ax, ay, az, 3, 19)

    def residue(i):
        centre, total = around(v, ax, ay, az, i)
        return (s[i] + total - d[i] * centre)[8:16]

    block_means(residue, rows, out, 0)


def opens_of(sc):
    values = [sc[3 + k].astype(F32) for k in range(6)]
    return values[0::2], values[1::2]


def start_body(
    sc, own, low, high, b, ax, ay, az, w, d, v, out, low_faces, rho, va, rows
):
    along_y(sc, own, low, high, b, rho, low_faces)
    coefs = (ax, ay, az, w, d)
    for ref in (ax, ay, az, w, d, v):
        ref[0] = jnp.zeros((NYP, NZP), F32)
        ref[21] = jnp.zeros((NYP, NZP), F32)
    coefficients(rho, opens_of(sc), 1.0, coefs, 1, 21, False)
    presmooth(b, v, va, coefs, rows, out)
    block_means(lambda i: rho[i, 8:16, :], rows, out, 16)


def pre_body(b, ax, ay, az, w, d, v, out, va, rows):
    v[0] = jnp.zeros((NYP, NZP), F32)
    v[21] = jnp.zeros((NYP, NZP), F32)
    presmooth(b, v, va, (ax, ay, az, w, d), rows, out)


def again_body(b, p, ax, ay, az, w, d, s, v, out, va, rows):
    for ref in (s, v):
        ref[0] = jnp.zeros((NYP, NZP), F32)
        ref[21] = jnp.zeros((NYP, NZP), F32)

    def one(i):
        centre, total = around(p, ax, ay, az, i)
        s[i] = b[i] + total - d[i] * centre

    planes(1, 21, one, 5)
    presmooth(s, v, va, (ax, ay, az, w, d), rows, out)


def whole_plane(parts, first, dst):
    for k in range(2):
        dst[k] = jnp.zeros((32, 128), F32)
        dst[18 + k] = jnp.zeros((32, 128), F32)
    for device in range(32):
        x, y = divmod(device, 8)
        for k in range(4):
            dst[2 + 4 * x + k, 4 * y : 4 * y + 4, :] = parts[
                device, first + 4 * k : first + 4 * k + 4, :
            ]


def restrict_whole(read, rows, dst):
    for k in range(8):
        rows[32 * k : 32 * k + 32, :] = read(2 + 2 * k) + read(3 + 2 * k)
    rows[...] = chosen_dot(rows[...], lane_pairs(128, 128, 64))
    for k in range(8):
        total = (
            rows[pl.ds(32 * k, 16, stride=2), :] + rows[pl.ds(32 * k + 1, 16, stride=2), :]
        )
        dst[1 + k] = 0.125 * total


def coarse_body(
    sc, parts, ax1, ay1, az1, w1, d1, ax2, ay2, az2, w2, d2, rho1, rho2, rows
):
    for ref in (ax1, ay1, az1, w1, d1):
        ref[...] = jnp.zeros(L1, F32)
    for ref in (ax2, ay2, az2, w2, d2, rho2):
        ref[...] = jnp.zeros(L2, F32)
    opens = opens_of(sc)
    whole_plane(parts, 16, rho1)
    coefficients(rho1, opens, 0.25, (ax1, ay1, az1, w1, d1), 2, 18, True)
    restrict_whole(lambda i: rho1[i], rows, rho2)
    coefficients(rho2, opens, 0.0625, (ax2, ay2, az2, w2, d2), 1, 9, True)


def correct(
    sc, parts, coefs1, coefs2, s1, v1, u1, s2, v2, u2, rows, wide_a, wide_b
):
    ax1, ay1, az1, w1, d1 = coefs1
    ax2, ay2, az2, w2, d2 = coefs2
    whole_plane(parts, 0, s1)
    for ref in (v1, u1):
        for k in (0, 1, 18, 19):
            ref[k] = jnp.zeros((32, 128), F32)
    for ref in (v2, u2):
        for k in (0, 9):
            ref[k] = jnp.zeros((16, 128), F32)
    first_sweep(v1, s1, w1, 2, 18)
    sweep(v1, u1, s1, w1, ax1, ay1, az1, 2, 18)
    sweep(u1, v1, s1, w1, ax1, ay1, az1, 2, 18)

    def residue(i):
        centre, total = around(v1, ax1, ay1, az1, i)
        return s1[i] + total - d1[i] * centre

    restrict_whole(residue, rows, s2)
    first_sweep(v2, s2, w2, 1, 9)
    for k in range(5):
        a, b = (v2, u2) if k % 2 == 0 else (u2, v2)
        sweep(a, b, s2, w2, ax2, ay2, az2, 1, 9)
    spread = chosen_dot(
        jnp.concatenate([u2[1 + k] for k in range(8)], axis=0), lane_spread(128, 128)
    )
    rows[pl.ds(0, 128, stride=2), :] = spread
    rows[pl.ds(1, 128, stride=2), :] = spread
    for k in range(8):
        more = rows[32 * k : 32 * k + 32, :]
        v1[2 + 2 * k] = v1[2 + 2 * k] + more
        v1[3 + 2 * k] = v1[3 + 2 * k] + more
    sweep(v1, u1, s1, w1, ax1, ay1, az1, 2, 18)
    sweep(u1, v1, s1, w1, ax1, ay1, az1, 2, 18)
    sweep(v1, u1, s1, w1, ax1, ay1, az1, 2, 18)
    base = sc[0] * 4
    near = jnp.concatenate([u1[base + k] for k in range(8)], axis=0)
    wide = chosen_dot(near, lane_spread(128, 256))
    for lanes, ref in ((slice(0, 128), wide_a), (slice(128, 256), wide_b)):
        for k in range(8):
            ref[80 * k : 80 * k + 8, :] = jnp.zeros((8, 128), F32)
            ref[80 * k + 72 : 80 * k + 80, :] = jnp.zeros((8, 128), F32)
            part = wide[32 * k : 32 * k + 32, lanes]
            ref[pl.ds(80 * k + 8, 32, stride=2), :] = part
            ref[pl.ds(80 * k + 9, 32, stride=2), :] = part


def postsmooth(sc, s, v, coefs, wide_a, wide_b, va, vb):
    ax, ay, az, w = coefs
    row = pl.multiple_of(sc[1] * 8, 8)
    for i in range(3, 19):
        k = (i - 3) // 2
        more = jnp.concatenate(
            [wide_a[pl.ds(80 * k + row, 24), :], wide_b[pl.ds(80 * k + row, 24), :]], axis=1
        )
        va[i] = v[i] + more
    sweep(va, vb, s, w, ax, ay, az, 4, 18)
    sweep(vb, va, s, w, ax, ay, az, 5, 17)


POST_SCRATCH = (
    [pltpu.VMEM(L1, F32)] * 3
    + [pltpu.VMEM(L2, F32)] * 3
    + [pltpu.VMEM((256, 128), F32)]
    + [pltpu.VMEM((640, 128), F32)] * 2
    + [pltpu.VMEM(REGION, F32)] * 2
)


def post_own_body(
    sc, parts, ax1, ay1, az1, w1, d1, ax2, ay2, az2, w2, d2, s, v, ax, ay, az, w, out, *scratch
):
    *inner, wide_a, wide_b, va, vb = scratch
    correct(
        sc,
        parts,
        (ax1, ay1, az1, w1, d1),
        (ax2, ay2, az2, w2, d2),
        *inner,
        wide_a,
        wide_b,
    )
    postsmooth(sc, s, v, (ax, ay, az, w), wide_a, wide_b, va, vb)
    for i in range(8):
        centre, total = around(va, ax, ay, az, i + 7)
        new = 0.2 * centre + w[i + 7] * (s[i + 7] + total)
        out[i] = new[8:16, 0:128]


def post_near_body(
    sc, parts, ax1, ay1, az1, w1, d1, ax2, ay2, az2, w2, d2, s, v, ax, ay, az, w, p, out, *scratch
):
    *inner, wide_a, wide_b, va, vb = scratch
    correct(
        sc,
        parts,
        (ax1, ay1, az1, w1, d1),
        (ax2, ay2, az2, w2, d2),
        *inner,
        wide_a,
        wide_b,
    )
    postsmooth(sc, s, v, (ax, ay, az, w), wide_a, wide_b, va, vb)
    for i in range(10):
        centre, total = around(va, ax, ay, az, i + 6)
        out[i] = p[i + 6] + 0.2 * centre + w[i + 6] * (s[i + 6] + total)


def members(count, groups):
    r = lax.broadcasted_iota(jnp.int32, (count, groups), 0)
    c = lax.broadcasted_iota(jnp.int32, (count, groups), 1)
    return jnp.where(r // 8 == c, F32(1.0), F32(0.0)).astype(BF16)


def same_row(x):
    r = lax.broadcasted_iota(jnp.int32, x.shape, 0)
    c = lax.broadcasted_iota(jnp.int32, x.shape, 1)
    return jnp.where(r % 8 == c % 8, x, F32(0.0)).astype(BF16)


ACROSS = (((1,), (1,)), ((), ()))


def dot_across(a, b, precision=None):
    return lax.dot_general(a, b, ACROSS, precision=precision, preferred_element_type=F32)


def closure_body(
    sc,
    features,
    fields,
    weights,
    flux,
    slope,
    hidden,
    message,
    target_faces,
    marks,
    kin,
    bias,
    kout,
):
    velocity, target = fields.at[0:3], fields.at[3:6]
    message[8:16] = fields[6]
    weight_in = weights[0:16, :].astype(BF16)
    weight_out = weights[24:27, :].astype(BF16)
    units = members(512, 64)
    narrow = dot_across(units, weight_in).astype(BF16)
    kin[...] = same_row(dot_across(narrow, members(128, 16)))
    narrow = jnp.dot(members(24, 3), weight_out, preferred_element_type=F32).astype(BF16)
    kout[...] = same_row(dot_across(narrow, units))
    bias[...] = dot_across(
        units.astype(F32), jnp.broadcast_to(weights[16:17, :], (128, 64)), HIGHEST
    )
    _, high = opens_of(sc)
    high_x = jnp.where(sc[0] == 3, high[0], F32(1.0))
    high_y = jnp.where(sc[1] == 7, high[1], F32(1.0))
    high_z = jnp.where(sc[2] == 7, high[2], F32(1.0))
    row = lax.broadcasted_iota(jnp.int32, (8, 128), 0)
    col = lax.broadcasted_iota(jnp.int32, (8, 128), 1)
    factor_y = jnp.where(row == 7, high_y, F32(1.0))
    factor_z = jnp.where(col == 127, high_z, F32(1.0))
    def one(x):
        columns = features[:, x, :, :].astype(F32).reshape(128, 128).astype(BF16)
        before = jnp.dot(kin[...], columns, preferred_element_type=F32) + bias[...]
        gate = 1.0 / (1.0 + jnp.exp(-before))
        unit = (before * gate).astype(BF16)
        hidden[x] = unit
        slope[x] = gate * (1.0 + before * (1.0 - gate))
        shift = jnp.dot(kout[...], unit, preferred_element_type=F32)
        factor_x = jnp.where(x == 7, high_x, F32(1.0))
        flux[0, x] = (velocity[0, x] + shift[0:8]) * factor_x
        flux[1, x] = (velocity[1, x] + shift[8:16]) * factor_y
        flux[2, x] = (velocity[2, x] + shift[16:24]) * factor_z

    planes(0, 8, one, CLOSURE)
    zero = jnp.zeros((8, 128), F32)
    ends = zero
    for x in range(8):
        bx, by, bz = shifted(
            lambda d, i: flux[d, i], lambda: zero, lambda i: zero, lambda i: zero, x
        )
        message[x] = -((flux[0, x] - bx) + (flux[1, x] - by) + (flux[2, x] - bz))
        message[17, x : x + 1, :] = flux[1, x, 7:8, :]
        target_faces[1, x : x + 1, :] = target[1, x, 7:8, :]
        ends = jnp.where(col == x, pltpu.roll(flux[2, x], x + 1, 1), ends)
        ends = jnp.where(col == x + 8, pltpu.roll(target[2, x], x + 9, 1), ends)
    message[16] = flux[0, 7]
    message[18] = ends
    target_faces[0] = target[0, 7]
    inside = inside_of(sc)
    wide_col = lax.broadcasted_iota(jnp.int32, (1, 256), 1)
    one_row = jnp.ones((1, 256), F32)
    marks[0:1, :] = jnp.where(wide_col < 64, inside[2][1], F32(0.0))
    marks[1:2, :] = jnp.where(wide_col < 64, F32(0.0), inside[2][0])
    for d in range(2):
        marks[2 + 2 * d : 3 + 2 * d, :] = one_row * inside[d][0]
        marks[3 + 2 * d : 4 + 2 * d, :] = one_row * inside[d][1]
    marks[6:8, :] = jnp.zeros((2, 256), F32)


def shifted(field, low_x, low_y, low_z, x):
    row = lax.broadcasted_iota(jnp.int32, (8, 128), 0)
    col = lax.broadcasted_iota(jnp.int32, (8, 128), 1)
    before_x = low_x() if x == 0 else field(0, x - 1)
    before_y = jnp.where(row == 0, low_y(x), forth(field(1, x), 0))
    before_z = jnp.where(col == 0, low_z(x), forth(field(2, x), 1))
    return before_x, before_y, before_z


def inside_of(sc):
    last = (3, 7, 7)
    return [
        (
            jnp.where(sc[d] > 0, F32(1.0), F32(0.0)),
            jnp.where(sc[d] < last[d], F32(1.0), F32(0.0)),
        )
        for d in range(3)
    ]


def along_z_body(sc, own, before, after, target_faces, wide, up, down):
    has_before, has_after = inside_of(sc)[2]
    col = lax.broadcasted_iota(jnp.int32, (8, 128), 1)

    def around_z(k):
        return jnp.where(col < 64, after[k] * has_after, before[k] * has_before)

    for k in range(18):
        here, there = own[k], around_z(k)
        if k < 8:
            turn = (128 - k) % 128
            low = pltpu.roll(before[18], turn, 1) if turn else before[18]
            high = pltpu.roll(own[18], turn, 1) if turn else own[18]
            here = jnp.where(col == 0, here + low * has_before, here)
            there = jnp.where(col == 0, there + high * has_after, there)
        wide[k, :, 0:128] = here
        wide[k, :, 128:256] = there
    for k in range(7):
        up[k] = wide[k + 1]
        up[k + 7] = wide[k + 9]
        down[k] = wide[k]
        down[k + 7] = wide[k + 8]
    up[14] = wide[17]
    down[14] = wide[17]
    up[15] = wide[16]
    up[16, :, 0:128] = target_faces[0]
    up[16, :, 128:256] = jnp.zeros((8, 128), F32)


def along_x_body(sc, wide, low, high, target_faces, out):
    has_before, has_after = inside_of(sc)[0]
    for k in range(7):
        out[k] = low[k] * has_before
        out[k + 22] = low[k + 7] * has_before
        more = wide[16] if k == 0 else jnp.zeros((8, 256), F32)
        out[k + 15] = (high[k] + more) * has_after
        out[k + 37] = high[k + 7] * has_after
    for k in range(8):
        out[k + 7] = wide[k] + low[15] * has_before if k == 0 else wide[k]
        out[k + 29] = wide[k + 8]
    out[44] = low[14] * has_before
    out[45] = wide[17]
    out[46] = high[14] * has_after
    out[47, :, 0:128] = target_faces[1]
    out[47, :, 128:256] = jnp.zeros((8, 128), F32)


def along_y(sc, own, low, high, b, rho, low_faces):
    has_before, has_after = inside_of(sc)[1]
    row = lax.broadcasted_iota(jnp.int32, (8, 256), 0)
    for i in range(22):
        k, r = divmod(i + 1, 8)
        more = jnp.broadcast_to(low[44 + k, r : r + 1, :] * has_before, (8, 256))
        next_more = jnp.broadcast_to(own[44 + k, r : r + 1, :], (8, 256))
        b[i, 0:8, :] = low[i] * has_before
        b[i, 8:16, :] = jnp.where(row == 0, own[i] + more, own[i])
        b[i, 16:24, :] = jnp.where(row == 0, high[i] + next_more, high[i]) * has_after
        rho[i, 0:8, :] = low[i + 22] * has_before
        rho[i, 8:16, :] = own[i + 22]
        rho[i, 16:24, :] = high[i + 22] * has_after
    low_faces[0] = low[45, :, 0:128]
    low_faces[1] = low[47, :, 0:128]


def middle_body(sc, near, flux, fields, from_x, low_y, from_z, ax, ay, az, new, misfit, out):
    scale = F32(1.0 / CELLS)
    target = fields.at[3:6]
    inner = [jnp.where(sc[d] > 0, F32(1.0), F32(0.0)) for d in range(3)]

    def rises(i):
        p = near[i]
        return p, back(p, 0) - p, back(p, 1) - p

    for x in range(8):
        p, rise_y, rise_z = rises(x + 1)
        rise_x = near[x + 2] - p
        parts = (ax[x + 7] * rise_x, ay[x + 7] * rise_y, az[x + 7] * rise_z)
        for d in range(3):
            value = flux[d, x] - parts[d][8:16, 0:128]
            new[d, x] = value
            misfit[d, x] = (value - target[d, x]) * scale

    def low_weighted_x():
        up = ax[6, 8:16, 0:128]
        rise = (near[1] - near[0])[8:16, 0:128]
        value = from_x[15, :, 0:128] - up * rise - from_x[16, :, 0:128]
        return up * (value * (scale * inner[0]))

    def low_weighted_y(x):
        up = ay[x + 7, 7:8, 0:128]
        rise = near[x + 1, 8:9, 0:128] - near[x + 1, 7:8, 0:128]
        value = low_y[0, x : x + 1, :] - up * rise - low_y[1, x : x + 1, :]
        return jnp.broadcast_to(up * (value * (scale * inner[1])), (8, 128))

    def low_weighted_z(x):
        p = near[x + 1, 8:16, :]
        rise = (back(p, 1) - p)[:, 128:256]
        up = az[x + 7, 8:16, 128:256]
        low_flux = pltpu.roll(from_z[18], 127 - x, 1)
        low_target = pltpu.roll(from_z[18], 119 - x, 1)
        value = up * ((low_flux - up * rise - low_target) * (scale * inner[2]))
        return forth(value, 1)

    refs = (ax, ay, az)

    def weighted(d, x):
        return refs[d][x + 7, 8:16, 0:128] * misfit[d, x]

    for x in range(8):
        bx, by, bz = shifted(weighted, low_weighted_x, low_weighted_y, low_weighted_z, x)
        out[x] = (weighted(0, x) - bx) + (weighted(1, x) - by) + (weighted(2, x) - bz)


def gradient_body(
    sc, near, misfit, features, slope, hidden, weights, out, acc_in, acc_bias, acc_out, kback
):
    narrow = dot_across(members(512, 64), weights[24:27, :].astype(BF16)).astype(BF16)
    kback[...] = same_row(dot_across(narrow, members(24, 3)))
    _, high = opens_of(sc)
    high_x = jnp.where(sc[0] == 3, high[0], F32(1.0))
    high_y = jnp.where(sc[1] == 7, high[1], F32(1.0))
    high_z = jnp.where(sc[2] == 7, high[2], F32(1.0))
    row = lax.broadcasted_iota(jnp.int32, (8, 128), 0)
    col = lax.broadcasted_iota(jnp.int32, (8, 128), 1)
    factor_y = jnp.where(row == 7, high_y, F32(1.0))
    factor_z = jnp.where(col == 127, high_z, F32(1.0))
    acc_in[...] = jnp.zeros((128, 512), F32)
    acc_bias[...] = jnp.zeros((512, 128), F32)
    acc_out[...] = jnp.zeros((24, 512), F32)
    across = ACROSS

    def one(x):
        p = near[x + 1]
        rise_x = (near[x + 2] - p)[8:16, 0:128]
        rise_y = (back(p, 0) - p)[8:16, 0:128]
        rise_z = (back(p, 1) - p)[8:16, 0:128]
        factor_x = jnp.where(x == 7, high_x, F32(1.0))
        grads = jnp.concatenate(
            [
                (misfit[0, x] + rise_x) * factor_x,
                (misfit[1, x] + rise_y) * factor_y,
                (misfit[2, x] + rise_z) * factor_z,
            ],
            axis=0,
        ).astype(BF16)
        columns = features[:, x, :, :].astype(F32).reshape(128, 128).astype(BF16)
        grad_before = jnp.dot(kback[...], grads, preferred_element_type=F32) * slope[x]
        acc_bias[...] += grad_before
        acc_in[...] += lax.dot_general(
            columns, grad_before.astype(BF16), across, preferred_element_type=F32
        )
        acc_out[...] += lax.dot_general(grads, hidden[x], across, preferred_element_type=F32)

    planes(0, 8, one, CLOSURE)

    def same(count):
        r = lax.broadcasted_iota(jnp.int32, (count, 512), 0)
        c = lax.broadcasted_iota(jnp.int32, (count, 512), 1)
        return r % 8 == c % 8

    def grouped(count, groups):
        r = lax.broadcasted_iota(jnp.int32, (groups, count), 0)
        c = lax.broadcasted_iota(jnp.int32, (groups, count), 1)
        return jnp.where(c // 8 == r, F32(1.0), F32(0.0))

    hr = lax.broadcasted_iota(jnp.int32, (512, 64), 0)
    hc = lax.broadcasted_iota(jnp.int32, (512, 64), 1)
    fold = jnp.where(hr // 8 == hc, F32(1.0), F32(0.0))
    in_part = exact_dot(grouped(128, 16), jnp.where(same(128), acc_in[...], F32(0.0)))
    out_part = exact_dot(grouped(24, 8), jnp.where(same(24), acc_out[...], F32(0.0)))
    bias_part = lax.dot_general(
        jnp.ones((8, 128), F32), acc_bias[...], across, precision=HIGHEST, preferred_element_type=F32
    )
    folded = exact_dot(jnp.concatenate([in_part, out_part, bias_part], axis=0), fold)
    packed = jnp.concatenate(
        [
            jnp.concatenate([folded[0:8], folded[8:16]], axis=1),
            jnp.concatenate([folded[16:24], folded[24:32]], axis=1),
        ],
        axis=0,
    )
    for k in range(32):
        out[k] = packed


def plane_sum_body(parts, out):
    total = parts[0]
    for k in range(1, 32):
        total = total + parts[k]
    for k in range(8):
        out[k] = total


def ring(up, down, axis):
    count = lax.axis_size(axis)
    ups = [(i, (i + 1) % count) for i in range(count)]
    return lax.ppermute(up, axis, ups), lax.ppermute(down, axis, [(b, a) for a, b in ups])


def exchanged(own, marks):
    before, after = ring(own, own, "gz")
    wide = jnp.concatenate([own, after * marks[0, :128] + before * marks[1, :128]], axis=2)
    low, high = ring(wide[1:8], wide[0:7], "gx")
    wide = jnp.concatenate([low * marks[2], wide, high * marks[3]], axis=0)
    low, high = ring(wide, wide, GY)
    return jnp.concatenate([low * marks[4], wide, high * marks[5]], axis=1)


def unpack_body(parts, grad_in, grad_bias, grad_out):
    total = parts[0]
    for k in range(1, 8):
        total = total + parts[k]
    grad_in[0:8, :] = total[0:8, 0:64]
    grad_in[8:16, :] = total[0:8, 64:128]
    grad_bias[...] = total[8:9, 64:128]
    grad_out[...] = total[8:11, 0:64]


def sent_to_all(copies, axis):
    return lax.all_to_all(copies, axis, split_axis=0, concat_axis=0, tiled=True)


def per_device(velocity, features, density, target, weight_in, bias_in, weight_out, open_faces):
    place = jnp.stack([lax.axis_index("gx"), lax.axis_index(GY), lax.axis_index("gz")])
    sc = jnp.concatenate([place.astype(jnp.int32), open_faces])
    block = (8, 8, 128)
    weights = (
        jnp.pad(weight_in.astype(F32), ((0, 16), (0, 0)))
        + jnp.pad(bias_in[None], ((16, 15), (0, 0)))
        + jnp.pad(weight_out.T.astype(F32), ((24, 5), (0, 0)))
    )
    fields = jnp.concatenate([velocity, target, density[None]], axis=0)
    flux, slope, hidden, message, target_faces, marks = call(
        closure_body,
        [
            shaped((3, *block)),
            shaped((8, 512, 128)),
            shaped((8, 512, 128), BF16),
            shaped((19, 8, 128)),
            shaped((2, 8, 128)),
            shaped((8, 256)),
        ],
        (sc, features, fields, weights),
        [
            pltpu.VMEM((512, 128), BF16),
            pltpu.VMEM((512, 128), F32),
            pltpu.VMEM((24, 512), BF16),
        ],
        smem=(0,),
    )
    from_z, after = ring(message, message, "gz")
    wide, up, down = call(
        along_z_body,
        [shaped((18, 8, 256)), shaped((17, 8, 256)), shaped((15, 8, 256))],
        (sc, message, from_z, after, target_faces),
        smem=(0,),
    )
    from_x, after = ring(up, down, "gx")
    (message,) = call(
        along_x_body, [shaped((48, 8, 256))], (sc, wide, from_x, after, target_faces), smem=(0,)
    )
    before, after = ring(message, message, GY)
    region, to_plane = shaped(REGION), shaped((32, 16, 128))
    one_region = [pltpu.VMEM(REGION, F32), pltpu.VMEM((32, 128), F32)]
    source, *coefs, v, part, low_y = call(
        start_body,
        [region] * 7 + [shaped((32, 32, 128)), shaped((2, 8, 128))],
        (sc, message, before, after),
        [pltpu.VMEM(REGION, F32), *one_region],
        smem=(0,),
    )
    ax, ay, az, w, d = coefs
    parts = sent_to_all(part, XY)
    coarse = call(
        coarse_body,
        [shaped(L1)] * 5 + [shaped(L2)] * 5,
        (sc, parts),
        [pltpu.VMEM(L1, F32), pltpu.VMEM(L2, F32), pltpu.VMEM((256, 128), F32)],
        smem=(0,),
    )

    def finish_solve(b, v, parts):
        (own,) = call(
            post_own_body,
            [shaped(block)],
            (sc, parts, *coarse, b, v, ax, ay, az, w),
            POST_SCRATCH,
            smem=(0,),
        )
        p = exchanged(own, marks)
        s, v, part = call(
            again_body, [region, region, to_plane], (b, p, *coefs), one_region
        )
        (near,) = call(
            post_near_body,
            [shaped((10, NYP, NZP))],
            (sc, sent_to_all(part, XY), *coarse, s, v, ax, ay, az, w, p),
            POST_SCRATCH,
            smem=(0,),
        )
        return near

    near = finish_solve(source, v, parts)
    new_velocity, misfit, grad_pressure = call(
        middle_body,
        [shaped((3, *block)), shaped((3, *block)), shaped(block)],
        (sc, near, flux, fields, from_x, low_y, from_z, ax, ay, az),
        smem=(0,),
    )
    b = exchanged(grad_pressure, marks)
    v, part = call(pre_body, [region, to_plane], (b, *coefs), one_region)
    near = finish_solve(b, v, sent_to_all(part, XY))
    (packed,) = call(
        gradient_body,
        [to_plane],
        (sc, near, misfit, features, slope, hidden, weights),
        [
            pltpu.VMEM((128, 512), F32),
            pltpu.VMEM((512, 128), F32),
            pltpu.VMEM((24, 512), F32),
            pltpu.VMEM((512, 24), BF16),
        ],
        smem=(0,),
    )
    (plane,) = call(plane_sum_body, [shaped((8, 16, 128))], (sent_to_all(packed, XY),))
    grad_in, grad_bias, grad_out = call(
        unpack_body,
        [shaped((16, 64)), shaped((1, 64)), shaped((3, 64))],
        (sent_to_all(plane, "gz"),),
    )
    return new_velocity, grad_in, grad_bias[0], grad_out.T


def solution(mesh):
    split = Mesh(
        mesh.devices.reshape(mesh.shape["gx"], 4, 2, mesh.shape["gz"]), ("gx", "gy_0", "gy_1", "gz")
    )
    placed = (
        P(None, "gx", GY, "gz"),
        P(None, "gx", GY, "gz"),
        P("gx", GY, "gz"),
        P(None, "gx", GY, "gz"),
        P(),
        P(),
        P(),
        P(),
    )
    return jax.shard_map(
        per_device,
        mesh=split,
        in_specs=placed,
        out_specs=(P(None, "gx", GY, "gz"), P(), P(), P()),
        check_vma=False,
    )
```

```python
import jax
import jax.numpy as jnp
from jax import lax
from jax.experimental import pallas as pl
from jax.experimental.pallas import tpu as pltpu
from jax.sharding import Mesh
from jax.sharding import PartitionSpec as P

GY = ("gy_0", "gy_1")
CLOSURE = 8
XY = ("gx", "gy_0", "gy_1")
ALL = ("gx", "gy_0", "gy_1", "gz")
F32 = jnp.float32
BF16 = jnp.bfloat16
HIGHEST = lax.Precision.HIGHEST
MASS_SHIFT = 0.05
CELLS = 2097152.0

NXP, NYP, NZP = 22, 24, 256
REGION = (NXP, NYP, NZP)
L1 = (20, 32, 128)
L2 = (10, 16, 128)
MOST = {24: 10, 32: 16, 16: 8}


def shaped(shape, dtype=F32):
    return jax.ShapeDtypeStruct(shape, dtype)


def call(body, outs, args, scratch=(), smem=()):
    spaces = [
        pltpu.SMEM if i in smem else pltpu.VMEM for i in range(len(args))
    ]
    specs = [pl.BlockSpec(memory_space=space) for space in spaces]
    return pl.pallas_call(
        body,
        out_shape=outs,
        in_specs=specs,
        out_specs=[pl.BlockSpec(memory_space=pltpu.VMEM)] * len(outs),
        scratch_shapes=list(scratch),
        compiler_params=pltpu.CompilerParams(vmem_limit_bytes=12 << 20),
    )(*args)


def back(x, axis):
    return pltpu.roll(x, x.shape[axis] - 1, axis)


def forth(x, axis):
    return pltpu.roll(x, 1, axis)


def exact_dot(a, b):
    return jnp.dot(a, b, precision=HIGHEST, preferred_element_type=F32)


def chosen_dot(a, b):
    high = a.astype(BF16)
    rest = a - high.astype(F32)
    middle = rest.astype(BF16)
    low = (rest - middle.astype(F32)).astype(BF16)
    count = a.shape[0]
    parts = jnp.dot(
        jnp.concatenate([high, middle, low], axis=0), b.astype(BF16), preferred_element_type=F32
    )
    return (parts[2 * count :] + parts[count : 2 * count]) + parts[:count]


def steps(count, rows):
    return max(k for k in range(1, MOST[rows] + 1) if count % k == 0)


def planes(lo, hi, body, unroll=2):
    def step(i, carry):
        body(i)
        return carry

    lax.fori_loop(lo, hi, step, 0, unroll=unroll)


def around(src, ax, ay, az, i):
    v = src[i]
    y, z = ay[i], az[i]
    total = ax[i] * src[i + 1] + ax[i - 1] * src[i - 1]
    total = total + (y * back(v, 0) + forth(y * v, 0))
    return v, total + (z * back(v, 1) + forth(z * v, 1))


def sweep(src, dst, s, w, ax, ay, az, lo, hi):
    def one(i):
        v, total = around(src, ax, ay, az, i)
        dst[i] = 0.2 * v + w[i] * (s[i] + total)

    planes(lo, hi, one, steps(hi - lo, src.shape[1]))


def first_sweep(dst, s, w, lo, hi):
    def one(i):
        dst[i] = w[i] * s[i]

    planes(lo, hi, one, steps(hi - lo, s.shape[1]))


def face(here, there, weight, low, high):
    has, next_has = here > 0.0, there > 0.0
    factor = jnp.where(
        has, jnp.where(next_has, F32(1.0), high), jnp.where(next_has, low, F32(0.0))
    )
    total = jnp.where(has | next_has, here + there, F32(1.0))
    return weight * 2.0 / total * factor


def coefficients(rho, opens, weight, refs, lo, hi, whole_y):
    ax, ay, az, w, d = refs
    low, high = opens
    count = rho.shape[1]

    def one_face(i):
        ax[i] = face(rho[i], rho[i + 1], weight, low[0], high[0])

    planes(lo - 1, hi, one_face, 7 if count == 24 else (hi - lo + 1))

    def one(i):
        r = rho[i]
        after = back(r, 0)
        row = lax.broadcasted_iota(jnp.int32, r.shape, 0)
        if whole_y:
            after = jnp.where(row == count - 1, F32(0.0), after)
        up_y = face(r, after, weight, low[1], high[1])
        if whole_y:
            first = jnp.where(r > 0.0, weight * 2.0 / jnp.where(r > 0.0, r, F32(1.0)), F32(0.0))
            down_y = jnp.where(row == 0, first * low[1], forth(up_y, 0))
        else:
            down_y = forth(up_y, 0)
        up_z = face(r, back(r, 1), weight, low[2], high[2])
        diagonal = MASS_SHIFT + ax[i] + ax[i - 1] + up_y + down_y + up_z + forth(up_z, 1)
        ay[i] = jnp.where(row == count - 1, F32(0.0), up_y) if whole_y else up_y
        az[i] = up_z
        d[i] = diagonal
        w[i] = jnp.where(r > 0.0, 0.8 / diagonal, F32(0.0))

    planes(lo, hi, one, 5 if count == 24 else 8)


def lane_pairs(cells, kept, repeat):
    row = lax.broadcasted_iota(jnp.int32, (cells, kept), 0)
    col = lax.broadcasted_iota(jnp.int32, (cells, kept), 1)
    return jnp.where(row // 2 == col % repeat, F32(1.0), F32(0.0))


def lane_spread(cells, kept):
    row = lax.broadcasted_iota(jnp.int32, (cells, kept), 0)
    col = lax.broadcasted_iota(jnp.int32, (cells, kept), 1)
    return jnp.where(col // 2 == row, F32(1.0), F32(0.0))


def block_means(read, rows, out, out_row):
    pairs = [read(7 + 2 * k) + read(8 + 2 * k) for k in range(4)]
    rows[...] = chosen_dot(jnp.concatenate(pairs, axis=0), lane_pairs(256, 128, 128))
    total = 0.125 * (rows[pl.ds(0, 16, stride=2), :] + rows[pl.ds(1, 16, stride=2), :])
    for k in range(32):
        out[k, out_row : out_row + 16, :] = total


def presmooth(s, v, va, coefs, rows, out):
    ax, ay, az, w, d = coefs
    first_sweep(v, s, w, 1, 21)
    sweep(v, va, s, w, ax, ay, az, 2, 20)
    sweep(va, v, s, w, ax, ay, az, 3, 19)

    def residue(i):
        centre, total = around(v, ax, ay, az, i)
        return (s[i] + total - d[i] * centre)[8:16]

    block_means(residue, rows, out, 0)


def opens_of(sc):
    values = [sc[3 + k].astype(F32) for k in range(6)]
    return values[0::2], values[1::2]


def start_body(
    sc, own, low, high, b, ax, ay, az, w, d, v, out, low_faces, rho, va, rows
):
    along_y(sc, own, low, high, b, rho, low_faces)
    coefs = (ax, ay, az, w, d)
    for ref in (ax, ay, az, w, d, v):
        ref[0] = jnp.zeros((NYP, NZP), F32)
        ref[21] = jnp.zeros((NYP, NZP), F32)
    coefficients(rho, opens_of(sc), 1.0, coefs, 1, 21, False)
    presmooth(b, v, va, coefs, rows, out)
    block_means(lambda i: rho[i, 8:16, :], rows, out, 16)


def pre_body(b, ax, ay, az, w, d, v, out, va, rows):
    v[0] = jnp.zeros((NYP, NZP), F32)
    v[21] = jnp.zeros((NYP, NZP), F32)
    presmooth(b, v, va, (ax, ay, az, w, d), rows, out)


def again_body(b, p, ax, ay, az, w, d, s, v, out, va, rows):
    for ref in (s, v):
        ref[0] = jnp.zeros((NYP, NZP), F32)
        ref[21] = jnp.zeros((NYP, NZP), F32)

    def one(i):
        centre, total = around(p, ax, ay, az, i)
        s[i] = b[i] + total - d[i] * centre

    planes(1, 21, one, 10)
    presmooth(s, v, va, (ax, ay, az, w, d), rows, out)


def whole_plane(parts, first, dst):
    for k in range(2):
        dst[k] = jnp.zeros((32, 128), F32)
        dst[18 + k] = jnp.zeros((32, 128), F32)
    for device in range(32):
        x, y = divmod(device, 8)
        for k in range(4):
            dst[2 + 4 * x + k, 4 * y : 4 * y + 4, :] = parts[
                device, first + 4 * k : first + 4 * k + 4, :
            ]


def restrict_whole(read, rows, dst):
    for k in range(8):
        rows[32 * k : 32 * k + 32, :] = read(2 + 2 * k) + read(3 + 2 * k)
    rows[...] = chosen_dot(rows[...], lane_pairs(128, 128, 64))
    for k in range(8):
        total = (
            rows[pl.ds(32 * k, 16, stride=2), :] + rows[pl.ds(32 * k + 1, 16, stride=2), :]
        )
        dst[1 + k] = 0.125 * total


def coarse_body(
    sc, parts, ax1, ay1, az1, w1, d1, ax2, ay2, az2, w2, d2, rho1, rho2, rows
):
    for ref in (ax1, ay1, az1, w1, d1):
        ref[...] = jnp.zeros(L1, F32)
    for ref in (ax2, ay2, az2, w2, d2, rho2):
        ref[...] = jnp.zeros(L2, F32)
    opens = opens_of(sc)
    whole_plane(parts, 16, rho1)
    coefficients(rho1, opens, 0.25, (ax1, ay1, az1, w1, d1), 2, 18, True)
    restrict_whole(lambda i: rho1[i], rows, rho2)
    coefficients(rho2, opens, 0.0625, (ax2, ay2, az2, w2, d2), 1, 9, True)


def correct(
    sc, parts, coefs1, coefs2, s1, v1, u1, s2, v2, u2, rows, wide_a, wide_b
):
    ax1, ay1, az1, w1, d1 = coefs1
    ax2, ay2, az2, w2, d2 = coefs2
    whole_plane(parts, 0, s1)
    for ref in (v1, u1):
        for k in (0, 1, 18, 19):
            ref[k] = jnp.zeros((32, 128), F32)
    for ref in (v2, u2):
        for k in (0, 9):
            ref[k] = jnp.zeros((16, 128), F32)
    first_sweep(v1, s1, w1, 2, 18)
    sweep(v1, u1, s1, w1, ax1, ay1, az1, 2, 18)
    sweep(u1, v1, s1, w1, ax1, ay1, az1, 2, 18)

    def residue(i):
        centre, total = around(v1, ax1, ay1, az1, i)
        return s1[i] + total - d1[i] * centre

    restrict_whole(residue, rows, s2)
    first_sweep(v2, s2, w2, 1, 9)
    for k in range(5):
        a, b = (v2, u2) if k % 2 == 0 else (u2, v2)
        sweep(a, b, s2, w2, ax2, ay2, az2, 1, 9)
    spread = chosen_dot(
        jnp.concatenate([u2[1 + k] for k in range(8)], axis=0), lane_spread(128, 128)
    )
    rows[pl.ds(0, 128, stride=2), :] = spread
    rows[pl.ds(1, 128, stride=2), :] = spread
    for k in range(8):
        more = rows[32 * k : 32 * k + 32, :]
        v1[2 + 2 * k] = v1[2 + 2 * k] + more
        v1[3 + 2 * k] = v1[3 + 2 * k] + more
    sweep(v1, u1, s1, w1, ax1, ay1, az1, 2, 18)
    sweep(u1, v1, s1, w1, ax1, ay1, az1, 2, 18)
    sweep(v1, u1, s1, w1, ax1, ay1, az1, 2, 18)
    base = sc[0] * 4
    near = jnp.concatenate([u1[base + k] for k in range(8)], axis=0)
    wide = chosen_dot(near, lane_spread(128, 256))
    for lanes, ref in ((slice(0, 128), wide_a), (slice(128, 256), wide_b)):
        for k in range(8):
            ref[80 * k : 80 * k + 8, :] = jnp.zeros((8, 128), F32)
            ref[80 * k + 72 : 80 * k + 80, :] = jnp.zeros((8, 128), F32)
            part = wide[32 * k : 32 * k + 32, lanes]
            ref[pl.ds(80 * k + 8, 32, stride=2), :] = part
            ref[pl.ds(80 * k + 9, 32, stride=2), :] = part


def postsmooth(sc, s, v, coefs, wide_a, wide_b, va, vb):
    ax, ay, az, w = coefs
    row = pl.multiple_of(sc[1] * 8, 8)
    for i in range(3, 19):
        k = (i - 3) // 2
        more = jnp.concatenate(
            [wide_a[pl.ds(80 * k + row, 24), :], wide_b[pl.ds(80 * k + row, 24), :]], axis=1
        )
        va[i] = v[i] + more
    sweep(va, vb, s, w, ax, ay, az, 4, 18)
    sweep(vb, va, s, w, ax, ay, az, 5, 17)


POST_SCRATCH = (
    [pltpu.VMEM(L1, F32)] * 3
    + [pltpu.VMEM(L2, F32)] * 3
    + [pltpu.VMEM((256, 128), F32)]
    + [pltpu.VMEM((640, 128), F32)] * 2
    + [pltpu.VMEM(REGION, F32)] * 2
)


def post_own_body(
    sc, parts, ax1, ay1, az1, w1, d1, ax2, ay2, az2, w2, d2, s, v, ax, ay, az, w, out, *scratch
):
    *inner, wide_a, wide_b, va, vb = scratch
    correct(
        sc,
        parts,
        (ax1, ay1, az1, w1, d1),
        (ax2, ay2, az2, w2, d2),
        *inner,
        wide_a,
        wide_b,
    )
    postsmooth(sc, s, v, (ax, ay, az, w), wide_a, wide_b, va, vb)
    for i in range(8):
        centre, total = around(va, ax, ay, az, i + 7)
        new = 0.2 * centre + w[i + 7] * (s[i + 7] + total)
        out[i] = new[8:16, 0:128]


def post_near_body(
    sc, parts, ax1, ay1, az1, w1, d1, ax2, ay2, az2, w2, d2, s, v, ax, ay, az, w, p, out, *scratch
):
    *inner, wide_a, wide_b, va, vb = scratch
    correct(
        sc,
        parts,
        (ax1, ay1, az1, w1, d1),
        (ax2, ay2, az2, w2, d2),
        *inner,
        wide_a,
        wide_b,
    )
    postsmooth(sc, s, v, (ax, ay, az, w), wide_a, wide_b, va, vb)
    for i in range(10):
        centre, total = around(va, ax, ay, az, i + 6)
        out[i] = p[i + 6] + 0.2 * centre + w[i + 6] * (s[i + 6] + total)


def members(count, groups):
    r = lax.broadcasted_iota(jnp.int32, (count, groups), 0)
    c = lax.broadcasted_iota(jnp.int32, (count, groups), 1)
    return jnp.where(r // 8 == c, F32(1.0), F32(0.0)).astype(BF16)


def same_row(x):
    r = lax.broadcasted_iota(jnp.int32, x.shape, 0)
    c = lax.broadcasted_iota(jnp.int32, x.shape, 1)
    return jnp.where(r % 8 == c % 8, x, F32(0.0)).astype(BF16)


ACROSS = (((1,), (1,)), ((), ()))


def dot_across(a, b, precision=None):
    return lax.dot_general(a, b, ACROSS, precision=precision, preferred_element_type=F32)


def closure_body(
    sc,
    features,
    fields,
    weights,
    flux,
    slope,
    hidden,
    message,
    target_faces,
    marks,
    kin,
    bias,
    kout,
):
    velocity, target = fields.at[0:3], fields.at[3:6]
    message[8:16] = fields[6]
    weight_in = weights[0:16, :].astype(BF16)
    weight_out = weights[24:27, :].astype(BF16)
    units = members(512, 64)
    narrow = dot_across(units, weight_in).astype(BF16)
    kin[...] = same_row(dot_across(narrow, members(128, 16)))
    narrow = jnp.dot(members(24, 3), weight_out, preferred_element_type=F32).astype(BF16)
    kout[...] = same_row(dot_across(narrow, units))
    bias[...] = dot_across(
        units.astype(F32), jnp.broadcast_to(weights[16:17, :], (128, 64)), HIGHEST
    )
    _, high = opens_of(sc)
    high_x = jnp.where(sc[0] == 3, high[0], F32(1.0))
    high_y = jnp.where(sc[1] == 7, high[1], F32(1.0))
    high_z = jnp.where(sc[2] == 7, high[2], F32(1.0))
    row = lax.broadcasted_iota(jnp.int32, (8, 128), 0)
    col = lax.broadcasted_iota(jnp.int32, (8, 128), 1)
    factor_y = jnp.where(row == 7, high_y, F32(1.0))
    factor_z = jnp.where(col == 127, high_z, F32(1.0))
    def one(x):
        columns = features[:, x, :, :].astype(F32).reshape(128, 128).astype(BF16)
        before = jnp.dot(kin[...], columns, preferred_element_type=F32) + bias[...]
        gate = 1.0 / (1.0 + jnp.exp(-before))
        unit = (before * gate).astype(BF16)
        hidden[x] = unit
        slope[x] = gate * (1.0 + before * (1.0 - gate))
        shift = jnp.dot(kout[...], unit, preferred_element_type=F32)
        factor_x = jnp.where(x == 7, high_x, F32(1.0))
        flux[0, x] = (velocity[0, x] + shift[0:8]) * factor_x
        flux[1, x] = (velocity[1, x] + shift[8:16]) * factor_y
        flux[2, x] = (velocity[2, x] + shift[16:24]) * factor_z

    planes(0, 8, one, CLOSURE)
    zero = jnp.zeros((8, 128), F32)
    ends = zero
    for x in range(8):
        bx, by, bz = shifted(
            lambda d, i: flux[d, i], lambda: zero, lambda i: zero, lambda i: zero, x
        )
        message[x] = -((flux[0, x] - bx) + (flux[1, x] - by) + (flux[2, x] - bz))
        message[17, x : x + 1, :] = flux[1, x, 7:8, :]
        target_faces[1, x : x + 1, :] = target[1, x, 7:8, :]
        ends = jnp.where(col == x, pltpu.roll(flux[2, x], x + 1, 1), ends)
        ends = jnp.where(col == x + 8, pltpu.roll(target[2, x], x + 9, 1), ends)
    message[16] = flux[0, 7]
    message[18] = ends
    target_faces[0] = target[0, 7]
    inside = inside_of(sc)
    wide_col = lax.broadcasted_iota(jnp.int32, (1, 256), 1)
    one_row = jnp.ones((1, 256), F32)
    marks[0:1, :] = jnp.where(wide_col < 64, inside[2][1], F32(0.0))
    marks[1:2, :] = jnp.where(wide_col < 64, F32(0.0), inside[2][0])
    for d in range(2):
        marks[2 + 2 * d : 3 + 2 * d, :] = one_row * inside[d][0]
        marks[3 + 2 * d : 4 + 2 * d, :] = one_row * inside[d][1]
    marks[6:8, :] = jnp.zeros((2, 256), F32)


def shifted(field, low_x, low_y, low_z, x):
    row = lax.broadcasted_iota(jnp.int32, (8, 128), 0)
    col = lax.broadcasted_iota(jnp.int32, (8, 128), 1)
    before_x = low_x() if x == 0 else field(0, x - 1)
    before_y = jnp.where(row == 0, low_y(x), forth(field(1, x), 0))
    before_z = jnp.where(col == 0, low_z(x), forth(field(2, x), 1))
    return before_x, before_y, before_z


def inside_of(sc):
    last = (3, 7, 7)
    return [
        (
            jnp.where(sc[d] > 0, F32(1.0), F32(0.0)),
            jnp.where(sc[d] < last[d], F32(1.0), F32(0.0)),
        )
        for d in range(3)
    ]


def along_z_body(sc, own, before, after, target_faces, wide, up, down):
    has_before, has_after = inside_of(sc)[2]
    col = lax.broadcasted_iota(jnp.int32, (8, 128), 1)

    def around_z(k):
        return jnp.where(col < 64, after[k] * has_after, before[k] * has_before)

    for k in range(18):
        here, there = own[k], around_z(k)
        if k < 8:
            turn = (128 - k) % 128
            low = pltpu.roll(before[18], turn, 1) if turn else before[18]
            high = pltpu.roll(own[18], turn, 1) if turn else own[18]
            here = jnp.where(col == 0, here + low * has_before, here)
            there = jnp.where(col == 0, there + high * has_after, there)
        wide[k, :, 0:128] = here
        wide[k, :, 128:256] = there
    for k in range(7):
        up[k] = wide[k + 1]
        up[k + 7] = wide[k + 9]
        down[k] = wide[k]
        down[k + 7] = wide[k + 8]
    up[14] = wide[17]
    down[14] = wide[17]
    up[15] = wide[16]
    up[16, :, 0:128] = target_faces[0]
    up[16, :, 128:256] = jnp.zeros((8, 128), F32)


def along_x_body(sc, wide, low, high, target_faces, out):
    has_before, has_after = inside_of(sc)[0]
    for k in range(7):
        out[k] = low[k] * has_before
        out[k + 22] = low[k + 7] * has_before
        more = wide[16] if k == 0 else jnp.zeros((8, 256), F32)
        out[k + 15] = (high[k] + more) * has_after
        out[k + 37] = high[k + 7] * has_after
    for k in range(8):
        out[k + 7] = wide[k] + low[15] * has_before if k == 0 else wide[k]
        out[k + 29] = wide[k + 8]
    out[44] = low[14] * has_before
    out[45] = wide[17]
    out[46] = high[14] * has_after
    out[47, :, 0:128] = target_faces[1]
    out[47, :, 128:256] = jnp.zeros((8, 128), F32)


def along_y(sc, own, low, high, b, rho, low_faces):
    has_before, has_after = inside_of(sc)[1]
    row = lax.broadcasted_iota(jnp.int32, (8, 256), 0)
    for i in range(22):
        k, r = divmod(i + 1, 8)
        more = jnp.broadcast_to(low[44 + k, r : r + 1, :] * has_before, (8, 256))
        next_more = jnp.broadcast_to(own[44 + k, r : r + 1, :], (8, 256))
        b[i, 0:8, :] = low[i] * has_before
        b[i, 8:16, :] = jnp.where(row == 0, own[i] + more, own[i])
        b[i, 16:24, :] = jnp.where(row == 0, high[i] + next_more, high[i]) * has_after
        rho[i, 0:8, :] = low[i + 22] * has_before
        rho[i, 8:16, :] = own[i + 22]
        rho[i, 16:24, :] = high[i + 22] * has_after
    low_faces[0] = low[45, :, 0:128]
    low_faces[1] = low[47, :, 0:128]


def middle_body(sc, near, flux, fields, from_x, low_y, from_z, ax, ay, az, new, misfit, out):
    scale = F32(1.0 / CELLS)
    target = fields.at[3:6]
    inner = [jnp.where(sc[d] > 0, F32(1.0), F32(0.0)) for d in range(3)]

    def rises(i):
        p = near[i]
        return p, back(p, 0) - p, back(p, 1) - p

    for x in range(8):
        p, rise_y, rise_z = rises(x + 1)
        rise_x = near[x + 2] - p
        parts = (ax[x + 7] * rise_x, ay[x + 7] * rise_y, az[x + 7] * rise_z)
        for d in range(3):
            value = flux[d, x] - parts[d][8:16, 0:128]
            new[d, x] = value
            misfit[d, x] = (value - target[d, x]) * scale

    def low_weighted_x():
        up = ax[6, 8:16, 0:128]
        rise = (near[1] - near[0])[8:16, 0:128]
        value = from_x[15, :, 0:128] - up * rise - from_x[16, :, 0:128]
        return up * (value * (scale * inner[0]))

    def low_weighted_y(x):
        up = ay[x + 7, 7:8, 0:128]
        rise = near[x + 1, 8:9, 0:128] - near[x + 1, 7:8, 0:128]
        value = low_y[0, x : x + 1, :] - up * rise - low_y[1, x : x + 1, :]
        return jnp.broadcast_to(up * (value * (scale * inner[1])), (8, 128))

    def low_weighted_z(x):
        p = near[x + 1, 8:16, :]
        rise = (back(p, 1) - p)[:, 128:256]
        up = az[x + 7, 8:16, 128:256]
        low_flux = pltpu.roll(from_z[18], 127 - x, 1)
        low_target = pltpu.roll(from_z[18], 119 - x, 1)
        value = up * ((low_flux - up * rise - low_target) * (scale * inner[2]))
        return forth(value, 1)

    refs = (ax, ay, az)

    def weighted(d, x):
        return refs[d][x + 7, 8:16, 0:128] * misfit[d, x]

    for x in range(8):
        bx, by, bz = shifted(weighted, low_weighted_x, low_weighted_y, low_weighted_z, x)
        out[x] = (weighted(0, x) - bx) + (weighted(1, x) - by) + (weighted(2, x) - bz)


def gradient_body(
    sc, near, misfit, features, slope, hidden, weights, out, acc_in, acc_bias, acc_out, kback
):
    narrow = dot_across(members(512, 64), weights[24:27, :].astype(BF16)).astype(BF16)
    kback[...] = same_row(dot_across(narrow, members(24, 3)))
    _, high = opens_of(sc)
    high_x = jnp.where(sc[0] == 3, high[0], F32(1.0))
    high_y = jnp.where(sc[1] == 7, high[1], F32(1.0))
    high_z = jnp.where(sc[2] == 7, high[2], F32(1.0))
    row = lax.broadcasted_iota(jnp.int32, (8, 128), 0)
    col = lax.broadcasted_iota(jnp.int32, (8, 128), 1)
    factor_y = jnp.where(row == 7, high_y, F32(1.0))
    factor_z = jnp.where(col == 127, high_z, F32(1.0))
    acc_in[...] = jnp.zeros((128, 512), F32)
    acc_bias[...] = jnp.zeros((512, 128), F32)
    acc_out[...] = jnp.zeros((24, 512), F32)
    across = ACROSS

    def one(x):
        p = near[x + 1]
        rise_x = (near[x + 2] - p)[8:16, 0:128]
        rise_y = (back(p, 0) - p)[8:16, 0:128]
        rise_z = (back(p, 1) - p)[8:16, 0:128]
        factor_x = jnp.where(x == 7, high_x, F32(1.0))
        grads = jnp.concatenate(
            [
                (misfit[0, x] + rise_x) * factor_x,
                (misfit[1, x] + rise_y) * factor_y,
                (misfit[2, x] + rise_z) * factor_z,
            ],
            axis=0,
        ).astype(BF16)
        columns = features[:, x, :, :].astype(F32).reshape(128, 128).astype(BF16)
        grad_before = jnp.dot(kback[...], grads, preferred_element_type=F32) * slope[x]
        acc_bias[...] += grad_before
        acc_in[...] += lax.dot_general(
            columns, grad_before.astype(BF16), across, preferred_element_type=F32
        )
        acc_out[...] += lax.dot_general(grads, hidden[x], across, preferred_element_type=F32)

    planes(0, 8, one, CLOSURE)

    def same(count):
        r = lax.broadcasted_iota(jnp.int32, (count, 512), 0)
        c = lax.broadcasted_iota(jnp.int32, (count, 512), 1)
        return r % 8 == c % 8

    def grouped(count, groups):
        r = lax.broadcasted_iota(jnp.int32, (groups, count), 0)
        c = lax.broadcasted_iota(jnp.int32, (groups, count), 1)
        return jnp.where(c // 8 == r, F32(1.0), F32(0.0))

    hr = lax.broadcasted_iota(jnp.int32, (512, 64), 0)
    hc = lax.broadcasted_iota(jnp.int32, (512, 64), 1)
    fold = jnp.where(hr // 8 == hc, F32(1.0), F32(0.0))
    in_part = exact_dot(grouped(128, 16), jnp.where(same(128), acc_in[...], F32(0.0)))
    out_part = exact_dot(grouped(24, 8), jnp.where(same(24), acc_out[...], F32(0.0)))
    bias_part = lax.dot_general(
        jnp.ones((8, 128), F32), acc_bias[...], across, precision=HIGHEST, preferred_element_type=F32
    )
    folded = exact_dot(jnp.concatenate([in_part, out_part, bias_part], axis=0), fold)
    packed = jnp.concatenate(
        [
            jnp.concatenate([folded[0:8], folded[8:16]], axis=1),
            jnp.concatenate([folded[16:24], folded[24:32]], axis=1),
        ],
        axis=0,
    )
    for k in range(32):
        out[k] = packed


def plane_sum_body(parts, out):
    total = parts[0]
    for k in range(1, 32):
        total = total + parts[k]
    for k in range(8):
        out[k] = total


def ring(up, down, axis):
    count = lax.axis_size(axis)
    ups = [(i, (i + 1) % count) for i in range(count)]
    return lax.ppermute(up, axis, ups), lax.ppermute(down, axis, [(b, a) for a, b in ups])


def exchanged(own, marks):
    before, after = ring(own, own, "gz")
    wide = jnp.concatenate([own, after * marks[0, :128] + before * marks[1, :128]], axis=2)
    low, high = ring(wide[1:8], wide[0:7], "gx")
    wide = jnp.concatenate([low * marks[2], wide, high * marks[3]], axis=0)
    low, high = ring(wide, wide, GY)
    return jnp.concatenate([low * marks[4], wide, high * marks[5]], axis=1)


def unpack_body(parts, grad_in, grad_bias, grad_out):
    total = parts[0]
    for k in range(1, 8):
        total = total + parts[k]
    grad_in[0:8, :] = total[0:8, 0:64]
    grad_in[8:16, :] = total[0:8, 64:128]
    grad_bias[...] = total[8:9, 64:128]
    grad_out[...] = total[8:11, 0:64]


def sent_to_all(copies, axis):
    return lax.all_to_all(copies, axis, split_axis=0, concat_axis=0, tiled=True)


def per_device(velocity, features, density, target, weight_in, bias_in, weight_out, open_faces):
    place = jnp.stack([lax.axis_index("gx"), lax.axis_index(GY), lax.axis_index("gz")])
    sc = jnp.concatenate([place.astype(jnp.int32), open_faces])
    block = (8, 8, 128)
    weights = (
        jnp.pad(weight_in.astype(F32), ((0, 16), (0, 0)))
        + jnp.pad(bias_in[None], ((16, 15), (0, 0)))
        + jnp.pad(weight_out.T.astype(F32), ((24, 5), (0, 0)))
    )
    fields = jnp.concatenate([velocity, target, density[None]], axis=0)
    flux, slope, hidden, message, target_faces, marks = call(
        closure_body,
        [
            shaped((3, *block)),
            shaped((8, 512, 128)),
            shaped((8, 512, 128), BF16),
            shaped((19, 8, 128)),
            shaped((2, 8, 128)),
            shaped((8, 256)),
        ],
        (sc, features, fields, weights),
        [
            pltpu.VMEM((512, 128), BF16),
            pltpu.VMEM((512, 128), F32),
            pltpu.VMEM((24, 512), BF16),
        ],
        smem=(0,),
    )
    from_z, after = ring(message, message, "gz")
    wide, up, down = call(
        along_z_body,
        [shaped((18, 8, 256)), shaped((17, 8, 256)), shaped((15, 8, 256))],
        (sc, message, from_z, after, target_faces),
        smem=(0,),
    )
    from_x, after = ring(up, down, "gx")
    (message,) = call(
        along_x_body, [shaped((48, 8, 256))], (sc, wide, from_x, after, target_faces), smem=(0,)
    )
    before, after = ring(message, message, GY)
    region, to_plane = shaped(REGION), shaped((32, 16, 128))
    one_region = [pltpu.VMEM(REGION, F32), pltpu.VMEM((32, 128), F32)]
    source, *coefs, v, part, low_y = call(
        start_body,
        [region] * 7 + [shaped((32, 32, 128)), shaped((2, 8, 128))],
        (sc, message, before, after),
        [pltpu.VMEM(REGION, F32), *one_region],
        smem=(0,),
    )
    ax, ay, az, w, d = coefs
    parts = sent_to_all(part, XY)
    coarse = call(
        coarse_body,
        [shaped(L1)] * 5 + [shaped(L2)] * 5,
        (sc, parts),
        [pltpu.VMEM(L1, F32), pltpu.VMEM(L2, F32), pltpu.VMEM((256, 128), F32)],
        smem=(0,),
    )

    def finish_solve(b, v, parts):
        (own,) = call(
            post_own_body,
            [shaped(block)],
            (sc, parts, *coarse, b, v, ax, ay, az, w),
            POST_SCRATCH,
            smem=(0,),
        )
        p = exchanged(own, marks)
        s, v, part = call(
            again_body, [region, region, to_plane], (b, p, *coefs), one_region
        )
        (near,) = call(
            post_near_body,
            [shaped((10, NYP, NZP))],
            (sc, sent_to_all(part, XY), *coarse, s, v, ax, ay, az, w, p),
            POST_SCRATCH,
            smem=(0,),
        )
        return near

    near = finish_solve(source, v, parts)
    new_velocity, misfit, grad_pressure = call(
        middle_body,
        [shaped((3, *block)), shaped((3, *block)), shaped(block)],
        (sc, near, flux, fields, from_x, low_y, from_z, ax, ay, az),
        smem=(0,),
    )
    b = exchanged(grad_pressure, marks)
    v, part = call(pre_body, [region, to_plane], (b, *coefs), one_region)
    near = finish_solve(b, v, sent_to_all(part, XY))
    (packed,) = call(
        gradient_body,
        [to_plane],
        (sc, near, misfit, features, slope, hidden, weights),
        [
            pltpu.VMEM((128, 512), F32),
            pltpu.VMEM((512, 128), F32),
            pltpu.VMEM((24, 512), F32),
            pltpu.VMEM((512, 24), BF16),
        ],
        smem=(0,),
    )
    (plane,) = call(plane_sum_body, [shaped((8, 16, 128))], (sent_to_all(packed, XY),))
    grad_in, grad_bias, grad_out = call(
        unpack_body,
        [shaped((16, 64)), shaped((1, 64)), shaped((3, 64))],
        (sent_to_all(plane, "gz"),),
    )
    return new_velocity, grad_in, grad_bias[0], grad_out.T


def solution(mesh):
    split = Mesh(
        mesh.devices.reshape(mesh.shape["gx"], 4, 2, mesh.shape["gz"]), ("gx", "gy_0", "gy_1", "gz")
    )
    placed = (
        P(None, "gx", GY, "gz"),
        P(None, "gx", GY, "gz"),
        P("gx", GY, "gz"),
        P(None, "gx", GY, "gz"),
        P(),
        P(),
        P(),
        P(),
    )
    return jax.shard_map(
        per_device,
        mesh=split,
        in_specs=placed,
        out_specs=(P(None, "gx", GY, "gz"), P(), P(), P()),
        check_vma=False,
    )
```

```python
import jax
import jax.numpy as jnp
from jax import lax
from jax.experimental import pallas as pl
from jax.experimental.pallas import tpu as pltpu
from jax.sharding import Mesh
from jax.sharding import PartitionSpec as P

GY = ("gy_0", "gy_1")
CLOSURE = 8
XY = ("gx", "gy_0", "gy_1")
ALL = ("gx", "gy_0", "gy_1", "gz")
F32 = jnp.float32
BF16 = jnp.bfloat16
HIGHEST = lax.Precision.HIGHEST
MASS_SHIFT = 0.05
CELLS = 2097152.0

NXP, NYP, NZP = 22, 24, 256
REGION = (NXP, NYP, NZP)
L1 = (20, 32, 128)
L2 = (10, 16, 128)
MOST = {24: 10, 32: 16, 16: 8}


def shaped(shape, dtype=F32):
    return jax.ShapeDtypeStruct(shape, dtype)


def call(body, outs, args, scratch=(), smem=()):
    spaces = [
        pltpu.SMEM if i in smem else pltpu.VMEM for i in range(len(args))
    ]
    specs = [pl.BlockSpec(memory_space=space) for space in spaces]
    return pl.pallas_call(
        body,
        out_shape=outs,
        in_specs=specs,
        out_specs=[pl.BlockSpec(memory_space=pltpu.VMEM)] * len(outs),
        scratch_shapes=list(scratch),
        compiler_params=pltpu.CompilerParams(vmem_limit_bytes=12 << 20),
    )(*args)


def back(x, axis):
    return pltpu.roll(x, x.shape[axis] - 1, axis)


def forth(x, axis):
    return pltpu.roll(x, 1, axis)


def exact_dot(a, b):
    return jnp.dot(a, b, precision=HIGHEST, preferred_element_type=F32)


def chosen_dot(a, b):
    high = a.astype(BF16)
    rest = a - high.astype(F32)
    middle = rest.astype(BF16)
    low = (rest - middle.astype(F32)).astype(BF16)
    count = a.shape[0]
    parts = jnp.dot(
        jnp.concatenate([high, middle, low], axis=0), b.astype(BF16), preferred_element_type=F32
    )
    return (parts[2 * count :] + parts[count : 2 * count]) + parts[:count]


def steps(count, rows):
    return max(k for k in range(1, MOST[rows] + 1) if count % k == 0)


def planes(lo, hi, body, unroll=2):
    def step(i, carry):
        body(i)
        return carry

    lax.fori_loop(lo, hi, step, 0, unroll=unroll)


def around(src, ax, ay, az, i):
    v = src[i]
    y, z = ay[i], az[i]
    total = ax[i] * src[i + 1] + ax[i - 1] * src[i - 1]
    total = total + (y * back(v, 0) + forth(y * v, 0))
    return v, total + (z * back(v, 1) + forth(z * v, 1))


def sweep(src, dst, s, w, ax, ay, az, lo, hi):
    def one(i):
        v, total = around(src, ax, ay, az, i)
        dst[i] = 0.2 * v + w[i] * (s[i] + total)

    planes(lo, hi, one, steps(hi - lo, src.shape[1]))


def first_sweep(dst, s, w, lo, hi):
    def one(i):
        dst[i] = w[i] * s[i]

    planes(lo, hi, one, steps(hi - lo, s.shape[1]))


def face(here, there, weight, low, high):
    has, next_has = here > 0.0, there > 0.0
    factor = jnp.where(
        has, jnp.where(next_has, F32(1.0), high), jnp.where(next_has, low, F32(0.0))
    )
    total = jnp.where(has | next_has, here + there, F32(1.0))
    return weight * 2.0 / total * factor


def coefficients(rho, opens, weight, refs, lo, hi, whole_y):
    ax, ay, az, w, d = refs
    low, high = opens
    count = rho.shape[1]

    def one_face(i):
        ax[i] = face(rho[i], rho[i + 1], weight, low[0], high[0])

    planes(lo - 1, hi, one_face, hi - lo + 1)

    def one(i):
        r = rho[i]
        after = back(r, 0)
        row = lax.broadcasted_iota(jnp.int32, r.shape, 0)
        if whole_y:
            after = jnp.where(row == count - 1, F32(0.0), after)
        up_y = face(r, after, weight, low[1], high[1])
        if whole_y:
            first = jnp.where(r > 0.0, weight * 2.0 / jnp.where(r > 0.0, r, F32(1.0)), F32(0.0))
            down_y = jnp.where(row == 0, first * low[1], forth(up_y, 0))
        else:
            down_y = forth(up_y, 0)
        up_z = face(r, back(r, 1), weight, low[2], high[2])
        diagonal = MASS_SHIFT + ax[i] + ax[i - 1] + up_y + down_y + up_z + forth(up_z, 1)
        ay[i] = jnp.where(row == count - 1, F32(0.0), up_y) if whole_y else up_y
        az[i] = up_z
        d[i] = diagonal
        w[i] = jnp.where(r > 0.0, 0.8 / diagonal, F32(0.0))

    planes(lo, hi, one, 10 if count == 24 else hi - lo)


def lane_pairs(cells, kept, repeat):
    row = lax.broadcasted_iota(jnp.int32, (cells, kept), 0)
    col = lax.broadcasted_iota(jnp.int32, (cells, kept), 1)
    return jnp.where(row // 2 == col % repeat, F32(1.0), F32(0.0))


def lane_spread(cells, kept):
    row = lax.broadcasted_iota(jnp.int32, (cells, kept), 0)
    col = lax.broadcasted_iota(jnp.int32, (cells, kept), 1)
    return jnp.where(col // 2 == row, F32(1.0), F32(0.0))


def block_means(read, rows, out, out_row):
    pairs = [read(7 + 2 * k) + read(8 + 2 * k) for k in range(4)]
    rows[...] = chosen_dot(jnp.concatenate(pairs, axis=0), lane_pairs(256, 128, 128))
    total = 0.125 * (rows[pl.ds(0, 16, stride=2), :] + rows[pl.ds(1, 16, stride=2), :])
    for k in range(32):
        out[k, out_row : out_row + 16, :] = total


def presmooth(s, v, va, coefs, rows, out):
    ax, ay, az, w, d = coefs
    first_sweep(v, s, w, 1, 21)
    sweep(v, va, s, w, ax, ay, az, 2, 20)
    sweep(va, v, s, w, ax, ay, az, 3, 19)

    def residue(i):
        centre, total = around(v, ax, ay, az, i)
        return (s[i] + total - d[i] * centre)[8:16]

    block_means(residue, rows, out, 0)


def opens_of(sc):
    values = [sc[3 + k].astype(F32) for k in range(6)]
    return values[0::2], values[1::2]


def start_body(
    sc, own, low, high, b, ax, ay, az, w, d, v, out, low_faces, rho, va, rows
):
    along_y(sc, own, low, high, b, rho, low_faces)
    coefs = (ax, ay, az, w, d)
    for ref in (ax, ay, az, w, d, v):
        ref[0] = jnp.zeros((NYP, NZP), F32)
        ref[21] = jnp.zeros((NYP, NZP), F32)
    coefficients(rho, opens_of(sc), 1.0, coefs, 1, 21, False)
    presmooth(b, v, va, coefs, rows, out)
    block_means(lambda i: rho[i, 8:16, :], rows, out, 16)


def pre_body(b, ax, ay, az, w, d, v, out, va, rows):
    v[0] = jnp.zeros((NYP, NZP), F32)
    v[21] = jnp.zeros((NYP, NZP), F32)
    presmooth(b, v, va, (ax, ay, az, w, d), rows, out)


def again_body(b, p, ax, ay, az, w, d, s, v, out, va, rows):
    for ref in (s, v):
        ref[0] = jnp.zeros((NYP, NZP), F32)
        ref[21] = jnp.zeros((NYP, NZP), F32)

    def one(i):
        centre, total = around(p, ax, ay, az, i)
        s[i] = b[i] + total - d[i] * centre

    planes(1, 21, one, 10)
    presmooth(s, v, va, (ax, ay, az, w, d), rows, out)


def whole_plane(parts, first, dst):
    for k in range(2):
        dst[k] = jnp.zeros((32, 128), F32)
        dst[18 + k] = jnp.zeros((32, 128), F32)
    for device in range(32):
        x, y = divmod(device, 8)
        for k in range(4):
            dst[2 + 4 * x + k, 4 * y : 4 * y + 4, :] = parts[
                device, first + 4 * k : first + 4 * k + 4, :
            ]


def restrict_whole(read, rows, dst):
    for k in range(8):
        rows[32 * k : 32 * k + 32, :] = read(2 + 2 * k) + read(3 + 2 * k)
    rows[...] = chosen_dot(rows[...], lane_pairs(128, 128, 64))
    for k in range(8):
        total = (
            rows[pl.ds(32 * k, 16, stride=2), :] + rows[pl.ds(32 * k + 1, 16, stride=2), :]
        )
        dst[1 + k] = 0.125 * total


def coarse_body(
    sc, parts, ax1, ay1, az1, w1, d1, ax2, ay2, az2, w2, d2, rho1, rho2, rows
):
    for ref in (ax1, ay1, az1, w1, d1):
        ref[...] = jnp.zeros(L1, F32)
    for ref in (ax2, ay2, az2, w2, d2, rho2):
        ref[...] = jnp.zeros(L2, F32)
    opens = opens_of(sc)
    whole_plane(parts, 16, rho1)
    coefficients(rho1, opens, 0.25, (ax1, ay1, az1, w1, d1), 2, 18, True)
    restrict_whole(lambda i: rho1[i], rows, rho2)
    coefficients(rho2, opens, 0.0625, (ax2, ay2, az2, w2, d2), 1, 9, True)


def correct(
    sc, parts, coefs1, coefs2, s1, v1, u1, s2, v2, u2, rows, wide_a, wide_b
):
    ax1, ay1, az1, w1, d1 = coefs1
    ax2, ay2, az2, w2, d2 = coefs2
    whole_plane(parts, 0, s1)
    for ref in (v1, u1):
        for k in (0, 1, 18, 19):
            ref[k] = jnp.zeros((32, 128), F32)
    for ref in (v2, u2):
        for k in (0, 9):
            ref[k] = jnp.zeros((16, 128), F32)
    first_sweep(v1, s1, w1, 2, 18)
    sweep(v1, u1, s1, w1, ax1, ay1, az1, 2, 18)
    sweep(u1, v1, s1, w1, ax1, ay1, az1, 2, 18)

    def residue(i):
        centre, total = around(v1, ax1, ay1, az1, i)
        return s1[i] + total - d1[i] * centre

    restrict_whole(residue, rows, s2)
    first_sweep(v2, s2, w2, 1, 9)
    for k in range(5):
        a, b = (v2, u2) if k % 2 == 0 else (u2, v2)
        sweep(a, b, s2, w2, ax2, ay2, az2, 1, 9)
    spread = chosen_dot(
        jnp.concatenate([u2[1 + k] for k in range(8)], axis=0), lane_spread(128, 128)
    )
    rows[pl.ds(0, 128, stride=2), :] = spread
    rows[pl.ds(1, 128, stride=2), :] = spread
    for k in range(8):
        more = rows[32 * k : 32 * k + 32, :]
        v1[2 + 2 * k] = v1[2 + 2 * k] + more
        v1[3 + 2 * k] = v1[3 + 2 * k] + more
    sweep(v1, u1, s1, w1, ax1, ay1, az1, 2, 18)
    sweep(u1, v1, s1, w1, ax1, ay1, az1, 2, 18)
    sweep(v1, u1, s1, w1, ax1, ay1, az1, 2, 18)
    base = sc[0] * 4
    near = jnp.concatenate([u1[base + k] for k in range(8)], axis=0)
    wide = chosen_dot(near, lane_spread(128, 256))
    for lanes, ref in ((slice(0, 128), wide_a), (slice(128, 256), wide_b)):
        for k in range(8):
            ref[80 * k : 80 * k + 8, :] = jnp.zeros((8, 128), F32)
            ref[80 * k + 72 : 80 * k + 80, :] = jnp.zeros((8, 128), F32)
            part = wide[32 * k : 32 * k + 32, lanes]
            ref[pl.ds(80 * k + 8, 32, stride=2), :] = part
            ref[pl.ds(80 * k + 9, 32, stride=2), :] = part


def postsmooth(sc, s, v, coefs, wide_a, wide_b, va, vb):
    ax, ay, az, w = coefs
    row = pl.multiple_of(sc[1] * 8, 8)
    for i in range(3, 19):
        k = (i - 3) // 2
        more = jnp.concatenate(
            [wide_a[pl.ds(80 * k + row, 24), :], wide_b[pl.ds(80 * k + row, 24), :]], axis=1
        )
        va[i] = v[i] + more
    sweep(va, vb, s, w, ax, ay, az, 4, 18)
    sweep(vb, va, s, w, ax, ay, az, 5, 17)


POST_SCRATCH = (
    [pltpu.VMEM(L1, F32)] * 3
    + [pltpu.VMEM(L2, F32)] * 3
    + [pltpu.VMEM((256, 128), F32)]
    + [pltpu.VMEM((640, 128), F32)] * 2
    + [pltpu.VMEM(REGION, F32)] * 2
)


def post_own_body(
    sc, parts, ax1, ay1, az1, w1, d1, ax2, ay2, az2, w2, d2, s, v, ax, ay, az, w, out, *scratch
):
    *inner, wide_a, wide_b, va, vb = scratch
    correct(
        sc,
        parts,
        (ax1, ay1, az1, w1, d1),
        (ax2, ay2, az2, w2, d2),
        *inner,
        wide_a,
        wide_b,
    )
    postsmooth(sc, s, v, (ax, ay, az, w), wide_a, wide_b, va, vb)
    for i in range(8):
        centre, total = around(va, ax, ay, az, i + 7)
        new = 0.2 * centre + w[i + 7] * (s[i + 7] + total)
        out[i] = new[8:16, 0:128]


def post_near_body(
    sc, parts, ax1, ay1, az1, w1, d1, ax2, ay2, az2, w2, d2, s, v, ax, ay, az, w, p, out, *scratch
):
    *inner, wide_a, wide_b, va, vb = scratch
    correct(
        sc,
        parts,
        (ax1, ay1, az1, w1, d1),
        (ax2, ay2, az2, w2, d2),
        *inner,
        wide_a,
        wide_b,
    )
    postsmooth(sc, s, v, (ax, ay, az, w), wide_a, wide_b, va, vb)
    for i in range(10):
        centre, total = around(va, ax, ay, az, i + 6)
        out[i] = p[i + 6] + 0.2 * centre + w[i + 6] * (s[i + 6] + total)


def members(count, groups):
    r = lax.broadcasted_iota(jnp.int32, (count, groups), 0)
    c = lax.broadcasted_iota(jnp.int32, (count, groups), 1)
    return jnp.where(r // 8 == c, F32(1.0), F32(0.0)).astype(BF16)


def same_row(x):
    r = lax.broadcasted_iota(jnp.int32, x.shape, 0)
    c = lax.broadcasted_iota(jnp.int32, x.shape, 1)
    return jnp.where(r % 8 == c % 8, x, F32(0.0)).astype(BF16)


ACROSS = (((1,), (1,)), ((), ()))


def dot_across(a, b, precision=None):
    return lax.dot_general(a, b, ACROSS, precision=precision, preferred_element_type=F32)


def closure_body(
    sc,
    features,
    fields,
    weights,
    flux,
    slope,
    hidden,
    message,
    target_faces,
    marks,
    kin,
    bias,
    kout,
):
    velocity, target = fields.at[0:3], fields.at[3:6]
    message[8:16] = fields[6]
    weight_in = weights[0:16, :].astype(BF16)
    weight_out = weights[24:27, :].astype(BF16)
    units = members(512, 64)
    narrow = dot_across(units, weight_in).astype(BF16)
    kin[...] = same_row(dot_across(narrow, members(128, 16)))
    narrow = jnp.dot(members(24, 3), weight_out, preferred_element_type=F32).astype(BF16)
    kout[...] = same_row(dot_across(narrow, units))
    bias[...] = dot_across(
        units.astype(F32), jnp.broadcast_to(weights[16:17, :], (128, 64)), HIGHEST
    )
    _, high = opens_of(sc)
    high_x = jnp.where(sc[0] == 3, high[0], F32(1.0))
    high_y = jnp.where(sc[1] == 7, high[1], F32(1.0))
    high_z = jnp.where(sc[2] == 7, high[2], F32(1.0))
    row = lax.broadcasted_iota(jnp.int32, (8, 128), 0)
    col = lax.broadcasted_iota(jnp.int32, (8, 128), 1)
    factor_y = jnp.where(row == 7, high_y, F32(1.0))
    factor_z = jnp.where(col == 127, high_z, F32(1.0))
    def one(x):
        columns = features[:, x, :, :].astype(F32).reshape(128, 128).astype(BF16)
        before = jnp.dot(kin[...], columns, preferred_element_type=F32) + bias[...]
        gate = 1.0 / (1.0 + jnp.exp(-before))
        unit = (before * gate).astype(BF16)
        hidden[x] = unit
        slope[x] = gate * (1.0 + before * (1.0 - gate))
        shift = jnp.dot(kout[...], unit, preferred_element_type=F32)
        factor_x = jnp.where(x == 7, high_x, F32(1.0))
        flux[0, x] = (velocity[0, x] + shift[0:8]) * factor_x
        flux[1, x] = (velocity[1, x] + shift[8:16]) * factor_y
        flux[2, x] = (velocity[2, x] + shift[16:24]) * factor_z

    planes(0, 8, one, CLOSURE)
    zero = jnp.zeros((8, 128), F32)
    ends = zero
    for x in range(8):
        bx, by, bz = shifted(
            lambda d, i: flux[d, i], lambda: zero, lambda i: zero, lambda i: zero, x
        )
        message[x] = -((flux[0, x] - bx) + (flux[1, x] - by) + (flux[2, x] - bz))
        message[17, x : x + 1, :] = flux[1, x, 7:8, :]
        target_faces[1, x : x + 1, :] = target[1, x, 7:8, :]
        ends = jnp.where(col == x, pltpu.roll(flux[2, x], x + 1, 1), ends)
        ends = jnp.where(col == x + 8, pltpu.roll(target[2, x], x + 9, 1), ends)
    message[16] = flux[0, 7]
    message[18] = ends
    target_faces[0] = target[0, 7]
    inside = inside_of(sc)
    wide_col = lax.broadcasted_iota(jnp.int32, (1, 256), 1)
    one_row = jnp.ones((1, 256), F32)
    marks[0:1, :] = jnp.where(wide_col < 64, inside[2][1], F32(0.0))
    marks[1:2, :] = jnp.where(wide_col < 64, F32(0.0), inside[2][0])
    for d in range(2):
        marks[2 + 2 * d : 3 + 2 * d, :] = one_row * inside[d][0]
        marks[3 + 2 * d : 4 + 2 * d, :] = one_row * inside[d][1]
    marks[6:8, :] = jnp.zeros((2, 256), F32)


def shifted(field, low_x, low_y, low_z, x):
    row = lax.broadcasted_iota(jnp.int32, (8, 128), 0)
    col = lax.broadcasted_iota(jnp.int32, (8, 128), 1)
    before_x = low_x() if x == 0 else field(0, x - 1)
    before_y = jnp.where(row == 0, low_y(x), forth(field(1, x), 0))
    before_z = jnp.where(col == 0, low_z(x), forth(field(2, x), 1))
    return before_x, before_y, before_z


def inside_of(sc):
    last = (3, 7, 7)
    return [
        (
            jnp.where(sc[d] > 0, F32(1.0), F32(0.0)),
            jnp.where(sc[d] < last[d], F32(1.0), F32(0.0)),
        )
        for d in range(3)
    ]


def along_z_body(sc, own, before, after, target_faces, wide, up, down):
    has_before, has_after = inside_of(sc)[2]
    col = lax.broadcasted_iota(jnp.int32, (8, 128), 1)

    def around_z(k):
        return jnp.where(col < 64, after[k] * has_after, before[k] * has_before)

    for k in range(18):
        here, there = own[k], around_z(k)
        if k < 8:
            turn = (128 - k) % 128
            low = pltpu.roll(before[18], turn, 1) if turn else before[18]
            high = pltpu.roll(own[18], turn, 1) if turn else own[18]
            here = jnp.where(col == 0, here + low * has_before, here)
            there = jnp.where(col == 0, there + high * has_after, there)
        wide[k, :, 0:128] = here
        wide[k, :, 128:256] = there
    for k in range(7):
        up[k] = wide[k + 1]
        up[k + 7] = wide[k + 9]
        down[k] = wide[k]
        down[k + 7] = wide[k + 8]
    up[14] = wide[17]
    down[14] = wide[17]
    up[15] = wide[16]
    up[16, :, 0:128] = target_faces[0]
    up[16, :, 128:256] = jnp.zeros((8, 128), F32)


def along_x_body(sc, wide, low, high, target_faces, out):
    has_before, has_after = inside_of(sc)[0]
    for k in range(7):
        out[k] = low[k] * has_before
        out[k + 22] = low[k + 7] * has_before
        more = wide[16] if k == 0 else jnp.zeros((8, 256), F32)
        out[k + 15] = (high[k] + more) * has_after
        out[k + 37] = high[k + 7] * has_after
    for k in range(8):
        out[k + 7] = wide[k] + low[15] * has_before if k == 0 else wide[k]
        out[k + 29] = wide[k + 8]
    out[44] = low[14] * has_before
    out[45] = wide[17]
    out[46] = high[14] * has_after
    out[47, :, 0:128] = target_faces[1]
    out[47, :, 128:256] = jnp.zeros((8, 128), F32)


def along_y(sc, own, low, high, b, rho, low_faces):
    has_before, has_after = inside_of(sc)[1]
    row = lax.broadcasted_iota(jnp.int32, (8, 256), 0)
    for i in range(22):
        k, r = divmod(i + 1, 8)
        more = jnp.broadcast_to(low[44 + k, r : r + 1, :] * has_before, (8, 256))
        next_more = jnp.broadcast_to(own[44 + k, r : r + 1, :], (8, 256))
        b[i, 0:8, :] = low[i] * has_before
        b[i, 8:16, :] = jnp.where(row == 0, own[i] + more, own[i])
        b[i, 16:24, :] = jnp.where(row == 0, high[i] + next_more, high[i]) * has_after
        rho[i, 0:8, :] = low[i + 22] * has_before
        rho[i, 8:16, :] = own[i + 22]
        rho[i, 16:24, :] = high[i + 22] * has_after
    low_faces[0] = low[45, :, 0:128]
    low_faces[1] = low[47, :, 0:128]


def middle_body(sc, near, flux, fields, from_x, low_y, from_z, ax, ay, az, new, misfit, out):
    scale = F32(1.0 / CELLS)
    target = fields.at[3:6]
    inner = [jnp.where(sc[d] > 0, F32(1.0), F32(0.0)) for d in range(3)]

    def rises(i):
        p = near[i]
        return p, back(p, 0) - p, back(p, 1) - p

    for x in range(8):
        p, rise_y, rise_z = rises(x + 1)
        rise_x = near[x + 2] - p
        parts = (ax[x + 7] * rise_x, ay[x + 7] * rise_y, az[x + 7] * rise_z)
        for d in range(3):
            value = flux[d, x] - parts[d][8:16, 0:128]
            new[d, x] = value
            misfit[d, x] = (value - target[d, x]) * scale

    def low_weighted_x():
        up = ax[6, 8:16, 0:128]
        rise = (near[1] - near[0])[8:16, 0:128]
        value = from_x[15, :, 0:128] - up * rise - from_x[16, :, 0:128]
        return up * (value * (scale * inner[0]))

    def low_weighted_y(x):
        up = ay[x + 7, 7:8, 0:128]
        rise = near[x + 1, 8:9, 0:128] - near[x + 1, 7:8, 0:128]
        value = low_y[0, x : x + 1, :] - up * rise - low_y[1, x : x + 1, :]
        return jnp.broadcast_to(up * (value * (scale * inner[1])), (8, 128))

    def low_weighted_z(x):
        p = near[x + 1, 8:16, :]
        rise = (back(p, 1) - p)[:, 128:256]
        up = az[x + 7, 8:16, 128:256]
        low_flux = pltpu.roll(from_z[18], 127 - x, 1)
        low_target = pltpu.roll(from_z[18], 119 - x, 1)
        value = up * ((low_flux - up * rise - low_target) * (scale * inner[2]))
        return forth(value, 1)

    refs = (ax, ay, az)

    def weighted(d, x):
        return refs[d][x + 7, 8:16, 0:128] * misfit[d, x]

    for x in range(8):
        bx, by, bz = shifted(weighted, low_weighted_x, low_weighted_y, low_weighted_z, x)
        out[x] = (weighted(0, x) - bx) + (weighted(1, x) - by) + (weighted(2, x) - bz)


def gradient_body(
    sc, near, misfit, features, slope, hidden, weights, out, acc_in, acc_bias, acc_out, kback
):
    narrow = dot_across(members(512, 64), weights[24:27, :].astype(BF16)).astype(BF16)
    kback[...] = same_row(dot_across(narrow, members(24, 3)))
    _, high = opens_of(sc)
    high_x = jnp.where(sc[0] == 3, high[0], F32(1.0))
    high_y = jnp.where(sc[1] == 7, high[1], F32(1.0))
    high_z = jnp.where(sc[2] == 7, high[2], F32(1.0))
    row = lax.broadcasted_iota(jnp.int32, (8, 128), 0)
    col = lax.broadcasted_iota(jnp.int32, (8, 128), 1)
    factor_y = jnp.where(row == 7, high_y, F32(1.0))
    factor_z = jnp.where(col == 127, high_z, F32(1.0))
    acc_in[...] = jnp.zeros((128, 512), F32)
    acc_bias[...] = jnp.zeros((512, 128), F32)
    acc_out[...] = jnp.zeros((24, 512), F32)
    across = ACROSS

    def one(x):
        p = near[x + 1]
        rise_x = (near[x + 2] - p)[8:16, 0:128]
        rise_y = (back(p, 0) - p)[8:16, 0:128]
        rise_z = (back(p, 1) - p)[8:16, 0:128]
        factor_x = jnp.where(x == 7, high_x, F32(1.0))
        grads = jnp.concatenate(
            [
                (misfit[0, x] + rise_x) * factor_x,
                (misfit[1, x] + rise_y) * factor_y,
                (misfit[2, x] + rise_z) * factor_z,
            ],
            axis=0,
        ).astype(BF16)
        columns = features[:, x, :, :].astype(F32).reshape(128, 128).astype(BF16)
        grad_before = jnp.dot(kback[...], grads, preferred_element_type=F32) * slope[x]
        acc_bias[...] += grad_before
        acc_in[...] += lax.dot_general(
            columns, grad_before.astype(BF16), across, preferred_element_type=F32
        )
        acc_out[...] += lax.dot_general(grads, hidden[x], across, preferred_element_type=F32)

    planes(0, 8, one, CLOSURE)

    def same(count):
        r = lax.broadcasted_iota(jnp.int32, (count, 512), 0)
        c = lax.broadcasted_iota(jnp.int32, (count, 512), 1)
        return r % 8 == c % 8

    def grouped(count, groups):
        r = lax.broadcasted_iota(jnp.int32, (groups, count), 0)
        c = lax.broadcasted_iota(jnp.int32, (groups, count), 1)
        return jnp.where(c // 8 == r, F32(1.0), F32(0.0))

    hr = lax.broadcasted_iota(jnp.int32, (512, 64), 0)
    hc = lax.broadcasted_iota(jnp.int32, (512, 64), 1)
    fold = jnp.where(hr // 8 == hc, F32(1.0), F32(0.0))
    in_part = exact_dot(grouped(128, 16), jnp.where(same(128), acc_in[...], F32(0.0)))
    out_part = exact_dot(grouped(24, 8), jnp.where(same(24), acc_out[...], F32(0.0)))
    bias_part = lax.dot_general(
        jnp.ones((8, 128), F32), acc_bias[...], across, precision=HIGHEST, preferred_element_type=F32
    )
    folded = exact_dot(jnp.concatenate([in_part, out_part, bias_part], axis=0), fold)
    packed = jnp.concatenate(
        [
            jnp.concatenate([folded[0:8], folded[8:16]], axis=1),
            jnp.concatenate([folded[16:24], folded[24:32]], axis=1),
        ],
        axis=0,
    )
    for k in range(32):
        out[k] = packed


def plane_sum_body(parts, out):
    total = parts[0]
    for k in range(1, 32):
        total = total + parts[k]
    for k in range(8):
        out[k] = total


def ring(up, down, axis):
    count = lax.axis_size(axis)
    ups = [(i, (i + 1) % count) for i in range(count)]
    return lax.ppermute(up, axis, ups), lax.ppermute(down, axis, [(b, a) for a, b in ups])


def exchanged(own, marks):
    before, after = ring(own, own, "gz")
    wide = jnp.concatenate([own, after * marks[0, :128] + before * marks[1, :128]], axis=2)
    low, high = ring(wide[1:8], wide[0:7], "gx")
    wide = jnp.concatenate([low * marks[2], wide, high * marks[3]], axis=0)
    low, high = ring(wide, wide, GY)
    return jnp.concatenate([low * marks[4], wide, high * marks[5]], axis=1)


def unpack_body(parts, grad_in, grad_bias, grad_out):
    total = parts[0]
    for k in range(1, 8):
        total = total + parts[k]
    grad_in[0:8, :] = total[0:8, 0:64]
    grad_in[8:16, :] = total[0:8, 64:128]
    grad_bias[...] = total[8:9, 64:128]
    grad_out[...] = total[8:11, 0:64]


def sent_to_all(copies, axis):
    return lax.all_to_all(copies, axis, split_axis=0, concat_axis=0, tiled=True)


def per_device(velocity, features, density, target, weight_in, bias_in, weight_out, open_faces):
    place = jnp.stack([lax.axis_index("gx"), lax.axis_index(GY), lax.axis_index("gz")])
    sc = jnp.concatenate([place.astype(jnp.int32), open_faces])
    block = (8, 8, 128)
    weights = (
        jnp.pad(weight_in.astype(F32), ((0, 16), (0, 0)))
        + jnp.pad(bias_in[None], ((16, 15), (0, 0)))
        + jnp.pad(weight_out.T.astype(F32), ((24, 5), (0, 0)))
    )
    fields = jnp.concatenate([velocity, target, density[None]], axis=0)
    flux, slope, hidden, message, target_faces, marks = call(
        closure_body,
        [
            shaped((3, *block)),
            shaped((8, 512, 128)),
            shaped((8, 512, 128), BF16),
            shaped((19, 8, 128)),
            shaped((2, 8, 128)),
            shaped((8, 256)),
        ],
        (sc, features, fields, weights),
        [
            pltpu.VMEM((512, 128), BF16),
            pltpu.VMEM((512, 128), F32),
            pltpu.VMEM((24, 512), BF16),
        ],
        smem=(0,),
    )
    from_z, after = ring(message, message, "gz")
    wide, up, down = call(
        along_z_body,
        [shaped((18, 8, 256)), shaped((17, 8, 256)), shaped((15, 8, 256))],
        (sc, message, from_z, after, target_faces),
        smem=(0,),
    )
    from_x, after = ring(up, down, "gx")
    (message,) = call(
        along_x_body, [shaped((48, 8, 256))], (sc, wide, from_x, after, target_faces), smem=(0,)
    )
    before, after = ring(message, message, GY)
    region, to_plane = shaped(REGION), shaped((32, 16, 128))
    one_region = [pltpu.VMEM(REGION, F32), pltpu.VMEM((32, 128), F32)]
    source, *coefs, v, part, low_y = call(
        start_body,
        [region] * 7 + [shaped((32, 32, 128)), shaped((2, 8, 128))],
        (sc, message, before, after),
        [pltpu.VMEM(REGION, F32), *one_region],
        smem=(0,),
    )
    ax, ay, az, w, d = coefs
    parts = sent_to_all(part, XY)
    coarse = call(
        coarse_body,
        [shaped(L1)] * 5 + [shaped(L2)] * 5,
        (sc, parts),
        [pltpu.VMEM(L1, F32), pltpu.VMEM(L2, F32), pltpu.VMEM((256, 128), F32)],
        smem=(0,),
    )

    def finish_solve(b, v, parts):
        (own,) = call(
            post_own_body,
            [shaped(block)],
            (sc, parts, *coarse, b, v, ax, ay, az, w),
            POST_SCRATCH,
            smem=(0,),
        )
        p = exchanged(own, marks)
        s, v, part = call(
            again_body, [region, region, to_plane], (b, p, *coefs), one_region
        )
        (near,) = call(
            post_near_body,
            [shaped((10, NYP, NZP))],
            (sc, sent_to_all(part, XY), *coarse, s, v, ax, ay, az, w, p),
            POST_SCRATCH,
            smem=(0,),
        )
        return near

    near = finish_solve(source, v, parts)
    new_velocity, misfit, grad_pressure = call(
        middle_body,
        [shaped((3, *block)), shaped((3, *block)), shaped(block)],
        (sc, near, flux, fields, from_x, low_y, from_z, ax, ay, az),
        smem=(0,),
    )
    b = exchanged(grad_pressure, marks)
    v, part = call(pre_body, [region, to_plane], (b, *coefs), one_region)
    near = finish_solve(b, v, sent_to_all(part, XY))
    (packed,) = call(
        gradient_body,
        [to_plane],
        (sc, near, misfit, features, slope, hidden, weights),
        [
            pltpu.VMEM((128, 512), F32),
            pltpu.VMEM((512, 128), F32),
            pltpu.VMEM((24, 512), F32),
            pltpu.VMEM((512, 24), BF16),
        ],
        smem=(0,),
    )
    (plane,) = call(plane_sum_body, [shaped((8, 16, 128))], (sent_to_all(packed, XY),))
    grad_in, grad_bias, grad_out = call(
        unpack_body,
        [shaped((16, 64)), shaped((1, 64)), shaped((3, 64))],
        (sent_to_all(plane, "gz"),),
    )
    return new_velocity, grad_in, grad_bias[0], grad_out.T


def solution(mesh):
    split = Mesh(
        mesh.devices.reshape(mesh.shape["gx"], 4, 2, mesh.shape["gz"]), ("gx", "gy_0", "gy_1", "gz")
    )
    placed = (
        P(None, "gx", GY, "gz"),
        P(None, "gx", GY, "gz"),
        P("gx", GY, "gz"),
        P(None, "gx", GY, "gz"),
        P(),
        P(),
        P(),
        P(),
    )
    return jax.shard_map(
        per_device,
        mesh=split,
        in_specs=placed,
        out_specs=(P(None, "gx", GY, "gz"), P(), P(), P()),
        check_vma=False,
    )
```
